512 devices in a mesh: gx: 32 (over z_hi, x, y), gy: 16 (over z_lo, core).
Axes of the slice: x: 4, y: 4, z: 16 (z_hi: 2, z_lo: 8; z = z_hi * 8 + z_lo), core: 2. Of those that a mesh axis runs over, the one named last changes fastest.
Arguments:
- particles: float32 [32, 16, 128, 8, 128], P('gx', 'gy'), may hold values from -4 to 4, as said below
- send_list: int32 [32, 16, 4, 64], P('gx', 'gy'), may hold values from 0 to 127, as said below
- move_count: int32 [32, 16, 2, 4], P('gx', 'gy'), may hold values from 0 to 16, as said below
- tile_pairs: int32 [32, 16, 512, 2], P('gx', 'gy'), may hold values from 0 to 383, as said below
- tile_count: int32 [32, 16], P('gx', 'gy'), may hold values from 128 to 512, as said below
- drag_tiles: int32 [32, 16, 384, 4], P('gx', 'gy'), may hold values from 0 to 99, as said below
- cell_slot: int32 [32, 16, 384, 128], P('gx', 'gy'), may hold values from 0 to 511
- fluid_velocity: float32 [3, 256, 128, 128], P(None, 'gx', 'gy'), may hold values from -6 to 6
- pressure_init: float32 [256, 128, 128], P('gx', 'gy'), may hold values from -6 to 6
- source: float32 [256, 128, 128], P('gx', 'gy'), may hold values from -6 to 6
- solid_old: float32 [256, 128, 128], P('gx', 'gy'), may hold values from 0 to 0.5
- screening: float32 [256, 128, 128], P('gx', 'gy'), may hold values from 0.5 to 2
Outputs:
- pressure: float32 [256, 128, 128], P('gx', 'gy')
- drag_sum: float32 [3, 256, 128, 128], P(None, 'gx', 'gy')
- block_force: float32 [32, 16, 384, 3, 128], P('gx', 'gy')
The draws below stay inside these ranges and needn't reach their ends.
Inputs may be any that keep to these rules, and one draw needn't show every extreme that they name: `particles`: positions lie in 0 to 3, radii in 0.3 to 0.7, drag coefficients in 0.5 to 4. `send_list`: row d of a device sends toward the neighbour of higher gx (d 0), lower gx (1), higher gy (2), lower gy (3). Its first move_count[0, d] entries are blocks that move there, all different over the four rows; the others are copies, and every slot is sent. `move_count`: entry [0, d] counts blocks leaving in direction d of send_list; entry [1, d] equals entry [0, d] of the neighbour that feeds received group d (lower gx, higher gx, lower gy, higher gy). Counts toward or from outside the grid are 0; 16 is reached in every draw. `tile_pairs`: the first block of every tile slot is owned by the device after migration; the second is an own block or a slot received from a neighbour inside the grid. `tile_count`: devices at the lowest and highest gy use all 512 tiles. `drag_tiles`: the 4 columns of a block are different.
All inputs are finite; a program needn't handle non-finite values.
Results may differ from the reference program's by a relative error of at most 0.0003.
Values sent between devices are 32-bit elements; how exact they have to be, the bound alone decides.
No kernel may reach another device: no remote copies, remote signals or barrier semaphores. Data moves between devices by JAX's collectives and lax.ppermute only.
A program may use at most 64 MiB of HBM per device.

```python
import jax
import jax.numpy as jnp
from jax import lax

CX = 8
CY = 8
NZ = 128
NB = 128
BLK = 128
K = 4
ITERS = 4
SLOTS = 64
MIGMAX = 16
POOL = 384
MAXT = 512
COLS = 100
NX = 256
NY = 128
N_GX = 32
N_GY = 16


def layout(key):
    keys = jax.random.split(jax.random.fold_in(key, 5), 6)
    grid_x = jnp.arange(N_GX)[:, None, None]
    grid_y = jnp.arange(N_GY)[None, :, None]
    heading = jnp.arange(4)[None, None, :]
    outward = (heading == 0) & (grid_x == N_GX - 1) | (heading == 1) & (grid_x == 0) | (heading == 2) & (grid_y == N_GY - 1) | (heading == 3) & (grid_y == 0)
    leave_count = jax.random.randint(keys[0], (N_GX, N_GY, 4), 0, MIGMAX + 1)
    leave_count = jnp.where(outward, 0, leave_count).at[0, 0, 0].set(MIGMAX).astype(jnp.int32)
    arrive_count = jnp.stack([jnp.roll(leave_count[:, :, 0], 1, axis=0), jnp.roll(leave_count[:, :, 1], -1, axis=0), jnp.roll(leave_count[:, :, 2], 1, axis=1), jnp.roll(leave_count[:, :, 3], -1, axis=1)], axis=-1)
    inward = jnp.stack([jnp.arange(N_GX)[:, None] > 0 + jnp.zeros((1, N_GY), jnp.int32), jnp.arange(N_GX)[:, None] < N_GX - 1 + jnp.zeros((1, N_GY), jnp.int32), jnp.arange(N_GY)[None, :] > 0 + jnp.zeros((N_GX, 1), jnp.int32), jnp.arange(N_GY)[None, :] < N_GY - 1 + jnp.zeros((N_GX, 1), jnp.int32)], axis=-1)
    scores = jax.random.randint(keys[1], (N_GX, N_GY, NB), 0, 1 << 20) * NB + jnp.arange(NB)[None, None, :]
    shuffled = jnp.argsort(scores, axis=-1).astype(jnp.int32)
    slot_iota = jnp.arange(SLOTS)[None, None, None, :]
    where_from = jnp.minimum(heading[..., None] * MIGMAX + slot_iota, NB - 1) + jnp.zeros((N_GX, N_GY, 4, SLOTS), jnp.int32)
    migrant = jnp.take_along_axis(jnp.broadcast_to(shuffled[:, :, None, :], (N_GX, N_GY, 4, NB)), where_from, axis=-1)
    copies = jax.random.randint(keys[2], (N_GX, N_GY, 4, SLOTS), 0, NB)
    send_list = jnp.where(slot_iota < leave_count[..., None], migrant, copies).astype(jnp.int32)
    leaving = (send_list[..., None] == jnp.arange(NB)[None, None, None, None, :]) & (slot_iota[..., None] < leave_count[..., None, None])
    stayed = jnp.logical_not(jnp.any(leaving, axis=(2, 3))).astype(jnp.int32)
    arrived = (slot_iota < arrive_count[..., None]).astype(jnp.int32).reshape(N_GX, N_GY, 4 * SLOTS)
    owned = jnp.concatenate([stayed, arrived], axis=-1)
    present = jnp.concatenate([jnp.ones((N_GX, N_GY, NB), jnp.int32), jnp.broadcast_to(inward[..., None], (N_GX, N_GY, 4, SLOTS)).astype(jnp.int32).reshape(N_GX, N_GY, 4 * SLOTS)], axis=-1)
    wall = (jnp.arange(N_GY)[None, :] == 0) | (jnp.arange(N_GY)[None, :] == N_GY - 1)
    wall = wall | jnp.zeros((N_GX, 1), bool)
    tile_count = jnp.where(wall, MAXT, jax.random.randint(keys[3], (N_GX, N_GY), MAXT // 4, MAXT // 2 + 1)).astype(jnp.int32)
    pool_iota = jnp.arange(POOL)[None, None, :]
    owned_order = jnp.argsort((1 - owned) * POOL + pool_iota, axis=-1)
    present_order = jnp.argsort((1 - present) * POOL + pool_iota, axis=-1)
    owned_total = jnp.sum(owned, axis=-1)
    present_total = jnp.sum(present, axis=-1)
    first_rank = jax.random.randint(keys[4], (N_GX, N_GY, MAXT), 0, owned_total[..., None])
    second_rank = jax.random.randint(keys[5], (N_GX, N_GY, MAXT), 0, present_total[..., None])
    first_block = jnp.take_along_axis(owned_order, first_rank, axis=-1)
    second_block = jnp.take_along_axis(present_order, second_rank, axis=-1)
    tile_pairs = jnp.stack([first_block, second_block], axis=-1).astype(jnp.int32)
    move_count = jnp.stack([leave_count, arrive_count], axis=2).astype(jnp.int32)
    return (send_list, move_count, tile_pairs, tile_count)


def draw_send_list(key, part):
    return layout(key)[0]


def draw_move_count(key, part):
    return layout(key)[1]


def draw_tile_pairs(key, part):
    return layout(key)[2]


def draw_tile_count(key, part):
    return layout(key)[3]


def draw_drag_tiles(key, part):
    scores = jax.random.randint(jax.random.fold_in(key, 9), (N_GX, N_GY, POOL, COLS), 0, 1 << 20) * COLS + jnp.arange(COLS)[None, None, None, :]
    return jnp.argsort(scores, axis=-1)[..., :K].astype(jnp.int32)


def draw_particles(key, part):
    keys = jax.random.split(jax.random.fold_in(key, 11), 4)
    spot_shape = (N_GX, N_GY, NB, 3, BLK)
    lone_shape = (N_GX, N_GY, NB, 1, BLK)
    spot = jax.random.uniform(keys[0], spot_shape, jnp.float32, 0.0, 3.0)
    radius = jax.random.uniform(keys[1], lone_shape, jnp.float32, 0.3, 0.7)
    speed = jnp.clip(jax.random.normal(keys[2], spot_shape, jnp.float32), -4.0, 4.0)
    coeff = jnp.exp(jax.random.uniform(keys[3], lone_shape, jnp.float32, jnp.log(0.5), jnp.log(4.0)))
    return jnp.concatenate([spot, radius, speed, coeff], axis=3).astype(jnp.float32)


def with_ends(array, key, least, top_value):
    spot = [jax.random.randint(jax.random.fold_in(key, axis), (), 0, length) for axis, length in enumerate(array.shape)]
    main_axis = array.shape.index(max(array.shape))
    beside = spot[:main_axis] + [(spot[main_axis] + 1) % array.shape[main_axis]] + spot[main_axis + 1:]
    return array.at[tuple(spot)].set(least).at[tuple(beside)].set(top_value)


def block_scale(rng, extent, cuts, least, high):
    level = 1.0
    for dim, blocks in cuts:
        steps = jax.random.uniform(jax.random.fold_in(jax.random.fold_in(rng, 6), dim), (blocks,), jnp.float32, least / len(cuts), high / len(cuts))
        level = level * jnp.repeat(jnp.exp(steps), extent[dim] // blocks).reshape((-1,) + (1,) * (len(extent) - 1 - dim))
    return level


def gaussian(rng, extent, deviation, bound, cuts=(), kind=jnp.bfloat16):
    entries = deviation * jax.random.normal(rng, extent, jnp.float32)
    if cuts:
        entries = entries * block_scale(rng, extent, cuts, -0.22, 0.18)
    return jnp.clip(entries, -bound, bound).astype(kind)


def setup_inputs(seed: int = 0) -> dict:
    key_of = jax.random.split(jax.random.key(seed), 13)
    particles = draw_particles(jax.random.fold_in(key_of[12], 71), 0)
    send_list = draw_send_list(jax.random.fold_in(key_of[12], 71), 0)
    move_count = draw_move_count(jax.random.fold_in(key_of[12], 71), 0)
    tile_pairs = draw_tile_pairs(jax.random.fold_in(key_of[12], 71), 0)
    tile_count = draw_tile_count(jax.random.fold_in(key_of[12], 71), 0)
    drag_tiles = draw_drag_tiles(jax.random.fold_in(key_of[12], 71), 0)
    cell_slot = with_ends(jax.random.randint(key_of[6], (N_GX, N_GY, POOL, BLK), 0, K * NZ), jax.random.fold_in(key_of[6], 1), 0, (K * NZ) - 1).astype(jnp.int32)
    fluid_velocity = gaussian(key_of[7], (3, NX, NY, NZ), 1.0, 6.0, ((1, 32), (2, 16)), jnp.float32)
    pressure_init = gaussian(key_of[8], (NX, NY, NZ), 1.0, 6.0, ((0, 32), (1, 16)), jnp.float32)
    source = gaussian(key_of[9], (NX, NY, NZ), 1.0, 6.0, ((0, 32), (1, 16)), jnp.float32)
    solid_old = jnp.clip(0.5 * jax.random.uniform(key_of[10], (NX, NY, NZ), jnp.float32) ** block_scale(key_of[10], (NX, NY, NZ), ((0, 32), (1, 16)), -0.2, 0.2), 0.0, 0.5)
    screening = jnp.clip(0.5 + 1.5 * jax.random.uniform(key_of[11], (NX, NY, NZ), jnp.float32) ** block_scale(key_of[11], (NX, NY, NZ), ((0, 32), (1, 16)), -0.2, 0.2), 0.5, 2.0)
    return dict(particles=particles, send_list=send_list, move_count=move_count, tile_pairs=tile_pairs, tile_count=tile_count, drag_tiles=drag_tiles, cell_slot=cell_slot, fluid_velocity=fluid_velocity, pressure_init=pressure_init, source=source, solid_old=solid_old, screening=screening)


topmost_value = lax.Precision.HIGHEST
stiffness = 0.5
density_ratio = 2.0
tile_group = 32
block_groups = 6


def gather_pool(particles, send_list, grid_x, grid_y):
    own_blocks = particles[grid_x, grid_y]
    pieces = [own_blocks]
    for step_x, step_y, heading in ((-1, 0, 0), (1, 0, 1), (0, -1, 2), (0, 1, 3)):
        source_x = grid_x + step_x
        source_y = grid_y + step_y
        inside = (source_x >= 0) & (source_x < N_GX) & (source_y >= 0) & (source_y < N_GY)
        clip_x = jnp.clip(source_x, 0, N_GX - 1)
        clip_y = jnp.clip(source_y, 0, N_GY - 1)
        picked = particles[clip_x, clip_y][send_list[clip_x, clip_y, heading]]
        pieces.append(jnp.where(inside, picked, jnp.zeros_like(picked)))
    return jnp.concatenate(pieces, axis=0)


def ownership(send_rows, leave_count, arrive_count, block_count):
    slot_count = send_rows.shape[1]
    slot_iota = jnp.arange(slot_count, dtype=jnp.int32)
    leaving = (send_rows[:, :, None] == jnp.arange(block_count, dtype=jnp.int32)[None, None, :]) & (slot_iota[None, :, None] < leave_count[:, None, None])
    stayed = jnp.logical_not(jnp.any(leaving, axis=(0, 1)))
    arrived = slot_iota[None, :] < arrive_count[:, None]
    return jnp.concatenate([stayed, arrived.reshape(-1)]).astype(jnp.float32)


def contact_forces(block_pool, tile_rows, tile_total):
    slot_total = tile_rows.shape[0]
    grouped = tile_rows.reshape(slot_total // tile_group, tile_group, 2)
    marks = (jnp.arange(slot_total, dtype=jnp.int32) < tile_total).astype(jnp.float32).reshape(-1, tile_group)

    def tile_step(force_total, step_item):
        pair_group, mark_group = step_item
        first_side = block_pool[pair_group[:, 0], 0:4, :]
        second_side = block_pool[pair_group[:, 1], 0:4, :]
        distance = (first_side[:, 0, :, None] - second_side[:, 0, None, :]) ** 2
        distance = distance + (first_side[:, 1, :, None] - second_side[:, 1, None, :]) ** 2
        distance = distance + (first_side[:, 2, :, None] - second_side[:, 2, None, :]) ** 2
        reach = first_side[:, 3, :, None] + second_side[:, 3, None, :]
        weight = jnp.maximum(1.0 - distance / (reach * reach), 0.0) * mark_group[:, None, None]
        pulled = jnp.einsum('tab,tcb->tca', weight, second_side[:, 0:3, :], precision=topmost_value)
        pushed = first_side[:, 0:3, :] * jnp.sum(weight, axis=2)[:, None, :]
        return force_total.at[pair_group[:, 0]].add(stiffness * (pushed - pulled)), None

    start_force = jnp.zeros((block_pool.shape[0], 3, block_pool.shape[2]), jnp.float32)
    force_total, unused = lax.scan(tile_step, start_force, (grouped, marks))
    return force_total


def couple(block_pool, owned_mask, tile_ids, slot_ids, columns):
    depth_count = columns.shape[2]
    column_count = columns.shape[0]
    tile_width = tile_ids.shape[1]
    per_group = block_pool.shape[0] // block_groups

    def group_advance(deposit, step_item):
        block_state, owned_rows, group_tiles, group_slots = step_item
        depth_ids = group_slots % depth_count
        slot_tile = group_slots // depth_count
        depth_pick = (depth_ids[:, :, None] == jnp.arange(depth_count, dtype=jnp.int32)[None, None, :]).astype(jnp.float32)
        slot_selection = (slot_tile[:, :, None] == jnp.arange(tile_width, dtype=jnp.int32)[None, None, :]).astype(jnp.float32)
        local_flow = columns[group_tiles]
        depth_position = jnp.einsum('gkcz,gpz->gkcp', local_flow, depth_pick, precision=topmost_value)
        fluid_sampled_locally = jnp.einsum('hxdq,hqx->hdq', depth_position, slot_selection, precision=topmost_value)
        drag_force = block_state[:, 7:8, :] * (fluid_sampled_locally - block_state[:, 4:7, :]) * owned_rows[:, None, None]
        volume = block_state[:, 3:4, :] ** 3 * owned_rows[:, None, None]
        loading_contributions = jnp.concatenate([drag_force, volume], axis=1)
        slot_breakdown = jnp.einsum('bfm,bmd->bdfm', loading_contributions, slot_selection, precision=topmost_value)
        spread = jnp.einsum('gkcp,gpz->gkcz', slot_breakdown, depth_pick, precision=topmost_value)
        column_pick = (group_tiles[:, :, None] == jnp.arange(column_count, dtype=jnp.int32)[None, None, :]).astype(jnp.float32)
        deposit = deposit + jnp.einsum('gkn,gkcz->ncz', column_pick, spread, precision=topmost_value)
        return deposit, drag_force

    step_items = (block_pool.reshape(block_groups, per_group, block_pool.shape[1], block_pool.shape[2]),
                  owned_mask.reshape(block_groups, per_group),
                  tile_ids.reshape(block_groups, per_group, tile_width),
                  slot_ids.reshape(block_groups, per_group, slot_ids.shape[1]))
    start_deposit = jnp.zeros((column_count, 4, depth_count), jnp.float32)
    deposit, drag_force = lax.scan(group_advance, start_deposit, step_items)
    return drag_force.reshape(block_pool.shape[0], 3, block_pool.shape[2]), deposit


def reference(particles, send_list, move_count, tile_pairs, tile_count, drag_tiles, cell_slot, fluid_velocity, pressure_init, source, solid_old, screening):
    flow_padded = jnp.pad(fluid_velocity, ((0, 0), (1, 1), (1, 1), (0, 0)))
    column_count = (CX + 2) * (CY + 2)
    zero_index = jnp.zeros((), jnp.int32)

    def per_device(device_flat):
        grid_x = (device_flat // N_GY).astype(jnp.int32)
        grid_y = (device_flat % N_GY).astype(jnp.int32)
        block_pool = gather_pool(particles, send_list, grid_x, grid_y)
        owned_mask = ownership(send_list[grid_x, grid_y], move_count[grid_x, grid_y, 0], move_count[grid_x, grid_y, 1], NB)
        contact = contact_forces(block_pool, tile_pairs[grid_x, grid_y], tile_count[grid_x, grid_y])
        window = lax.dynamic_slice(flow_padded, (zero_index, grid_x * CX, grid_y * CY, zero_index), (3, CX + 2, CY + 2, NZ))
        columns = window.reshape(3, column_count, NZ).transpose(1, 0, 2)
        drag_force, deposit = couple(block_pool, owned_mask, drag_tiles[grid_x, grid_y], cell_slot[grid_x, grid_y], columns)
        return contact + drag_force, deposit.transpose(1, 0, 2).reshape(4, CX + 2, CY + 2, NZ)

    forces, deposits = lax.map(per_device, jnp.arange(N_GX * N_GY, dtype=jnp.int32))

    def place(device_flat, field):
        grid_x = (device_flat // N_GY).astype(jnp.int32)
        grid_y = (device_flat % N_GY).astype(jnp.int32)
        corner = (zero_index, grid_x * CX, grid_y * CY, zero_index)
        current = lax.dynamic_slice(field, corner, (4, CX + 2, CY + 2, NZ))
        return lax.dynamic_update_slice(field, current + deposits[device_flat], corner)

    field = lax.fori_loop(0, N_GX * N_GY, place, jnp.zeros((4, NX + 2, NY + 2, NZ), jnp.float32))
    loads = field[:, 1:-1, 1:-1]
    drag_sum = loads[0:3]
    relax_gain = 1.0 / (6.0 + screening)
    offset = relax_gain * (source + density_ratio * (loads[3] - solid_old))
    pressure = pressure_init
    for sweep_turn in range(ITERS):
        padded = jnp.pad(pressure, 1)
        neighbours = padded[2:, 1:-1, 1:-1] + padded[:-2, 1:-1, 1:-1]
        neighbours = neighbours + padded[1:-1, 2:, 1:-1] + padded[1:-1, :-2, 1:-1]
        neighbours = neighbours + padded[1:-1, 1:-1, 2:] + padded[1:-1, 1:-1, :-2]
        pressure = relax_gain * neighbours + offset
    return pressure, drag_sum, forces.reshape(N_GX, N_GY, POOL, 3, BLK)
```

```python
import functools

import jax
import jax.numpy as jnp
from jax import lax
from jax.experimental import pallas as pl
from jax.experimental.pallas import tpu as pltpu
from jax.sharding import PartitionSpec as P

F32 = jnp.float32
BF16 = jnp.bfloat16
NB = 128
SLOTS = 64
MOVERS = 16
PAIRS = (SLOTS - MOVERS) // 2
GROUP = MOVERS + PAIRS
OWNABLE = NB + 4 * MOVERS
POOL_TILES = NB + 4 * GROUP
ITERS = 4

VM = pl.BlockSpec(memory_space=pltpu.VMEM)
SM = pl.BlockSpec(memory_space=pltpu.SMEM)
PARAMS = pltpu.CompilerParams(vmem_limit_bytes=32 * 2**20)


def shape(*dims):
    return jax.ShapeDtypeStruct(dims, F32)


def call(kernel, outs, in_specs, scratch=(), flops=10**6, moved=10**6):
    return pl.pallas_call(
        kernel,
        out_shape=outs,
        in_specs=in_specs,
        out_specs=jax.tree.map(lambda _: VM, outs),
        scratch_shapes=list(scratch),
        compiler_params=PARAMS,
        cost_estimate=pl.CostEstimate(flops=flops, bytes_accessed=moved, transcendentals=0),
    )


def put_blocks(parts, sends, direction, out):
    for s in range(MOVERS):
        out[s] = parts[sends[direction, s]]
    for k in range(PAIRS):
        out[MOVERS + k, 0:4, :] = parts[sends[direction, MOVERS + k], 0:4, :]
        out[MOVERS + k, 4:8, :] = parts[sends[direction, MOVERS + PAIRS + k], 0:4, :]


def pack_y(parts, sends, flow, pres, screen, source, solid, out_e, out_o, gain_ref, rest_ref):
    parity = lax.axis_index("gy") % 2
    gain_ref[...] = 1.0 / (6.0 + screen[...])
    rest_ref[...] = source[...] - 2.0 * solid[...]
    for out, up in ((out_e, parity == 0), (out_o, parity == 1)):
        put_blocks(parts, sends, jnp.where(up, 2, 3), out)
        for c in range(3):
            out[GROUP + c] = jnp.where(up, flow[c, :, 7, :], flow[c, :, 0, :])
        at = GROUP + 3
        for ref in (pres, gain_ref, rest_ref):
            for x in range(8):
                row = 4 * (x % 2)
                out[at + x // 2, row : row + 4, :] = jnp.where(up, ref[x, 4:8, :], ref[x, 0:4, :])
            at += 4


Y_TILES = GROUP + 3 + 12
X_TILES = GROUP + 6 + 8 + 6 + 6


def pack_x(
    parts, sends, flow, pres, gain, rest, in_e, in_o, out_e, out_o, flow_x, pres_x, gain_x, rest_x
):
    parity = lax.axis_index("gy") % 2
    even = parity == 0
    for c in range(3):
        flow_x[c, :, 4:12, :] = flow[c]
        a = in_e[GROUP + c]
        b = in_o[GROUP + c]
        flow_x[c, :, 12, :] = jnp.where(even, a, b)
        flow_x[c, :, 3, :] = jnp.where(even, b, a)
    at = GROUP + 3
    for wide, ref in ((pres_x, pres), (gain_x, gain), (rest_x, rest)):
        wide[:, 4:12, :] = ref[...]
        for x in range(8):
            row = 4 * (x % 2)
            a = in_e[at + x // 2, row : row + 4, :]
            b = in_o[at + x // 2, row : row + 4, :]
            wide[x, 12:16, :] = jnp.where(even, a, b)
            wide[x, 0:4, :] = jnp.where(even, b, a)
        at += 4
    parity = lax.axis_index("gx") % 2
    for out, up in ((out_e, parity == 0), (out_o, parity == 1)):
        put_blocks(parts, sends, jnp.where(up, 0, 1), out)
        at = GROUP
        for c in range(3):
            edge = jnp.where(up, 7, 0)
            out[at] = flow_x[c, edge, 0:8, :]
            out[at + 1] = flow_x[c, edge, 8:16, :]
            at += 2
        for wide, count in ((pres_x, 4), (gain_x, 3), (rest_x, 3)):
            first = jnp.where(up, 8 - count, 0)
            for r in range(count):
                out[at] = wide[first + r, 0:8, :]
                out[at + 1] = wide[first + r, 8:16, :]
                at += 2


def couple(
    parts, sends, moves, tiles, slots, flow_x, in_xe, in_xo, in_ye, in_yo,
    drag, dep, out_e, out_o,
    pool, table, sums, owned,
):
    x_even = lax.axis_index("gx") % 2 == 0
    y_even = lax.axis_index("gy") % 2 == 0
    pool[0:NB] = parts[...]
    for d, (up, even, a, b) in enumerate(
        ((0, x_even, in_xe, in_xo), (1, x_even, in_xe, in_xo), (0, y_even, in_ye, in_yo), (1, y_even, in_ye, in_yo))
    ):
        first, second = (b, a) if up == 0 else (a, b)
        pool[NB + d * MOVERS : NB + (d + 1) * MOVERS] = jnp.where(even, first[0:MOVERS], second[0:MOVERS])

    def stay(k, carry):
        owned[k] = 1.0
        return carry

    lax.fori_loop(0, NB, stay, 0)
    for d in range(4):

        def leave(s, carry, d=d):
            owned[sends[d, s]] = 0.0
            return carry

        lax.fori_loop(0, moves[0, d], leave, 0)
        for s in range(MOVERS):
            owned[NB + d * MOVERS + s] = jnp.where(s < moves[1, d], 1.0, 0.0)
    for c in range(3):
        high = jnp.where(x_even, in_xe[GROUP + 2 * c], in_xo[GROUP + 2 * c])
        high2 = jnp.where(x_even, in_xe[GROUP + 2 * c + 1], in_xo[GROUP + 2 * c + 1])
        low = jnp.where(x_even, in_xo[GROUP + 2 * c], in_xe[GROUP + 2 * c])
        low2 = jnp.where(x_even, in_xo[GROUP + 2 * c + 1], in_xe[GROUP + 2 * c + 1])
        for x in range(10):
            if x == 0:
                one, two = low, low2
            elif x == 9:
                one, two = high, high2
            else:
                one, two = flow_x[c, x - 1, 0:8, :], flow_x[c, x - 1, 8:16, :]
            table[x * 10 : x * 10 + 5, 4 + c, :] = one[3:8]
            table[x * 10 + 5 : x * 10 + 10, 4 + c, :] = two[0:5]
    sums[...] = jnp.zeros_like(sums)
    drag[...] = jnp.zeros_like(drag)

    row = lax.broadcasted_iota(jnp.int32, (8, NB), 0)
    low_rows = row < 4
    last_row = row == 7
    half = jnp.where(low_rows, 0, 1)
    depth_rows = lax.broadcasted_iota(jnp.int32, (128, NB), 0)

    def one_block(m, at):
        own = owned[m]
        state = pool[m]
        code = jnp.broadcast_to(slots[pl.ds(at, 1), :], (8, NB))
        depth = code & 127
        slot = code >> 7
        columns = [tiles[k, at] for k in range(4)]
        seen = [jnp.take_along_axis(table[n], depth, axis=1, mode="promise_in_bounds") for n in columns]
        at_particle = jnp.where(
            slot < 2, jnp.where(slot == 0, seen[0], seen[1]), jnp.where(slot == 2, seen[2], seen[3])
        )
        coeff = jnp.broadcast_to(state[7:8], (8, NB))
        radius = jnp.broadcast_to(state[3:4], (8, NB))
        values = jnp.where(last_row, radius * radius * radius, coeff * (at_particle - state)) * own
        both = jnp.where(low_rows, pltpu.roll(values, 4, 0), values)
        for c in range(3):
            drag[c, pl.ds(at, 1), :] = both[c : c + 1]
        first = jnp.where(slot == half, both, 0.0)
        second = jnp.where(slot == half + 2, both, 0.0)
        sixteen = jnp.concatenate([first, second], axis=0)
        upper = sixteen.astype(BF16)
        lower = (sixteen - upper.astype(F32)).astype(BF16)
        pick = (depth_rows == jnp.broadcast_to(depth[0:1], (128, NB))).astype(BF16)
        spread = lax.dot_general(
            jnp.concatenate([upper, lower], axis=0), pick, (((1,), (1,)), ((), ())),
            preferred_element_type=F32,
        )
        spread = spread[0:16] + spread[16:32]
        parts_ = (
            jnp.where(low_rows, spread[0:8], 0.0), jnp.where(low_rows, 0.0, spread[0:8]),
            jnp.where(low_rows, spread[8:16], 0.0), jnp.where(low_rows, 0.0, spread[8:16]),
        )
        return columns, parts_

    def add(columns, pieces):
        olds = [sums[n] for n in columns]
        for n, old, piece in zip(columns, olds, pieces, strict=True):
            sums[n] = old + piece

    def blocks(g, carry):
        made = []
        for u in range(4):
            m = g * 4 + u
            at = jnp.where(m < NB, m, NB + ((m - NB) // MOVERS) * SLOTS + (m - NB) % MOVERS)
            made.append(one_block(m, at))
        for columns, pieces in made:
            add(columns, pieces)
        return carry

    lax.fori_loop(0, OWNABLE // 4, blocks, 0)
    dep[...] = jnp.zeros_like(dep)
    for n in range(100):
        total = sums[n]
        total = total[0:4] + total[4:8]
        for f in range(4):
            dep[f, n // 10, n % 10 + 3, :] = total[f]
    for out, up in ((out_e, y_even), (out_o, jnp.logical_not(y_even))):
        for f in range(4):
            for x in range(10):
                i = f * 10 + x
                r = 4 * (i % 2)
                out[i // 2, r : r + 4, :] = jnp.where(up, dep[f, x, 9:13, :], dep[f, x, 3:7, :])


def fold_y(dep, in_e, in_o, dep_x, out_e, out_o):
    even = lax.axis_index("gy") % 2 == 0
    dep_x[...] = dep[...]
    for f in range(4):
        for x in range(10):
            i = f * 10 + x
            r = 4 * (i % 2)
            a = in_e[i // 2, r : r + 4, :]
            b = in_o[i // 2, r : r + 4, :]
            dep_x[f, x, 11:15, :] += jnp.where(even, a, b)
            dep_x[f, x, 1:5, :] += jnp.where(even, b, a)
    parity = lax.axis_index("gx") % 2
    for out, up in ((out_e, parity == 0), (out_o, parity == 1)):
        first = jnp.where(up, 6, 0)
        rim = jnp.where(up, 9, 0)
        for r in range(4):
            out[2 * r] = dep_x[3, first + r, 0:8, :]
            out[2 * r + 1] = dep_x[3, first + r, 8:16, :]
        for c in range(3):
            out[8 + 2 * c] = dep_x[c, rim, 0:8, :]
            out[9 + 2 * c] = dep_x[c, rim, 8:16, :]


D_TILES = 14


def tiles16(ref, at):
    return jnp.concatenate([ref[at], ref[at + 1]], axis=0)


def finish(dep_x, in_e, in_o, near_e, near_o, pres_x, gain_x, rest_x, pressure, drag_sum, now, new, gain, off):
    even = lax.axis_index("gx") % 2 == 0

    def from_up(a, b, at):
        return jnp.where(even, tiles16(a, at), tiles16(b, at))

    def from_down(a, b, at):
        return jnp.where(even, tiles16(b, at), tiles16(a, at))

    for c in range(3):
        drag_sum[c] = dep_x[c, 1:9, 4:12, :]
        drag_sum[c, 0] += from_down(in_e, in_o, 8 + 2 * c)[4:12]
        drag_sum[c, 7] += from_up(in_e, in_o, 8 + 2 * c)[4:12]
    p_at = GROUP + 6
    g_at = p_at + 8
    s_at = g_at + 6
    for x in range(16):
        if x < 4:
            now[x] = from_down(near_e, near_o, p_at + 2 * x)
        elif x < 12:
            now[x] = pres_x[x - 4]
        else:
            now[x] = from_up(near_e, near_o, p_at + 2 * (x - 12))
    for x in range(1, 15):
        if x < 4:
            g = from_down(near_e, near_o, g_at + 2 * (x - 1))
            s = from_down(near_e, near_o, s_at + 2 * (x - 1))
        elif x < 12:
            g = gain_x[x - 4]
            s = rest_x[x - 4]
        else:
            g = from_up(near_e, near_o, g_at + 2 * (x - 12))
            s = from_up(near_e, near_o, s_at + 2 * (x - 12))
        load = jnp.zeros((16, 128), F32)
        if 3 <= x <= 12:
            load = load + dep_x[3, x - 3]
        if x <= 4:
            load = load + from_down(in_e, in_o, 2 * (x - 1))
        if x >= 11:
            load = load + from_up(in_e, in_o, 2 * (x - 11))
        gain[x] = g
        off[x] = g * (s + 2.0 * load)
    lane = lax.broadcasted_iota(jnp.int32, (16, 128), 1)
    inner_low = lane > 0
    inner_high = lane < 127
    source, target = now, new
    for sweep in range(ITERS):
        for x in range(sweep + 1, 15 - sweep):
            p = source[x]
            near = source[x - 1] + source[x + 1]
            near = near + pltpu.roll(p, 1, 0) + pltpu.roll(p, 15, 0)
            near = near + jnp.where(inner_low, pltpu.roll(p, 1, 1), 0.0)
            near = near + jnp.where(inner_high, pltpu.roll(p, 127, 1), 0.0)
            target[x] = gain[x] * near + off[x]
        source, target = target, source
    pressure[...] = source[4:12, 4:12, :]


def contact(pairs, count, parts, in_xe, in_xo, in_ye, in_yo, drag, after, force, pool):
    x_even = lax.axis_index("gx") % 2 == 0
    y_even = lax.axis_index("gy") % 2 == 0
    pool[0 : NB * 8] = parts[...].reshape(NB * 8, 128)
    for d, (up, even, a, b) in enumerate(
        ((0, x_even, in_xe, in_xo), (1, x_even, in_xe, in_xo), (0, y_even, in_ye, in_yo), (1, y_even, in_ye, in_yo))
    ):
        first, second = (b, a) if up == 0 else (a, b)
        at = (NB + d * GROUP) * 8
        pool[at : at + GROUP * 8] = jnp.where(even, first[0:GROUP], second[0:GROUP]).reshape(GROUP * 8, 128)
    force[...] = drag[...]
    total = count[0, 0]

    def row_of(m):
        q = m - NB
        d = q // SLOTS
        s = q % SLOTS
        base = (NB + d * GROUP) * 8
        tail = jnp.where(
            s < MOVERS + PAIRS, 8 * s, 8 * (s - PAIRS) + 4
        )
        return jnp.where(m < NB, 8 * m, base + tail)

    def tile(t):
        i = pairs[0, t]
        j = pairs[1, t]
        x = pool[pl.ds(pl.multiple_of(row_of(i), 4), 4), :]
        y = pool[pl.ds(pl.multiple_of(row_of(j), 4), 4), :]
        xs = [jnp.broadcast_to(x[c : c + 1], (8, 128)) for c in range(4)]
        ys = [
            pltpu.roll(jnp.broadcast_to(y[c : c + 1], (8, 128)), 0, 1, stride=1, stride_axis=0)
            for c in range(4)
        ]
        sums = [jnp.zeros((8, 128), F32) for _ in range(3)]
        for step in range(16):
            turned = ys if step == 0 else [pltpu.roll(v, 8 * step, 1) for v in ys]
            apart = [xs[c] - turned[c] for c in range(3)]
            distance = apart[0] * apart[0] + apart[1] * apart[1] + apart[2] * apart[2]
            reach = xs[3] + turned[3]
            reach = reach * reach
            guess = pl.reciprocal(reach, approx=True)
            inverse = guess * (2.0 - reach * guess)
            weight = jnp.maximum(1.0 - distance * inverse, 0.0)
            sums = [s + weight * a for s, a in zip(sums, apart, strict=True)]
        scale = jnp.where(t < total, 0.5, 0.0)
        return i, [jnp.sum(s, axis=0, keepdims=True) * scale for s in sums]

    unroll = 4

    def step(g, carry):
        made = [tile(g * unroll + u) for u in range(unroll)]
        for i, sums in made:
            for c in range(3):
                force[c, pl.ds(i, 1), :] += sums[c]
        return carry

    lax.fori_loop(0, (total + unroll - 1) // unroll, step, 0)


def pairs_of(first, count, last):
    up = [(i, i + 1) for i in range(first, last, 2)]
    return up + [(b, a) for a, b in up]


def swap(array, axis, first):
    count = lax.axis_size(axis)
    return lax.ppermute(array, axis, pairs_of(first, count, count - 1))


def body(
    particles,
    send_list,
    move_count,
    tile_pairs,
    tile_count,
    drag_tiles,
    cell_slot,
    fluid_velocity,
    pressure_init,
    source,
    solid_old,
    screening,
):
    parts = particles[0, 0]
    sends = send_list[0, 0]
    moves = move_count[0, 0]
    tiles = drag_tiles[0, 0].T
    pairs = tile_pairs[0, 0].T
    slots = cell_slot[0, 0]
    cells = (8, 8, 128)
    wide = (8, 16, 128)
    ye, yo, gain, rest = call(
        pack_y, (shape(Y_TILES, 8, 128), shape(Y_TILES, 8, 128), shape(*cells), shape(*cells)), [VM, SM] + [VM] * 5
    )(parts, sends, fluid_velocity, pressure_init, screening, source, solid_old)
    got_ye = swap(ye, "gy", 0)
    got_yo = swap(yo, "gy", 1)
    xe, xo, flow_x, pres_x, gain_x, rest_x = call(
        pack_x,
        (shape(X_TILES, 8, 128), shape(X_TILES, 8, 128), shape(3, *wide), shape(*wide), shape(*wide), shape(*wide)),
        [VM, SM] + [VM] * 6,
    )(parts, sends, fluid_velocity, pressure_init, gain, rest, got_ye, got_yo)
    got_xo = swap(xo, "gx", 1)
    got_xe = swap(xe, "gx", 0)
    drag, dep, de, do = call(
        couple,
        (shape(3, 384, 128), shape(4, 10, 16, 128), shape(20, 8, 128), shape(20, 8, 128)),
        [VM, SM, SM, SM] + [VM] * 6,
        [
            pltpu.VMEM((OWNABLE, 8, 128), F32),
            pltpu.VMEM((100, 8, 128), F32),
            pltpu.VMEM((100, 8, 128), F32),
            pltpu.SMEM((OWNABLE,), F32),
        ],
    )(parts, sends, moves, tiles, slots, flow_x, got_xe, got_xo, got_ye, got_yo)
    got_de = swap(de, "gy", 0)
    got_do = swap(do, "gy", 1)
    dep_x, fe, fo = call(
        fold_y, (shape(4, 10, 16, 128), shape(D_TILES, 8, 128), shape(D_TILES, 8, 128)), [VM] * 3
    )(dep, got_de, got_do)
    got_fo = swap(fo, "gx", 1)
    got_fe = swap(fe, "gx", 0)
    force = call(
        contact,
        shape(3, 384, 128),
        [SM, SM] + [VM] * 7,
        [pltpu.VMEM((POOL_TILES * 8, 128), F32)],
        flops=10**9,
    )(pairs, tile_count, parts, got_xe, got_xo, got_ye, got_yo, drag, fo)
    pressure, drag_sum = call(
        finish,
        (shape(*cells), shape(3, *cells)),
        [VM] * 8,
        [pltpu.VMEM((16, 16, 128), F32)] * 4,
    )(dep_x, got_fe, got_fo, got_xe, got_xo, pres_x, gain_x, rest_x)
    return (pressure, drag_sum, force.transpose(1, 0, 2)[None, None])


def solution(mesh):
    in_specs = (
        P("gx", "gy", None, None, None),
        P("gx", "gy", None, None),
        P("gx", "gy", None, None),
        P("gx", "gy", None, None),
        P("gx", "gy"),
        P("gx", "gy", None, None),
        P("gx", "gy", None, None),
        P(None, "gx", "gy", None),
        P("gx", "gy", None),
        P("gx", "gy", None),
        P("gx", "gy", None),
        P("gx", "gy", None),
    )
    out_specs = (P("gx", "gy", None), P(None, "gx", "gy", None), P("gx", "gy", None, None, None))
    return jax.shard_map(body, mesh=mesh, in_specs=in_specs, out_specs=out_specs, check_vma=False)
```

```python
import functools

import jax
import jax.numpy as jnp
from jax import lax
from jax.experimental import pallas as pl
from jax.experimental.pallas import tpu as pltpu
from jax.sharding import PartitionSpec as P

F32 = jnp.float32
BF16 = jnp.bfloat16
NB = 128
SLOTS = 64
MOVERS = 16
PAIRS = (SLOTS - MOVERS) // 2
GROUP = MOVERS + PAIRS
OWNABLE = NB + 4 * MOVERS
POOL = 384
MAXT = 512
ITERS = 4
CONTACT_UNROLL = 32
PREPARE = 4
COUPLE_UNROLL = 32

VM = pl.BlockSpec(memory_space=pltpu.VMEM)
SM = pl.BlockSpec(memory_space=pltpu.SMEM)
HB = pl.BlockSpec(memory_space=pltpu.HBM)
PARAMS = pltpu.CompilerParams(vmem_limit_bytes=32 * 2**20)


def shape(*dims):
    return jax.ShapeDtypeStruct(dims, F32)


def call(kernel, outs, in_specs, scratch=(), flops=10**6, moved=10**6, aliases=None):
    return pl.pallas_call(
        kernel,
        out_shape=outs,
        in_specs=in_specs,
        out_specs=jax.tree.map(lambda _: VM, outs),
        scratch_shapes=list(scratch),
        input_output_aliases=aliases or {},
        compiler_params=PARAMS,
        cost_estimate=pl.CostEstimate(flops=flops, bytes_accessed=moved, transcendentals=0),
    )


def put_blocks(parts, sends, direction, out):
    for s in range(MOVERS):
        out[s] = parts[sends[direction, s]]
    for k in range(PAIRS):
        out[MOVERS + k, 0:4, :] = parts[sends[direction, MOVERS + k], 0:4, :]
        out[MOVERS + k, 4:8, :] = parts[sends[direction, MOVERS + PAIRS + k], 0:4, :]


def fetch(sources, targets, sems):
    copies = [pltpu.make_async_copy(a, b, sems.at[n]) for n, (a, b) in enumerate(zip(sources, targets, strict=True))]
    for copy in copies:
        copy.start()
    return copies


def pack_y(
    parts_in, sends_in, flow_in, pres_in, screen_in, source_in, solid_in, slots_in,
    out_e, out_o, gain_ref, rest_ref, parts, flow, pres, slots,
    sends, screen, source, solid, sems,
):
    parity = lax.axis_index("gy") % 2
    for copy in fetch(
        (sends_in, parts_in, flow_in, pres_in, screen_in, source_in, solid_in, slots_in),
        (sends, parts, flow, pres, screen, source, solid, slots),
        sems,
    ):
        copy.wait()
    gain_ref[...] = 1.0 / (6.0 + screen[...])
    rest_ref[...] = source[...] - 2.0 * solid[...]
    for out, up in ((out_e, parity == 0), (out_o, parity == 1)):
        put_blocks(parts, sends, jnp.where(up, 2, 3), out)
        for c in range(3):
            out[GROUP + c] = jnp.where(up, flow[c, :, 7, :], flow[c, :, 0, :])
        at = GROUP + 3
        for ref in (pres, gain_ref, rest_ref):
            for x in range(8):
                row = 4 * (x % 2)
                out[at + x // 2, row : row + 4, :] = jnp.where(up, ref[x, 4:8, :], ref[x, 0:4, :])
            at += 4


Y_TILES = GROUP + 3 + 12
X_TILES = GROUP + 6 + 8 + 6 + 6


def pack_x(
    parts, sends, flow, pres, gain, rest, in_e, in_o, out_o, out_e, flow_x, pres_x, gain_x, rest_x
):
    parity = lax.axis_index("gy") % 2
    even = parity == 0
    for c in range(3):
        flow_x[c, :, 4:12, :] = flow[c]
        a = in_e[GROUP + c]
        b = in_o[GROUP + c]
        flow_x[c, :, 12, :] = jnp.where(even, a, b)
        flow_x[c, :, 3, :] = jnp.where(even, b, a)
    at = GROUP + 3
    for wide, ref in ((pres_x, pres), (gain_x, gain), (rest_x, rest)):
        wide[:, 4:12, :] = ref[...]
        for x in range(8):
            row = 4 * (x % 2)
            a = in_e[at + x // 2, row : row + 4, :]
            b = in_o[at + x // 2, row : row + 4, :]
            wide[x, 12:16, :] = jnp.where(even, a, b)
            wide[x, 0:4, :] = jnp.where(even, b, a)
        at += 4
    parity = lax.axis_index("gx") % 2
    for out, up in ((out_e, parity == 0), (out_o, parity == 1)):
        put_blocks(parts, sends, jnp.where(up, 0, 1), out)
        at = GROUP
        for c in range(3):
            edge = jnp.where(up, 7, 0)
            out[at] = flow_x[c, edge, 0:8, :]
            out[at + 1] = flow_x[c, edge, 8:16, :]
            at += 2
        for wide, count in ((pres_x, 4), (gain_x, 3), (rest_x, 3)):
            first = jnp.where(up, 8 - count, 0)
            for r in range(count):
                out[at] = wide[first + r, 0:8, :]
                out[at + 1] = wide[first + r, 8:16, :]
                at += 2


def couple(
    parts, sends_in, moves_in, tiles_in, slots, flow_x, in_xe, in_xo, in_ye, in_yo, after,
    drag, dep, out_e, out_o,
    pool, table, sums, owned, sends, moves, tiles, sems,
):
    copies = fetch((sends_in, moves_in, tiles_in), (sends, moves, tiles), sems)
    x_even = lax.axis_index("gx") % 2 == 0
    y_even = lax.axis_index("gy") % 2 == 0
    pool[0:NB] = parts[...]
    for d, (up, even, a, b) in enumerate(
        ((0, x_even, in_xe, in_xo), (1, x_even, in_xe, in_xo), (0, y_even, in_ye, in_yo), (1, y_even, in_ye, in_yo))
    ):
        first, second = (b, a) if up == 0 else (a, b)
        pool[NB + d * MOVERS : NB + (d + 1) * MOVERS] = jnp.where(even, first[0:MOVERS], second[0:MOVERS])

    for c in range(3):
        high = jnp.where(x_even, in_xe[GROUP + 2 * c], in_xo[GROUP + 2 * c])
        high2 = jnp.where(x_even, in_xe[GROUP + 2 * c + 1], in_xo[GROUP + 2 * c + 1])
        low = jnp.where(x_even, in_xo[GROUP + 2 * c], in_xe[GROUP + 2 * c])
        low2 = jnp.where(x_even, in_xo[GROUP + 2 * c + 1], in_xe[GROUP + 2 * c + 1])
        for x in range(10):
            if x == 0:
                one, two = low, low2
            elif x == 9:
                one, two = high, high2
            else:
                one, two = flow_x[c, x - 1, 0:8, :], flow_x[c, x - 1, 8:16, :]
            table[x * 10 : x * 10 + 5, 4 + c, :] = one[3:8]
            table[x * 10 + 5 : x * 10 + 10, 4 + c, :] = two[0:5]
    sums[...] = jnp.zeros_like(sums)
    drag[...] = jnp.zeros_like(drag)
    for copy in copies:
        copy.wait()

    def stay(k, carry):
        owned[k] = 1.0
        return carry

    lax.fori_loop(0, NB, stay, 0)
    for d in range(4):

        def leave(s, carry, d=d):
            owned[sends[d, s]] = 0.0
            return carry

        lax.fori_loop(0, moves[0, d], leave, 0)
        for s in range(MOVERS):
            owned[NB + d * MOVERS + s] = jnp.where(s < moves[1, d], 1.0, 0.0)

    row = lax.broadcasted_iota(jnp.int32, (8, NB), 0)
    low_rows = row < 4
    last_row = row == 7
    half = jnp.where(low_rows, 0, 1)
    depth_rows = lax.broadcasted_iota(jnp.int32, (128, NB), 0)

    def one_block(m, at):
        own = owned[m]
        state = pool[m]
        code = jnp.broadcast_to(slots[pl.ds(at, 1), :], (8, NB))
        depth = code & 127
        slot = code >> 7
        columns = [tiles[k, at] for k in range(4)]
        seen = [jnp.take_along_axis(table[n], depth, axis=1, mode="promise_in_bounds") for n in columns]
        at_particle = jnp.where(
            slot < 2, jnp.where(slot == 0, seen[0], seen[1]), jnp.where(slot == 2, seen[2], seen[3])
        )
        coeff = jnp.broadcast_to(state[7:8], (8, NB))
        radius = jnp.broadcast_to(state[3:4], (8, NB))
        values = jnp.where(last_row, radius * radius * radius, coeff * (at_particle - state)) * own
        both = jnp.where(low_rows, pltpu.roll(values, 4, 0), values)
        for c in range(3):
            drag[c, pl.ds(at, 1), :] = both[c : c + 1]
        first = jnp.where(slot == half, both, 0.0)
        second = jnp.where(slot == half + 2, both, 0.0)
        sixteen = jnp.concatenate([first, second], axis=0)
        upper = sixteen.astype(BF16)
        lower = (sixteen - upper.astype(F32)).astype(BF16)
        pick = (depth_rows == jnp.broadcast_to(depth[0:1], (128, NB))).astype(BF16)
        spread = lax.dot_general(
            jnp.concatenate([upper, lower], axis=0), pick, (((1,), (1,)), ((), ())),
            preferred_element_type=F32,
        )
        spread = spread[0:16] + spread[16:32]
        parts_ = (
            jnp.where(low_rows, spread[0:8], 0.0), jnp.where(low_rows, 0.0, spread[0:8]),
            jnp.where(low_rows, spread[8:16], 0.0), jnp.where(low_rows, 0.0, spread[8:16]),
        )
        return columns, parts_

    def add(columns, pieces):
        olds = [sums[n] for n in columns]
        for n, old, piece in zip(columns, olds, pieces, strict=True):
            sums[n] = old + piece

    def blocks(g, carry):
        made = []
        for u in range(COUPLE_UNROLL):
            m = g * COUPLE_UNROLL + u
            at = jnp.where(m < NB, m, NB + ((m - NB) // MOVERS) * SLOTS + (m - NB) % MOVERS)
            made.append(one_block(m, at))
        for columns, pieces in made:
            add(columns, pieces)
        return carry

    lax.fori_loop(0, OWNABLE // COUPLE_UNROLL, blocks, 0)
    dep[...] = jnp.zeros_like(dep)
    for n in range(100):
        total = sums[n]
        total = total[0:4] + total[4:8]
        for f in range(4):
            dep[f, n // 10, n % 10 + 3, :] = total[f]
    for out, up in ((out_e, y_even), (out_o, jnp.logical_not(y_even))):
        for f in range(4):
            for x in range(10):
                i = f * 10 + x
                r = 4 * (i % 2)
                out[i // 2, r : r + 4, :] = jnp.where(up, dep[f, x, 9:13, :], dep[f, x, 3:7, :])


def fold_y(dep, in_e, in_o, dep_x, out_o, out_e):
    even = lax.axis_index("gy") % 2 == 0
    dep_x[...] = dep[...]
    for f in range(4):
        for x in range(10):
            i = f * 10 + x
            r = 4 * (i % 2)
            a = in_e[i // 2, r : r + 4, :]
            b = in_o[i // 2, r : r + 4, :]
            dep_x[f, x, 11:15, :] += jnp.where(even, a, b)
            dep_x[f, x, 1:5, :] += jnp.where(even, b, a)
    parity = lax.axis_index("gx") % 2
    for out, up in ((out_e, parity == 0), (out_o, parity == 1)):
        first = jnp.where(up, 6, 0)
        rim = jnp.where(up, 9, 0)
        for r in range(4):
            out[2 * r] = dep_x[3, first + r, 0:8, :]
            out[2 * r + 1] = dep_x[3, first + r, 8:16, :]
        for c in range(3):
            out[8 + 2 * c] = dep_x[c, rim, 0:8, :]
            out[9 + 2 * c] = dep_x[c, rim, 8:16, :]


D_TILES = 14


def tiles16(ref, at):
    return jnp.concatenate([ref[at], ref[at + 1]], axis=0)


def finish(dep_x, in_e, in_o, near_e, near_o, pres_x, gain_x, rest_x, pressure, drag_sum, now, new, gain, off):
    even = lax.axis_index("gx") % 2 == 0

    def from_up(a, b, at):
        return jnp.where(even, tiles16(a, at), tiles16(b, at))

    def from_down(a, b, at):
        return jnp.where(even, tiles16(b, at), tiles16(a, at))

    for c in range(3):
        drag_sum[c] = dep_x[c, 1:9, 4:12, :]
        drag_sum[c, 0] += from_down(in_e, in_o, 8 + 2 * c)[4:12]
        drag_sum[c, 7] += from_up(in_e, in_o, 8 + 2 * c)[4:12]
    p_at = GROUP + 6
    g_at = p_at + 8
    s_at = g_at + 6
    for x in range(16):
        if x < 4:
            now[x] = from_down(near_e, near_o, p_at + 2 * x)
        elif x < 12:
            now[x] = pres_x[x - 4]
        else:
            now[x] = from_up(near_e, near_o, p_at + 2 * (x - 12))
    for x in range(1, 15):
        if x < 4:
            g = from_down(near_e, near_o, g_at + 2 * (x - 1))
            s = from_down(near_e, near_o, s_at + 2 * (x - 1))
        elif x < 12:
            g = gain_x[x - 4]
            s = rest_x[x - 4]
        else:
            g = from_up(near_e, near_o, g_at + 2 * (x - 12))
            s = from_up(near_e, near_o, s_at + 2 * (x - 12))
        load = jnp.zeros((16, 128), F32)
        if 3 <= x <= 12:
            load = load + dep_x[3, x - 3]
        if x <= 4:
            load = load + from_down(in_e, in_o, 2 * (x - 1))
        if x >= 11:
            load = load + from_up(in_e, in_o, 2 * (x - 11))
        gain[x] = g
        off[x] = g * (s + 2.0 * load)
    lane = lax.broadcasted_iota(jnp.int32, (16, 128), 1)
    inner_low = lane > 0
    inner_high = lane < 127
    source, target = now, new
    for sweep in range(ITERS):
        for x in range(sweep + 1, 15 - sweep):
            p = source[x]
            near = source[x - 1] + source[x + 1]
            near = near + pltpu.roll(p, 1, 0) + pltpu.roll(p, 15, 0)
            near = near + jnp.where(inner_low, pltpu.roll(p, 1, 1), 0.0)
            near = near + jnp.where(inner_high, pltpu.roll(p, 127, 1), 0.0)
            target[x] = gain[x] * near + off[x]
        source, target = target, source
    pressure[...] = source[4:12, 4:12, :]


def head(v):
    return v.astype(BF16).astype(F32)

def preparers(left, near, right):
    row = lax.broadcasted_iota(jnp.int32, (8, 128), 0)
    first_four = row < 4
    space = row < 3
    bias = jnp.where(space, 1.5, 0.0)
    sign = jnp.where(row == 7, 1.0, jnp.where(first_four, 0.0, -1.0))
    turned_sign = jnp.where(space, -1.0, jnp.where(row == 3, 1.0, 0.0))
    last = jnp.where(row == 7, 1.0, 0.0)

    def left_of(tile, m):
        centred = tile - bias
        v = jnp.where(first_four, centred, pltpu.roll(centred * centred, 4, 0))
        h = head(v)
        rest = v - h
        mid = head(rest)
        low = rest - mid
        extra = jnp.where(space, 1.0, jnp.where(first_four, 0.0, low))
        shifted = jnp.where(first_four, 1.0, jnp.where(row == 7, 0.0, pltpu.roll(mid, 4, 0)))
        near[m] = jnp.concatenate([jnp.where(space, h, shifted), jnp.where(space, low, 0.0)], axis=0).astype(BF16)
        return [h, h, mid, extra]

    def right_of(tile, n):
        centred = tile - bias
        square = jnp.where(first_four, centred * centred, 0.0)
        t = jnp.broadcast_to(jnp.sum(square * turned_sign, axis=0, keepdims=True), (8, 128))
        r2 = jnp.broadcast_to(square[3:4], (8, 128))
        d = jnp.where(first_four, 2.0 * centred, sign)
        h = head(d)
        mid = head(d - h)

        def terms(v):
            a = head(v)
            b = head(v - a)
            return a, b, v - a - b

        ta, tb, tc = terms(t)
        ra, rb, rc = terms(r2)
        fourth = jnp.where(row == 0, ta, jnp.where(row == 1, tb, jnp.where(row == 2, tc, sign)))
        reach = jnp.where(row == 3, h, last)
        reach_mid = jnp.where(row == 3, mid, 0.0)
        fourth_reach = jnp.where(row == 0, ra, jnp.where(row == 1, rb, jnp.where(row == 2, rc, last)))
        right[n, :, 0:128] = jnp.concatenate([h, mid, h, fourth], axis=0).astype(BF16)
        right[n, :, 128:256] = jnp.concatenate([reach, reach_mid, reach, fourth_reach], axis=0).astype(BF16)

    def four(tiles, m):
        rows = []
        for b, tile in enumerate(tiles):
            rows += left_of(tile, m + b)
        left[m // 4] = jnp.concatenate(rows, axis=0).astype(BF16).T

    return four, right_of


def lister(pairs, total, chosen, wanted_own):
    def look(first, count, size):
        for v in range(size):
            t = first + v
            own = jnp.maximum(pairs[0, t], pairs[1, t]) < NB
            wanted = own if wanted_own else jnp.logical_not(own)
            chosen[count] = t
            count = count + jnp.where(wanted & (t < total), 1, 0)
        return count

    return look


def run_tiles(pairs, chosen, count, left, near, right, sums):
    def tile(n):
        t = chosen[jnp.minimum(n, count - 1)]
        i = pairs[0, t]
        j = pairs[1, t]
        q = i - NB
        i = jnp.where(i < NB, i, NB + (q // SLOTS) * MOVERS + q % SLOTS)
        mine = right[i]
        place = j % 4
        none = jnp.zeros_like(mine)
        weights = jnp.concatenate([jnp.where(place == k, mine, none) for k in range(4)], axis=0)
        both = jnp.dot(left[j // 4], weights, preferred_element_type=F32)
        overlap = jnp.maximum(both[:, :128], 0.0)
        reach = both[:, 128:]
        guess = pl.reciprocal(reach, approx=True)
        weight = overlap * (guess * (2.0 - reach * guess))
        upper = weight.astype(BF16)
        lower = (weight - upper.astype(F32)).astype(BF16)
        a = near[j]
        got = jnp.dot(a, upper, preferred_element_type=F32) + jnp.dot(a, lower, preferred_element_type=F32)
        got = got[0:8] + pltpu.roll(got[0:8], 4, 0) + got[8:16]
        return i, got * jnp.where(n < count, 1.0, 0.0)

    def step(g, carry):
        made = [tile(g * CONTACT_UNROLL + u) for u in range(CONTACT_UNROLL)]
        for i, got in made:
            sums[i] += got
        return carry

    lax.fori_loop(0, (count + CONTACT_UNROLL - 1) // CONTACT_UNROLL, step, 0)


def contact_own(pairs, total_ref, parts, after, left, near, right, sums, chosen):
    total = total_ref[0, 0]
    sums[...] = jnp.zeros_like(sums)
    four, right_of = preparers(left, near, right)
    look = lister(pairs, total, chosen, True)
    groups = NB // 4 // PREPARE

    def own(k, count):
        for u in range(PREPARE):
            m = 4 * (k * PREPARE + u)
            tiles = [parts[m + b] for b in range(4)]
            four(tiles, m)
            for b in range(4):
                right_of(tiles[b], m + b)
        return look(k * (MAXT // groups), count, MAXT // groups)

    count = lax.fori_loop(0, groups, own, 0)
    run_tiles(pairs, chosen, count, left, near, right, sums)


def contact_rest(
    pairs, total_ref, parts, in_xe, in_xo, in_ye, in_yo, drag, after, left_in, near_in, right_in, sums_in,
    force, left, near, right, sums, chosen,
):
    x_even = lax.axis_index("gx") % 2 == 0
    y_even = lax.axis_index("gy") % 2 == 0
    total = total_ref[0, 0]
    four, right_of = preparers(left, near, right)
    look = lister(pairs, total, chosen, False)
    groups = (
        (0, x_even, in_xe, in_xo), (1, x_even, in_xe, in_xo), (0, y_even, in_ye, in_yo), (1, y_even, in_ye, in_yo)
    )
    count = jnp.int32(0)
    part = MAXT // 16
    for d, (up, even, a, b) in enumerate(groups):
        first, second = (b, a) if up == 0 else (a, b)
        for u in range(MOVERS // 4):
            tiles = [jnp.where(even, first[4 * u + b], second[4 * u + b]) for b in range(4)]
            four(tiles, NB + d * SLOTS + 4 * u)
            for b in range(4):
                right_of(tiles[b], NB + d * MOVERS + 4 * u + b)
        count = look(d * 4 * part, count, part)

        def others(k, count, d=d, even=even, first=first, second=second):
            for u in range(2):
                s = MOVERS + 8 * k + 4 * u
                tiles = [jnp.where(even, first[s + b], second[s + b]) for b in range(4)]
                four(tiles, NB + d * SLOTS + s)
                four([pltpu.roll(tile, 4, 0) for tile in tiles], NB + d * SLOTS + s + PAIRS)
            return look((d * 4 + 1 + k) * part, count, part)

        count = lax.fori_loop(0, PAIRS // 8, others, count)
    run_tiles(pairs, chosen, count, left, near, right, sums)

    def put(n, at, position):
        for c in range(3):
            x = position(c) - 1.5
            w = sums[8 * n : 8 * n + 8, 3, :]
            y = sums[8 * n : 8 * n + 8, c, :]
            force[c, at : at + 8, :] = drag[c, at : at + 8, :] + 0.5 * (x * w - y)

    for n in range(NB // 8):
        put(n, 8 * n, lambda c, n=n: parts[8 * n : 8 * n + 8, c, :])
    for d, (up, even, a, b) in enumerate(groups):
        first, second = (b, a) if up == 0 else (a, b)
        for k in range(2):
            put(
                NB // 8 + 2 * d + k,
                NB + d * SLOTS + 8 * k,
                lambda c, k=k, even=even, first=first, second=second: jnp.where(
                    even, first[8 * k : 8 * k + 8, c, :], second[8 * k : 8 * k + 8, c, :]
                ),
            )
        for c in range(3):
            force[c, NB + d * SLOTS + MOVERS : NB + (d + 1) * SLOTS, :] = jnp.zeros((SLOTS - MOVERS, 128), F32)


def pairs_of(first, count, last):
    up = [(i, i + 1) for i in range(first, last, 2)]
    return up + [(b, a) for a, b in up]


def swap(array, axis, first):
    count = lax.axis_size(axis)
    return lax.ppermute(array, axis, pairs_of(first, count, count - 1))


def body(
    particles,
    send_list,
    move_count,
    tile_pairs,
    tile_count,
    drag_tiles,
    cell_slot,
    fluid_velocity,
    pressure_init,
    source,
    solid_old,
    screening,
):
    sends = send_list[0, 0]
    moves = move_count[0, 0]
    tiles = drag_tiles[0, 0].T
    pairs = tile_pairs[0, 0].T
    cells = (8, 8, 128)
    wide = (8, 16, 128)
    ye, yo, gain, rest, parts, flow, pres, slots = call(
        pack_y,
        (
            shape(Y_TILES, 8, 128), shape(Y_TILES, 8, 128), shape(*cells), shape(*cells),
            shape(NB, 8, 128), shape(3, *cells), shape(*cells), jax.ShapeDtypeStruct((384, 128), jnp.int32),
        ),
        [HB] * 8,
        [
            pltpu.SMEM((4, SLOTS), jnp.int32),
            pltpu.VMEM(cells, F32),
            pltpu.VMEM(cells, F32),
            pltpu.VMEM(cells, F32),
            pltpu.SemaphoreType.DMA((8,)),
        ],
    )(particles[0, 0], sends, fluid_velocity, pressure_init, screening, source, solid_old, cell_slot[0, 0])
    got_ye = swap(ye, "gy", 0)
    got_yo = swap(yo, "gy", 1)
    xo, xe, flow_x, pres_x, gain_x, rest_x = call(
        pack_x,
        (shape(X_TILES, 8, 128), shape(X_TILES, 8, 128), shape(3, *wide), shape(*wide), shape(*wide), shape(*wide)),
        [VM, SM] + [VM] * 6,
    )(parts, sends, flow, pres, gain, rest, got_ye, got_yo)
    got_xe = swap(xe, "gx", 0)
    got_xo = swap(xo, "gx", 1)
    operands = (
        jax.ShapeDtypeStruct((POOL // 4, 128, 128), BF16),
        jax.ShapeDtypeStruct((POOL, 16, 128), BF16),
        jax.ShapeDtypeStruct((OWNABLE, 32, 256), BF16),
        shape(OWNABLE, 8, 128),
    )
    prepared = call(
        contact_own, operands, [SM, SM, VM, VM], [pltpu.SMEM((MAXT + 1,), jnp.int32)], flops=10**8
    )(pairs, tile_count, parts, xo)
    drag, dep, de, do = call(
        couple,
        (shape(3, 384, 128), shape(4, 10, 16, 128), shape(20, 8, 128), shape(20, 8, 128)),
        [VM, HB, HB, HB] + [VM] * 7,
        [
            pltpu.VMEM((OWNABLE, 8, 128), F32),
            pltpu.VMEM((100, 8, 128), F32),
            pltpu.VMEM((100, 8, 128), F32),
            pltpu.SMEM((OWNABLE,), F32),
            pltpu.SMEM((4, SLOTS), jnp.int32),
            pltpu.SMEM((2, 4), jnp.int32),
            pltpu.SMEM((4, 384), jnp.int32),
            pltpu.SemaphoreType.DMA((3,)),
        ],
    )(parts, sends, moves, tiles, slots, flow_x, got_xe, got_xo, got_ye, got_yo, prepared[3])
    got_de = swap(de, "gy", 0)
    got_do = swap(do, "gy", 1)
    dep_x, fo, fe = call(
        fold_y, (shape(4, 10, 16, 128), shape(D_TILES, 8, 128), shape(D_TILES, 8, 128)), [VM] * 3
    )(dep, got_de, got_do)
    got_fe = swap(fe, "gx", 0)
    got_fo = swap(fo, "gx", 1)
    force = call(
        contact_rest,
        (shape(3, 384, 128), *operands),
        [SM, SM] + [VM] * 11,
        [pltpu.SMEM((MAXT + 1,), jnp.int32)],
        flops=10**9,
        aliases={9: 1, 10: 2, 11: 3, 12: 4},
    )(pairs, tile_count, parts, got_xe, got_xo, got_ye, got_yo, drag, fo, *prepared)[0]
    pressure, drag_sum = call(
        finish,
        (shape(*cells), shape(3, *cells)),
        [VM] * 8,
        [pltpu.VMEM((16, 16, 128), F32)] * 4,
    )(dep_x, got_fe, got_fo, got_xe, got_xo, pres_x, gain_x, rest_x)
    return (pressure, drag_sum, force.transpose(1, 0, 2)[None, None])


def solution(mesh):
    in_specs = (
        P("gx", "gy", None, None, None),
        P("gx", "gy", None, None),
        P("gx", "gy", None, None),
        P("gx", "gy", None, None),
        P("gx", "gy"),
        P("gx", "gy", None, None),
        P("gx", "gy", None, None),
        P(None, "gx", "gy", None),
        P("gx", "gy", None),
        P("gx", "gy", None),
        P("gx", "gy", None),
        P("gx", "gy", None),
    )
    out_specs = (P("gx", "gy", None), P(None, "gx", "gy", None), P("gx", "gy", None, None, None))
    return jax.shard_map(body, mesh=mesh, in_specs=in_specs, out_specs=out_specs, check_vma=False)
```

```python
import functools

import jax
import jax.numpy as jnp
from jax import lax
from jax.experimental import pallas as pl
from jax.experimental.pallas import tpu as pltpu
from jax.sharding import PartitionSpec as P

F32 = jnp.float32
BF16 = jnp.bfloat16
NB = 128
SLOTS = 64
MOVERS = 16
PAIRS = (SLOTS - MOVERS) // 2
GROUP = MOVERS + PAIRS
OWNABLE = NB + 4 * MOVERS
POOL = 384
MAXT = 512
ITERS = 4
CONTACT_UNROLL = 32
EARLY = 96
LIST = 640
LAST = LIST - 1
PREPARE = 4
COUPLE_UNROLL = 32

VM = pl.BlockSpec(memory_space=pltpu.VMEM)
SM = pl.BlockSpec(memory_space=pltpu.SMEM)
HB = pl.BlockSpec(memory_space=pltpu.HBM)
PARAMS = pltpu.CompilerParams(vmem_limit_bytes=32 * 2**20)


def shape(*dims):
    return jax.ShapeDtypeStruct(dims, F32)


def call(kernel, outs, in_specs, scratch=(), flops=10**6, moved=10**6, aliases=None):
    return pl.pallas_call(
        kernel,
        out_shape=outs,
        in_specs=in_specs,
        out_specs=jax.tree.map(lambda o: SM if len(o.shape) == 1 else VM, outs),
        scratch_shapes=list(scratch),
        input_output_aliases=aliases or {},
        compiler_params=PARAMS,
        cost_estimate=pl.CostEstimate(flops=flops, bytes_accessed=moved, transcendentals=0),
    )


def put_blocks(parts, sends, direction, out):
    for s in range(MOVERS):
        out[s] = parts[sends[direction, s]]
    for k in range(PAIRS):
        out[MOVERS + k, 0:4, :] = parts[sends[direction, MOVERS + k], 0:4, :]
        out[MOVERS + k, 4:8, :] = parts[sends[direction, MOVERS + PAIRS + k], 0:4, :]


def fetch(sources, targets, sems):
    copies = [pltpu.make_async_copy(a, b, sems.at[n]) for n, (a, b) in enumerate(zip(sources, targets, strict=True))]
    for copy in copies:
        copy.start()
    return copies


Y_TILES = GROUP + 3
X_TILES = GROUP + 6


def pack_y(parts, sends, flow, out_e, out_o):
    parity = lax.axis_index("gy") % 2
    for out, up in ((out_e, parity == 0), (out_o, parity == 1)):
        put_blocks(parts, sends, jnp.where(up, 2, 3), out)
        for c in range(3):
            out[GROUP + c] = jnp.where(up, flow[c, :, 7, :], flow[c, :, 0, :])


def put_flow(flow_x, up, out):
    edge = jnp.where(up, 7, 0)
    for c in range(3):
        out[GROUP + 2 * c] = flow_x[c, edge, 0:8, :]
        out[GROUP + 2 * c + 1] = flow_x[c, edge, 8:16, :]


def pack_first(parts, sends, flow, in_e, in_o, out, flow_x):
    even = lax.axis_index("gy") % 2 == 0
    for c in range(3):
        flow_x[c, :, 4:12, :] = flow[c]
        a = in_e[GROUP + c]
        b = in_o[GROUP + c]
        flow_x[c, :, 12, :] = jnp.where(even, a, b)
        flow_x[c, :, 3, :] = jnp.where(even, b, a)
    up = lax.axis_index("gx") % 2 == 0
    put_blocks(parts, sends, jnp.where(up, 0, 1), out)
    put_flow(flow_x, up, out)


def pack_second(parts, sends, flow_x, out):
    up = lax.axis_index("gx") % 2 == 1
    put_blocks(parts, sends, jnp.where(up, 0, 1), out)
    put_flow(flow_x, up, out)


def couple(
    parts, sends_in, moves_in, tiles_in, slots, flow_x, in_xo, in_xe, in_ye, in_yo, after,
    pres, screen, source, solid,
    drag, dep, out_e, gain, rest,
    pool, table, sums, owned, sends, moves, tiles, sems,
):
    copies = fetch((sends_in, moves_in, tiles_in), (sends, moves, tiles), sems)
    x_even = lax.axis_index("gx") % 2 == 0
    y_even = lax.axis_index("gy") % 2 == 0
    pool[0:NB] = parts[...]
    for d, (up, even, a, b) in enumerate(
        ((0, x_even, in_xe, in_xo), (1, x_even, in_xe, in_xo), (0, y_even, in_ye, in_yo), (1, y_even, in_ye, in_yo))
    ):
        first, second = (b, a) if up == 0 else (a, b)
        pool[NB + d * MOVERS : NB + (d + 1) * MOVERS] = jnp.where(even, first[0:MOVERS], second[0:MOVERS])

    for c in range(3):
        high = jnp.where(x_even, in_xe[GROUP + 2 * c], in_xo[GROUP + 2 * c])
        high2 = jnp.where(x_even, in_xe[GROUP + 2 * c + 1], in_xo[GROUP + 2 * c + 1])
        low = jnp.where(x_even, in_xo[GROUP + 2 * c], in_xe[GROUP + 2 * c])
        low2 = jnp.where(x_even, in_xo[GROUP + 2 * c + 1], in_xe[GROUP + 2 * c + 1])
        for x in range(10):
            if x == 0:
                one, two = low, low2
            elif x == 9:
                one, two = high, high2
            else:
                one, two = flow_x[c, x - 1, 0:8, :], flow_x[c, x - 1, 8:16, :]
            table[x * 10 : x * 10 + 5, 4 + c, :] = one[3:8]
            table[x * 10 + 5 : x * 10 + 10, 4 + c, :] = two[0:5]
    sums[...] = jnp.zeros_like(sums)
    drag[...] = jnp.zeros_like(drag)
    for copy in copies:
        copy.wait()

    def stay(k, carry):
        owned[k] = 1.0
        return carry

    lax.fori_loop(0, NB, stay, 0)
    for d in range(4):

        def leave(s, carry, d=d):
            owned[sends[d, s]] = 0.0
            return carry

        lax.fori_loop(0, moves[0, d], leave, 0)
        for s in range(MOVERS):
            owned[NB + d * MOVERS + s] = jnp.where(s < moves[1, d], 1.0, 0.0)

    row = lax.broadcasted_iota(jnp.int32, (8, NB), 0)
    low_rows = row < 4
    last_row = row == 7
    half = jnp.where(low_rows, 0, 1)
    depth_rows = lax.broadcasted_iota(jnp.int32, (128, NB), 0)

    def one_block(m, at):
        own = owned[m]
        state = pool[m]
        code = jnp.broadcast_to(slots[pl.ds(at, 1), :], (8, NB))
        depth = code & 127
        slot = code >> 7
        columns = [tiles[k, at] for k in range(4)]
        seen = [jnp.take_along_axis(table[n], depth, axis=1, mode="promise_in_bounds") for n in columns]
        at_particle = jnp.where(
            slot < 2, jnp.where(slot == 0, seen[0], seen[1]), jnp.where(slot == 2, seen[2], seen[3])
        )
        coeff = jnp.broadcast_to(state[7:8], (8, NB))
        radius = jnp.broadcast_to(state[3:4], (8, NB))
        values = jnp.where(last_row, radius * radius * radius, coeff * (at_particle - state)) * own
        both = jnp.where(low_rows, pltpu.roll(values, 4, 0), values)
        for c in range(3):
            drag[c, pl.ds(at, 1), :] = both[c : c + 1]
        first = jnp.where(slot == half, both, 0.0)
        second = jnp.where(slot == half + 2, both, 0.0)
        sixteen = jnp.concatenate([first, second], axis=0)
        upper = sixteen.astype(BF16)
        lower = (sixteen - upper.astype(F32)).astype(BF16)
        pick = (depth_rows == jnp.broadcast_to(depth[0:1], (128, NB))).astype(BF16)
        spread = lax.dot_general(
            jnp.concatenate([upper, lower], axis=0), pick, (((1,), (1,)), ((), ())),
            preferred_element_type=F32,
        )
        spread = spread[0:16] + spread[16:32]
        parts_ = (
            jnp.where(low_rows, spread[0:8], 0.0), jnp.where(low_rows, 0.0, spread[0:8]),
            jnp.where(low_rows, spread[8:16], 0.0), jnp.where(low_rows, 0.0, spread[8:16]),
        )
        return columns, parts_

    def add(columns, pieces):
        olds = [sums[n] for n in columns]
        for n, old, piece in zip(columns, olds, pieces, strict=True):
            sums[n] = old + piece

    def blocks(g, carry):
        made = []
        for u in range(COUPLE_UNROLL):
            m = g * COUPLE_UNROLL + u
            at = jnp.where(m < NB, m, NB + ((m - NB) // MOVERS) * SLOTS + (m - NB) % MOVERS)
            made.append(one_block(m, at))
        for columns, pieces in made:
            add(columns, pieces)
        return carry

    lax.fori_loop(0, OWNABLE // COUPLE_UNROLL, blocks, 0)
    dep[...] = jnp.zeros_like(dep)
    for n in range(100):
        total = sums[n]
        total = total[0:4] + total[4:8]
        for f in range(4):
            dep[f, n // 10, n % 10 + 3, :] = total[f]
    gain[...] = 1.0 / (6.0 + screen[...])
    rest[...] = source[...] - 2.0 * solid[...]
    put_rims(dep, pres, gain, rest, x_even, out_e)


P_AT = 14
G_AT = P_AT + 4
S_AT = G_AT + 3
D_TILES = S_AT + 3


def put_rims(dep, pres, gain, rest, up, out):
    first = jnp.where(up, 6, 0)
    rim = jnp.where(up, 9, 0)
    for r in range(4):
        out[2 * r] = dep[3, first + r, 0:8, :]
        out[2 * r + 1] = dep[3, first + r, 8:16, :]
    for c in range(3):
        out[8 + 2 * c] = dep[c, rim, 0:8, :]
        out[9 + 2 * c] = dep[c, rim, 8:16, :]
    for at, ref, count in ((P_AT, pres, 4), (G_AT, gain, 3), (S_AT, rest, 3)):
        start = jnp.where(up, 8 - count, 0)
        for r in range(count):
            out[at + r] = ref[start + r]


def pack_fo(dep, pres, gain, rest, out):
    put_rims(dep, pres, gain, rest, lax.axis_index("gx") % 2 == 1, out)


H_DRAG = 7
H_FIELDS = H_DRAG + 3
H_TILES = H_FIELDS + 24


def fold_x(dep, pres, gain, rest, in_o, in_e, after, load, drag, pres_w, gain_w, rest_w, out_e, out_o):
    even = lax.axis_index("gx") % 2 == 0

    def from_up(at):
        return jnp.where(even, in_e[at], in_o[at])

    def from_down(at):
        return jnp.where(even, in_o[at], in_e[at])

    def two(side, at):
        return jnp.concatenate([side(at), side(at + 1)], axis=0)

    for x in range(16):
        total = jnp.zeros((16, 128), F32)
        if 3 <= x <= 12:
            total = total + dep[3, x - 3]
        if 1 <= x <= 4:
            total = total + two(from_down, 2 * (x - 1))
        if 11 <= x <= 14:
            total = total + two(from_up, 2 * (x - 11))
        load[x] = total
    for c in range(3):
        drag[c] = dep[c, 1:9]
        drag[c, 0] += two(from_down, 8 + 2 * c)
        drag[c, 7] += two(from_up, 8 + 2 * c)
    for wide, ref, at, count in ((pres_w, pres, P_AT, 4), (gain_w, gain, G_AT, 3), (rest_w, rest, S_AT, 3)):
        wide[4:12] = ref[...]
        if count == 3:
            wide[0] = jnp.zeros((8, 128), F32)
            wide[15] = jnp.zeros((8, 128), F32)
        for r in range(count):
            wide[4 - count + r] = from_down(at + r)
            wide[12 + r] = from_up(at + r)
    parity = lax.axis_index("gy") % 2
    for out, up in ((out_e, parity == 0), (out_o, parity == 1)):
        for x in range(14):
            row = 4 * (x % 2)
            out[x // 2, row : row + 4, :] = jnp.where(up, load[x + 1, 9:13, :], load[x + 1, 3:7, :])
        for c in range(3):
            out[H_DRAG + c] = jnp.where(up, drag[c, :, 12, :], drag[c, :, 3, :])
        at = H_FIELDS
        for wide in (pres_w, gain_w, rest_w):
            for x in range(16):
                row = 4 * (x % 2)
                out[at + x // 2, row : row + 4, :] = jnp.where(up, wide[x, 4:8, :], wide[x, 0:4, :])
            at += 8


def finish(load, drag, pres_w, gain_w, rest_w, in_e, in_o, pressure, drag_sum, now, new, gain, off):
    even = lax.axis_index("gy") % 2 == 0

    def half(side_up, at, x):
        row = 4 * (x % 2)
        a = in_e[at + x // 2, row : row + 4, :]
        b = in_o[at + x // 2, row : row + 4, :]
        return jnp.where(even, a, b) if side_up else jnp.where(even, b, a)

    for c in range(3):
        drag_sum[c] = drag[c, :, 4:12, :]
        a = in_e[H_DRAG + c]
        b = in_o[H_DRAG + c]
        drag_sum[c, :, 0, :] += jnp.where(even, b, a)
        drag_sum[c, :, 7, :] += jnp.where(even, a, b)

    def rows(wide, n, x):
        at = H_FIELDS + 8 * n
        return jnp.concatenate([half(False, at, x), wide[x], half(True, at, x)], axis=0)

    for x in range(16):
        now[x] = rows(pres_w, 0, x)
    for x in range(1, 15):
        off[x] = load[x]
        off[x, 1:5, :] += half(False, 0, x - 1)
        off[x, 11:15, :] += half(True, 0, x - 1)
        g = rows(gain_w, 1, x)
        gain[x] = g
        off[x] = g * (rows(rest_w, 2, x) + 2.0 * off[x])
    lane = lax.broadcasted_iota(jnp.int32, (16, 128), 1)
    inner_low = lane > 0
    inner_high = lane < 127
    source, target = now, new
    for sweep in range(ITERS):
        for x in range(sweep + 1, 15 - sweep):
            p = source[x]
            near = source[x - 1] + source[x + 1]
            near = near + pltpu.roll(p, 1, 0) + pltpu.roll(p, 15, 0)
            near = near + jnp.where(inner_low, pltpu.roll(p, 1, 1), 0.0)
            near = near + jnp.where(inner_high, pltpu.roll(p, 127, 1), 0.0)
            target[x] = gain[x] * near + off[x]
        source, target = target, source
    pressure[...] = source[4:12, 4:12, :]


def head(v):
    return v.astype(BF16).astype(F32)

def preparers(left, near, right):
    row = lax.broadcasted_iota(jnp.int32, (8, 128), 0)
    first_four = row < 4
    space = row < 3
    bias = jnp.where(space, 1.5, 0.0)
    sign = jnp.where(row == 7, 1.0, jnp.where(first_four, 0.0, -1.0))
    turned_sign = jnp.where(space, -1.0, jnp.where(row == 3, 1.0, 0.0))
    last = jnp.where(row == 7, 1.0, 0.0)

    def left_of(tile, m):
        centred = tile - bias
        v = jnp.where(first_four, centred, pltpu.roll(centred * centred, 4, 0))
        h = head(v)
        rest = v - h
        mid = head(rest)
        low = rest - mid
        extra = jnp.where(space, 1.0, jnp.where(first_four, 0.0, low))
        shifted = jnp.where(first_four, 1.0, jnp.where(row == 7, 0.0, pltpu.roll(mid, 4, 0)))
        near[m] = jnp.concatenate([jnp.where(space, h, shifted), jnp.where(space, low, 0.0)], axis=0).astype(BF16)
        return [h, h, mid, extra]

    def right_of(tile, n):
        centred = tile - bias
        square = jnp.where(first_four, centred * centred, 0.0)
        t = jnp.broadcast_to(jnp.sum(square * turned_sign, axis=0, keepdims=True), (8, 128))
        r2 = jnp.broadcast_to(square[3:4], (8, 128))
        d = jnp.where(first_four, 2.0 * centred, sign)
        h = head(d)
        mid = head(d - h)

        def terms(v):
            a = head(v)
            b = head(v - a)
            return a, b, v - a - b

        ta, tb, tc = terms(t)
        ra, rb, rc = terms(r2)
        fourth = jnp.where(row == 0, ta, jnp.where(row == 1, tb, jnp.where(row == 2, tc, sign)))
        reach = jnp.where(row == 3, h, last)
        reach_mid = jnp.where(row == 3, mid, 0.0)
        fourth_reach = jnp.where(row == 0, ra, jnp.where(row == 1, rb, jnp.where(row == 2, rc, last)))
        right[n, :, 0:128] = jnp.concatenate([h, mid, h, fourth], axis=0).astype(BF16)
        right[n, :, 128:256] = jnp.concatenate([reach, reach_mid, reach, fourth_reach], axis=0).astype(BF16)

    def four(tiles, m):
        rows = []
        for b, tile in enumerate(tiles):
            rows += left_of(tile, m + b)
        left[m // 4] = jnp.concatenate(rows, axis=0).astype(BF16).T

    return four, right_of


def lister(pairs, total, chosen, wanted_own):
    def look(first, count, size):
        for v in range(size):
            t = first + v
            own = jnp.maximum(pairs[0, t], pairs[1, t]) < NB
            wanted = own if wanted_own else jnp.logical_not(own)
            chosen[count] = t
            count = count + jnp.where(wanted & (t < total), 1, 0)
        return count

    return look


def run_tiles(pairs, chosen, count, left, near, right, sums, begin, end):
    def tile(n):
        t = chosen[jnp.minimum(n, count - 1)]
        i = pairs[0, t]
        j = pairs[1, t]
        q = i - NB
        i = jnp.where(i < NB, i, NB + (q // SLOTS) * MOVERS + q % SLOTS)
        mine = right[i]
        place = j % 4
        none = jnp.zeros_like(mine)
        weights = jnp.concatenate([jnp.where(place == k, mine, none) for k in range(4)], axis=0)
        both = jnp.dot(left[j // 4], weights, preferred_element_type=F32)
        overlap = jnp.maximum(both[:, :128], 0.0)
        reach = both[:, 128:]
        guess = pl.reciprocal(reach, approx=True)
        weight = overlap * (guess * (2.0 - reach * guess))
        upper = weight.astype(BF16)
        lower = (weight - upper.astype(F32)).astype(BF16)
        a = near[j]
        got = jnp.dot(a, upper, preferred_element_type=F32) + jnp.dot(a, lower, preferred_element_type=F32)
        got = got[0:8] + pltpu.roll(got[0:8], 4, 0) + got[8:16]
        return i, got * jnp.where(n < count, 1.0, 0.0)

    def step(g, carry):
        made = [tile(begin + g * CONTACT_UNROLL + u) for u in range(CONTACT_UNROLL)]
        for i, got in made:
            sums[i] += got
        return carry

    lax.fori_loop(0, jnp.maximum(end - begin + CONTACT_UNROLL - 1, 0) // CONTACT_UNROLL, step, 0)


def contact_own(pairs, total_ref, parts, after, left, near, right, sums, chosen):
    total = total_ref[0, 0]
    sums[...] = jnp.zeros_like(sums)
    four, right_of = preparers(left, near, right)
    look = lister(pairs, total, chosen, True)
    groups = NB // 4 // PREPARE

    def own(k, count):
        for u in range(PREPARE):
            m = 4 * (k * PREPARE + u)
            tiles = [parts[m + b] for b in range(4)]
            four(tiles, m)
            for b in range(4):
                right_of(tiles[b], m + b)
        return look(k * (MAXT // groups), count, MAXT // groups)

    count = lax.fori_loop(0, groups, own, 0)
    run_tiles(pairs, chosen, count, left, near, right, sums, 0, count)


def received(in_xe, in_xo, in_ye, in_yo):
    x_even = lax.axis_index("gx") % 2 == 0
    y_even = lax.axis_index("gy") % 2 == 0
    return ((x_even, in_xo, in_xe), (x_even, in_xe, in_xo), (y_even, in_yo, in_ye), (y_even, in_ye, in_yo))


def contact_more(
    pairs, total_ref, in_xo, in_xe, in_ye, in_yo, after, left_in, near_in, right_in, sums_in,
    left, near, right, sums, chosen,
):
    total = total_ref[0, 0]
    four, right_of = preparers(left, near, right)
    look = lister(pairs, total, chosen, False)
    count = jnp.int32(0)
    part = MAXT // 16
    for d, (even, first, second) in enumerate(received(in_xe, in_xo, in_ye, in_yo)):
        for u in range(MOVERS // 4):
            tiles = [jnp.where(even, first[4 * u + b], second[4 * u + b]) for b in range(4)]
            four(tiles, NB + d * SLOTS + 4 * u)
            for b in range(4):
                right_of(tiles[b], NB + d * MOVERS + 4 * u + b)
        count = look(d * 4 * part, count, part)

        def others(k, count, d=d, even=even, first=first, second=second):
            for u in range(2):
                s = MOVERS + 8 * k + 4 * u
                tiles = [jnp.where(even, first[s + b], second[s + b]) for b in range(4)]
                four(tiles, NB + d * SLOTS + s)
                four([pltpu.roll(tile, 4, 0) for tile in tiles], NB + d * SLOTS + s + PAIRS)
            return look((d * 4 + 1 + k) * part, count, part)

        count = lax.fori_loop(0, PAIRS // 8, others, count)
    chosen[LAST] = count
    run_tiles(pairs, chosen, count, left, near, right, sums, 0, jnp.minimum(EARLY, count))


def contact_end(
    pairs, parts, in_xo, in_xe, in_ye, in_yo, drag, after, left, near, right, chosen, sums_in, force, sums
):
    count = chosen[LAST]
    run_tiles(pairs, chosen, count, left, near, right, sums, EARLY, count)

    def put(n, at, position):
        for c in range(3):
            x = position(c) - 1.5
            w = sums[8 * n : 8 * n + 8, 3, :]
            y = sums[8 * n : 8 * n + 8, c, :]
            force[c, at : at + 8, :] = drag[c, at : at + 8, :] + 0.5 * (x * w - y)

    for n in range(NB // 8):
        put(n, 8 * n, lambda c, n=n: parts[8 * n : 8 * n + 8, c, :])
    for d, (even, first, second) in enumerate(received(in_xe, in_xo, in_ye, in_yo)):
        for k in range(2):
            put(
                NB // 8 + 2 * d + k,
                NB + d * SLOTS + 8 * k,
                lambda c, k=k, even=even, first=first, second=second: jnp.where(
                    even, first[8 * k : 8 * k + 8, c, :], second[8 * k : 8 * k + 8, c, :]
                ),
            )
        for c in range(3):
            force[c, NB + d * SLOTS + MOVERS : NB + (d + 1) * SLOTS, :] = jnp.zeros((SLOTS - MOVERS, 128), F32)


def pairs_of(first, count, last):
    up = [(i, i + 1) for i in range(first, last, 2)]
    return up + [(b, a) for a, b in up]


def swap(array, axis, first):
    count = lax.axis_size(axis)
    return lax.ppermute(array, axis, pairs_of(first, count, count - 1))


def body(
    particles,
    send_list,
    move_count,
    tile_pairs,
    tile_count,
    drag_tiles,
    cell_slot,
    fluid_velocity,
    pressure_init,
    source,
    solid_old,
    screening,
):
    parts = particles[0, 0]
    sends = send_list[0, 0]
    moves = move_count[0, 0]
    tiles = drag_tiles[0, 0].T
    pairs = tile_pairs[0, 0].T
    slots = cell_slot[0, 0]
    cells = (8, 8, 128)
    ye, yo = call(pack_y, (shape(Y_TILES, 8, 128), shape(Y_TILES, 8, 128)), [VM, SM, VM])(parts, sends, fluid_velocity)
    got_ye = swap(ye, "gy", 0)
    got_yo = swap(yo, "gy", 1)
    xe, flow_x = call(pack_first, (shape(X_TILES, 8, 128), shape(3, 8, 16, 128)), [VM, SM, VM, VM, VM])(
        parts, sends, fluid_velocity, got_ye, got_yo
    )
    got_xe = swap(xe, "gx", 0)
    xo = call(pack_second, shape(X_TILES, 8, 128), [VM, SM, VM])(parts, sends, flow_x)
    got_xo = swap(xo, "gx", 1)
    operands = (
        jax.ShapeDtypeStruct((POOL // 4, 128, 128), BF16),
        jax.ShapeDtypeStruct((POOL, 16, 128), BF16),
        jax.ShapeDtypeStruct((OWNABLE, 32, 256), BF16),
        shape(OWNABLE, 8, 128),
    )
    prepared = call(
        contact_own, operands, [SM, SM, VM, VM], [pltpu.SMEM((LIST,), jnp.int32)], flops=10**8
    )(pairs, tile_count, parts, xo)
    drag, dep, fe, gain, rest = call(
        couple,
        (shape(3, 384, 128), shape(4, 10, 16, 128), shape(D_TILES, 8, 128), shape(*cells), shape(*cells)),
        [VM, HB, HB, HB] + [VM] * 11,
        [
            pltpu.VMEM((OWNABLE, 8, 128), F32),
            pltpu.VMEM((100, 8, 128), F32),
            pltpu.VMEM((100, 8, 128), F32),
            pltpu.SMEM((OWNABLE,), F32),
            pltpu.SMEM((4, SLOTS), jnp.int32),
            pltpu.SMEM((2, 4), jnp.int32),
            pltpu.SMEM((4, 384), jnp.int32),
            pltpu.SemaphoreType.DMA((3,)),
        ],
    )(
        parts, sends, moves, tiles, slots, flow_x, got_xo, got_xe, got_ye, got_yo, prepared[3],
        pressure_init, screening, source, solid_old,
    )
    got_fe = swap(fe, "gx", 0)
    fo = call(pack_fo, shape(D_TILES, 8, 128), [VM] * 4)(dep, pressure_init, gain, rest)
    got_fo = swap(fo, "gx", 1)
    *more, chosen = call(
        contact_more,
        (*operands, jax.ShapeDtypeStruct((LIST,), jnp.int32)),
        [SM, SM] + [VM] * 9,
        flops=10**8,
        aliases={7: 0, 8: 1, 9: 2, 10: 3},
    )(pairs, tile_count, got_xo, got_xe, got_ye, got_yo, fo, *prepared)
    load, drag_x, pres_w, gain_w, rest_w, he, ho = call(
        fold_x,
        (
            shape(16, 16, 128), shape(3, 8, 16, 128), shape(16, 8, 128), shape(16, 8, 128), shape(16, 8, 128),
            shape(H_TILES, 8, 128), shape(H_TILES, 8, 128),
        ),
        [VM] * 7,
    )(dep, pressure_init, gain, rest, got_fo, got_fe, more[3])
    got_he = swap(he, "gy", 0)
    got_ho = swap(ho, "gy", 1)
    force, unused = call(
        contact_end,
        (shape(3, 384, 128), operands[3]),
        [SM] + [VM] * 10 + [SM, VM],
        flops=10**9,
        aliases={12: 1},
    )(pairs, parts, got_xo, got_xe, got_ye, got_yo, drag, ho, *more[:3], chosen, more[3])
    pressure, drag_sum = call(
        finish,
        (shape(*cells), shape(3, *cells)),
        [VM] * 7,
        [pltpu.VMEM((16, 16, 128), F32)] * 4,
    )(load, drag_x, pres_w, gain_w, rest_w, got_he, got_ho)
    return (pressure, drag_sum, force.transpose(1, 0, 2)[None, None])


def solution(mesh):
    in_specs = (
        P("gx", "gy", None, None, None),
        P("gx", "gy", None, None),
        P("gx", "gy", None, None),
        P("gx", "gy", None, None),
        P("gx", "gy"),
        P("gx", "gy", None, None),
        P("gx", "gy", None, None),
        P(None, "gx", "gy", None),
        P("gx", "gy", None),
        P("gx", "gy", None),
        P("gx", "gy", None),
        P("gx", "gy", None),
    )
    out_specs = (P("gx", "gy", None), P(None, "gx", "gy", None), P("gx", "gy", None, None, None))
    return jax.shard_map(body, mesh=mesh, in_specs=in_specs, out_specs=out_specs, check_vma=False)
```

```python
import functools

import jax
import jax.numpy as jnp
from jax import lax
from jax.experimental import pallas as pl
from jax.experimental.pallas import tpu as pltpu
from jax.sharding import PartitionSpec as P

F32 = jnp.float32
BF16 = jnp.bfloat16
NB = 128
SLOTS = 64
MOVERS = 16
PAIRS = (SLOTS - MOVERS) // 2
GROUP = MOVERS + PAIRS
OWNABLE = NB + 4 * MOVERS
POOL = 384
MAXT = 512
ITERS = 4
CONTACT_UNROLL = 32
EARLY = 96
LIST = 640
LAST = LIST - 1
PREPARE = 4
COUPLE_UNROLL = 32

VM = pl.BlockSpec(memory_space=pltpu.VMEM)
SM = pl.BlockSpec(memory_space=pltpu.SMEM)
HB = pl.BlockSpec(memory_space=pltpu.HBM)
PARAMS = pltpu.CompilerParams(vmem_limit_bytes=32 * 2**20)


def shape(*dims):
    return jax.ShapeDtypeStruct(dims, F32)


def call(kernel, outs, in_specs, scratch=(), flops=10**6, moved=10**6, aliases=None):
    return pl.pallas_call(
        kernel,
        out_shape=outs,
        in_specs=in_specs,
        out_specs=jax.tree.map(lambda o: SM if len(o.shape) == 1 else VM, outs),
        scratch_shapes=list(scratch),
        input_output_aliases=aliases or {},
        compiler_params=PARAMS,
        cost_estimate=pl.CostEstimate(flops=flops, bytes_accessed=moved, transcendentals=0),
    )


def put_blocks(parts, sends, direction, out):
    for s in range(MOVERS):
        out[s] = parts[sends[direction, s]]
    for k in range(PAIRS):
        out[MOVERS + k, 0:4, :] = parts[sends[direction, MOVERS + k], 0:4, :]
        out[MOVERS + k, 4:8, :] = parts[sends[direction, MOVERS + PAIRS + k], 0:4, :]


def fetch(sources, targets, sems):
    copies = [pltpu.make_async_copy(a, b, sems.at[n]) for n, (a, b) in enumerate(zip(sources, targets, strict=True))]
    for copy in copies:
        copy.start()
    return copies


Y_TILES = GROUP + 3
X_TILES = GROUP + 6


def pack_y(parts, sends, flow, out_e, out_o):
    parity = lax.axis_index("gy") % 2
    for out, up in ((out_e, parity == 0), (out_o, parity == 1)):
        put_blocks(parts, sends, jnp.where(up, 2, 3), out)
        for c in range(3):
            out[GROUP + c] = jnp.where(up, flow[c, :, 7, :], flow[c, :, 0, :])


def put_flow(flow_x, up, out):
    edge = jnp.where(up, 7, 0)
    for c in range(3):
        out[GROUP + 2 * c] = flow_x[c, edge, 0:8, :]
        out[GROUP + 2 * c + 1] = flow_x[c, edge, 8:16, :]


def pack_first(parts, sends, flow, in_e, in_o, out, flow_x):
    even = lax.axis_index("gy") % 2 == 0
    for c in range(3):
        flow_x[c, :, 4:12, :] = flow[c]
        a = in_e[GROUP + c]
        b = in_o[GROUP + c]
        flow_x[c, :, 12, :] = jnp.where(even, a, b)
        flow_x[c, :, 3, :] = jnp.where(even, b, a)
    up = lax.axis_index("gx") % 2 == 0
    put_blocks(parts, sends, jnp.where(up, 0, 1), out)
    put_flow(flow_x, up, out)


def pack_second(parts, sends, flow_x, out):
    up = lax.axis_index("gx") % 2 == 1
    put_blocks(parts, sends, jnp.where(up, 0, 1), out)
    put_flow(flow_x, up, out)


def couple(
    parts, sends_in, moves_in, tiles_in, slots, flow_x, in_xo, in_xe, in_ye, in_yo, after,
    pres, screen, source, solid,
    drag, dep, out_e, gain, rest,
    pool, table, sums, owned, sends, moves, tiles, sems,
):
    copies = fetch((sends_in, moves_in, tiles_in), (sends, moves, tiles), sems)
    x_even = lax.axis_index("gx") % 2 == 0
    y_even = lax.axis_index("gy") % 2 == 0
    pool[0:NB] = parts[...]
    for d, (up, even, a, b) in enumerate(
        ((0, x_even, in_xe, in_xo), (1, x_even, in_xe, in_xo), (0, y_even, in_ye, in_yo), (1, y_even, in_ye, in_yo))
    ):
        first, second = (b, a) if up == 0 else (a, b)
        pool[NB + d * MOVERS : NB + (d + 1) * MOVERS] = jnp.where(even, first[0:MOVERS], second[0:MOVERS])

    for c in range(3):
        high = jnp.where(x_even, in_xe[GROUP + 2 * c], in_xo[GROUP + 2 * c])
        high2 = jnp.where(x_even, in_xe[GROUP + 2 * c + 1], in_xo[GROUP + 2 * c + 1])
        low = jnp.where(x_even, in_xo[GROUP + 2 * c], in_xe[GROUP + 2 * c])
        low2 = jnp.where(x_even, in_xo[GROUP + 2 * c + 1], in_xe[GROUP + 2 * c + 1])
        for x in range(10):
            if x == 0:
                one, two = low, low2
            elif x == 9:
                one, two = high, high2
            else:
                one, two = flow_x[c, x - 1, 0:8, :], flow_x[c, x - 1, 8:16, :]
            table[x * 10 : x * 10 + 5, 4 + c, :] = one[3:8]
            table[x * 10 + 5 : x * 10 + 10, 4 + c, :] = two[0:5]
    sums[...] = jnp.zeros_like(sums)
    drag[...] = jnp.zeros_like(drag)
    for copy in copies:
        copy.wait()

    def stay(k, carry):
        owned[k] = 1.0
        return carry

    lax.fori_loop(0, NB, stay, 0)
    for d in range(4):

        def leave(s, carry, d=d):
            owned[sends[d, s]] = 0.0
            return carry

        lax.fori_loop(0, moves[0, d], leave, 0)
        for s in range(MOVERS):
            owned[NB + d * MOVERS + s] = jnp.where(s < moves[1, d], 1.0, 0.0)

    row = lax.broadcasted_iota(jnp.int32, (8, NB), 0)
    low_rows = row < 4
    last_row = row == 7
    half = jnp.where(low_rows, 0, 1)
    depth_rows = lax.broadcasted_iota(jnp.int32, (128, NB), 0)

    def one_block(m, at):
        own = owned[m]
        state = pool[m]
        code = jnp.broadcast_to(slots[pl.ds(at, 1), :], (8, NB))
        depth = code & 127
        slot = code >> 7
        columns = [tiles[k, at] for k in range(4)]
        seen = [jnp.take_along_axis(table[n], depth, axis=1, mode="promise_in_bounds") for n in columns]
        at_particle = jnp.where(
            slot < 2, jnp.where(slot == 0, seen[0], seen[1]), jnp.where(slot == 2, seen[2], seen[3])
        )
        coeff = jnp.broadcast_to(state[7:8], (8, NB))
        radius = jnp.broadcast_to(state[3:4], (8, NB))
        values = jnp.where(last_row, radius * radius * radius, coeff * (at_particle - state)) * own
        both = jnp.where(low_rows, pltpu.roll(values, 4, 0), values)
        for c in range(3):
            drag[c, pl.ds(at, 1), :] = both[c : c + 1]
        first = jnp.where(slot == half, both, 0.0)
        second = jnp.where(slot == half + 2, both, 0.0)
        sixteen = jnp.concatenate([first, second], axis=0)
        upper = sixteen.astype(BF16)
        lower = (sixteen - upper.astype(F32)).astype(BF16)
        pick = (depth_rows == jnp.broadcast_to(depth[0:1], (128, NB))).astype(BF16)
        spread = lax.dot_general(
            jnp.concatenate([upper, lower], axis=0), pick, (((1,), (1,)), ((), ())),
            preferred_element_type=F32,
        )
        spread = spread[0:16] + spread[16:32]
        parts_ = (
            jnp.where(low_rows, spread[0:8], 0.0), jnp.where(low_rows, 0.0, spread[0:8]),
            jnp.where(low_rows, spread[8:16], 0.0), jnp.where(low_rows, 0.0, spread[8:16]),
        )
        return columns, parts_

    def add(columns, pieces):
        olds = [sums[n] for n in columns]
        for n, old, piece in zip(columns, olds, pieces, strict=True):
            sums[n] = old + piece

    def blocks(g, carry):
        made = []
        for u in range(COUPLE_UNROLL):
            m = g * COUPLE_UNROLL + u
            at = jnp.where(m < NB, m, NB + ((m - NB) // MOVERS) * SLOTS + (m - NB) % MOVERS)
            made.append(one_block(m, at))
        for columns, pieces in made:
            add(columns, pieces)
        return carry

    lax.fori_loop(0, OWNABLE // COUPLE_UNROLL, blocks, 0)
    dep[...] = jnp.zeros_like(dep)
    for n in range(100):
        total = sums[n]
        total = total[0:4] + total[4:8]
        for f in range(4):
            dep[f, n // 10, n % 10 + 3, :] = total[f]
    gain[...] = 1.0 / (6.0 + screen[...])
    rest[...] = source[...] - 2.0 * solid[...]
    put_rims(dep, pres, gain, rest, x_even, out_e)


P_AT = 14
G_AT = P_AT + 4
S_AT = G_AT + 3
D_TILES = S_AT + 3


def put_rims(dep, pres, gain, rest, up, out):
    first = jnp.where(up, 6, 0)
    rim = jnp.where(up, 9, 0)
    for r in range(4):
        out[2 * r] = dep[3, first + r, 0:8, :]
        out[2 * r + 1] = dep[3, first + r, 8:16, :]
    for c in range(3):
        out[8 + 2 * c] = dep[c, rim, 0:8, :]
        out[9 + 2 * c] = dep[c, rim, 8:16, :]
    for at, ref, count in ((P_AT, pres, 4), (G_AT, gain, 3), (S_AT, rest, 3)):
        start = jnp.where(up, 8 - count, 0)
        for r in range(count):
            out[at + r] = ref[start + r]


def pack_fo(dep, pres, gain, rest, out):
    put_rims(dep, pres, gain, rest, lax.axis_index("gx") % 2 == 1, out)


H_DRAG = 7
H_FIELDS = H_DRAG + 3
H_TILES = H_FIELDS + 24


def fold_x(dep, pres, gain, rest, in_o, in_e, after, load, drag, pres_w, gain_w, rest_w, out_e, out_o):
    even = lax.axis_index("gx") % 2 == 0

    def from_up(at):
        return jnp.where(even, in_e[at], in_o[at])

    def from_down(at):
        return jnp.where(even, in_o[at], in_e[at])

    def two(side, at):
        return jnp.concatenate([side(at), side(at + 1)], axis=0)

    for x in range(16):
        total = jnp.zeros((16, 128), F32)
        if 3 <= x <= 12:
            total = total + dep[3, x - 3]
        if 1 <= x <= 4:
            total = total + two(from_down, 2 * (x - 1))
        if 11 <= x <= 14:
            total = total + two(from_up, 2 * (x - 11))
        load[x] = total
    for c in range(3):
        drag[c] = dep[c, 1:9]
        drag[c, 0] += two(from_down, 8 + 2 * c)
        drag[c, 7] += two(from_up, 8 + 2 * c)
    for wide, ref, at, count in ((pres_w, pres, P_AT, 4), (gain_w, gain, G_AT, 3), (rest_w, rest, S_AT, 3)):
        wide[4:12] = ref[...]
        if count == 3:
            wide[0] = jnp.zeros((8, 128), F32)
            wide[15] = jnp.zeros((8, 128), F32)
        for r in range(count):
            wide[4 - count + r] = from_down(at + r)
            wide[12 + r] = from_up(at + r)
    parity = lax.axis_index("gy") % 2
    for out, up in ((out_e, parity == 0), (out_o, parity == 1)):
        for x in range(14):
            row = 4 * (x % 2)
            out[x // 2, row : row + 4, :] = jnp.where(up, load[x + 1, 9:13, :], load[x + 1, 3:7, :])
        for c in range(3):
            out[H_DRAG + c] = jnp.where(up, drag[c, :, 12, :], drag[c, :, 3, :])
        at = H_FIELDS
        for wide in (pres_w, gain_w, rest_w):
            for x in range(16):
                row = 4 * (x % 2)
                out[at + x // 2, row : row + 4, :] = jnp.where(up, wide[x, 4:8, :], wide[x, 0:4, :])
            at += 8


def finish(load, drag, pres_w, gain_w, rest_w, in_e, in_o, pressure, drag_sum, now, new, gain, off):
    even = lax.axis_index("gy") % 2 == 0

    def half(side_up, at, x):
        row = 4 * (x % 2)
        a = in_e[at + x // 2, row : row + 4, :]
        b = in_o[at + x // 2, row : row + 4, :]
        return jnp.where(even, a, b) if side_up else jnp.where(even, b, a)

    for c in range(3):
        drag_sum[c] = drag[c, :, 4:12, :]
        a = in_e[H_DRAG + c]
        b = in_o[H_DRAG + c]
        drag_sum[c, :, 0, :] += jnp.where(even, b, a)
        drag_sum[c, :, 7, :] += jnp.where(even, a, b)

    def rows(wide, n, x):
        at = H_FIELDS + 8 * n
        return jnp.concatenate([half(False, at, x), wide[x], half(True, at, x)], axis=0)

    for x in range(16):
        now[x] = rows(pres_w, 0, x)
    for x in range(1, 15):
        off[x] = load[x]
        off[x, 1:5, :] += half(False, 0, x - 1)
        off[x, 11:15, :] += half(True, 0, x - 1)
        g = rows(gain_w, 1, x)
        gain[x] = g
        off[x] = g * (rows(rest_w, 2, x) + 2.0 * off[x])
    lane = lax.broadcasted_iota(jnp.int32, (16, 128), 1)
    inner_low = lane > 0
    inner_high = lane < 127
    source, target = now, new
    for sweep in range(ITERS):
        for x in range(sweep + 1, 15 - sweep):
            p = source[x]
            near = source[x - 1] + source[x + 1]
            near = near + pltpu.roll(p, 1, 0) + pltpu.roll(p, 15, 0)
            near = near + jnp.where(inner_low, pltpu.roll(p, 1, 1), 0.0)
            near = near + jnp.where(inner_high, pltpu.roll(p, 127, 1), 0.0)
            target[x] = gain[x] * near + off[x]
        source, target = target, source
    pressure[...] = source[4:12, 4:12, :]


def head(v):
    return v.astype(BF16).astype(F32)

def preparers(left, near, right):
    row = lax.broadcasted_iota(jnp.int32, (8, 128), 0)
    first_four = row < 4
    space = row < 3
    bias = jnp.where(space, 1.5, 0.0)
    sign = jnp.where(row == 7, 1.0, jnp.where(first_four, 0.0, -1.0))
    turned_sign = jnp.where(space, -1.0, jnp.where(row == 3, 1.0, 0.0))
    last = jnp.where(row == 7, 1.0, 0.0)

    def left_of(tile, m):
        centred = tile - bias
        v = jnp.where(first_four, centred, pltpu.roll(centred * centred, 4, 0))
        h = head(v)
        rest = v - h
        mid = head(rest)
        low = rest - mid
        extra = jnp.where(space, 1.0, jnp.where(first_four, 0.0, low))
        shifted = jnp.where(first_four, 1.0, jnp.where(row == 7, 0.0, pltpu.roll(mid, 4, 0)))
        near[m] = jnp.concatenate([jnp.where(space, h, shifted), jnp.where(space, low, 0.0)], axis=0).astype(BF16)
        return [h, h, mid, extra]

    def right_of(tile, n):
        centred = tile - bias
        square = jnp.where(first_four, centred * centred, 0.0)
        t = jnp.broadcast_to(jnp.sum(square * turned_sign, axis=0, keepdims=True), (8, 128))
        r2 = jnp.broadcast_to(square[3:4], (8, 128))
        d = jnp.where(first_four, 2.0 * centred, sign)
        h = head(d)
        mid = head(d - h)

        def terms(v):
            a = head(v)
            b = head(v - a)
            return a, b, v - a - b

        ta, tb, tc = terms(t)
        ra, rb, rc = terms(r2)
        fourth = jnp.where(row == 0, ta, jnp.where(row == 1, tb, jnp.where(row == 2, tc, sign)))
        reach = jnp.where(row == 3, h, last)
        reach_mid = jnp.where(row == 3, mid, 0.0)
        fourth_reach = jnp.where(row == 0, ra, jnp.where(row == 1, rb, jnp.where(row == 2, rc, last)))
        right[n, :, 0:128] = jnp.concatenate([h, mid, h, fourth], axis=0).astype(BF16)
        right[n, :, 128:256] = jnp.concatenate([reach, reach_mid, reach, fourth_reach], axis=0).astype(BF16)

    def four(tiles, m):
        rows = []
        for b, tile in enumerate(tiles):
            rows += left_of(tile, m + b)
        left[m // 4] = jnp.concatenate(rows, axis=0).astype(BF16).T

    return four, right_of


def lister(pairs, total, chosen, from_x):
    def along_x(m):
        return (m >= NB) & (m < NB + 2 * SLOTS)

    def look(first, count, size):
        for v in range(size):
            t = first + v
            needs = along_x(pairs[0, t]) | along_x(pairs[1, t])
            wanted = needs if from_x else jnp.logical_not(needs)
            chosen[count] = t
            count = count + jnp.where(wanted & (t < total), 1, 0)
        return count

    return look


def run_tiles(pairs, chosen, count, left, near, right, sums, begin, end):
    def tile(n):
        t = chosen[jnp.minimum(n, count - 1)]
        i = pairs[0, t]
        j = pairs[1, t]
        q = i - NB
        i = jnp.where(i < NB, i, NB + (q // SLOTS) * MOVERS + q % SLOTS)
        mine = right[i]
        place = j % 4
        none = jnp.zeros_like(mine)
        weights = jnp.concatenate([jnp.where(place == k, mine, none) for k in range(4)], axis=0)
        both = jnp.dot(left[j // 4], weights, preferred_element_type=F32)
        overlap = jnp.maximum(both[:, :128], 0.0)
        reach = both[:, 128:]
        guess = pl.reciprocal(reach, approx=True)
        weight = overlap * (guess * (2.0 - reach * guess))
        upper = weight.astype(BF16)
        lower = (weight - upper.astype(F32)).astype(BF16)
        a = near[j]
        got = jnp.dot(a, upper, preferred_element_type=F32) + jnp.dot(a, lower, preferred_element_type=F32)
        got = got[0:8] + pltpu.roll(got[0:8], 4, 0) + got[8:16]
        return i, got * jnp.where(n < count, 1.0, 0.0)

    def step(g, carry):
        made = [tile(begin + g * CONTACT_UNROLL + u) for u in range(CONTACT_UNROLL)]
        for i, got in made:
            sums[i] += got
        return carry

    lax.fori_loop(0, jnp.maximum(end - begin + CONTACT_UNROLL - 1, 0) // CONTACT_UNROLL, step, 0)


def prepare_received(four, right_of, d, even, first, second, look, at, part, count):
    for u in range(MOVERS // 4):
        tiles = [jnp.where(even, first[4 * u + b], second[4 * u + b]) for b in range(4)]
        four(tiles, NB + d * SLOTS + 4 * u)
        for b in range(4):
            right_of(tiles[b], NB + d * MOVERS + 4 * u + b)
    count = look(at, count, part)

    def others(k, count):
        for u in range(2):
            s = MOVERS + 8 * k + 4 * u
            tiles = [jnp.where(even, first[s + b], second[s + b]) for b in range(4)]
            four(tiles, NB + d * SLOTS + s)
            four([pltpu.roll(tile, 4, 0) for tile in tiles], NB + d * SLOTS + s + PAIRS)
        return look(at + (1 + k) * part, count, part)

    return lax.fori_loop(0, PAIRS // 8, others, count)


def contact_near(pairs, total_ref, parts, in_ye, in_yo, after, left, near, right, sums, chosen):
    total = total_ref[0, 0]
    sums[...] = jnp.zeros_like(sums)
    four, right_of = preparers(left, near, right)
    look = lister(pairs, total, chosen, False)
    groups = NB // 4 // PREPARE
    part = MAXT // 2 // groups

    def own(k, count):
        for u in range(PREPARE):
            m = 4 * (k * PREPARE + u)
            tiles = [parts[m + b] for b in range(4)]
            four(tiles, m)
            for b in range(4):
                right_of(tiles[b], m + b)
        return look(k * part, count, part)

    count = lax.fori_loop(0, groups, own, jnp.int32(0))
    y_even = lax.axis_index("gy") % 2 == 0
    for d, first, second in ((2, in_yo, in_ye), (3, in_ye, in_yo)):
        at = MAXT // 2 + (d - 2) * (MAXT // 4)
        count = prepare_received(four, right_of, d, y_even, first, second, look, at, MAXT // 16, count)
    run_tiles(pairs, chosen, count, left, near, right, sums, 0, count)


def received(in_xe, in_xo, in_ye, in_yo):
    x_even = lax.axis_index("gx") % 2 == 0
    y_even = lax.axis_index("gy") % 2 == 0
    return ((x_even, in_xo, in_xe), (x_even, in_xe, in_xo), (y_even, in_yo, in_ye), (y_even, in_ye, in_yo))


def contact_more(
    pairs, total_ref, in_xo, in_xe, after, left_in, near_in, right_in, sums_in,
    left, near, right, sums, chosen,
):
    total = total_ref[0, 0]
    four, right_of = preparers(left, near, right)
    look = lister(pairs, total, chosen, True)
    x_even = lax.axis_index("gx") % 2 == 0
    count = jnp.int32(0)
    for d, first, second in ((0, in_xo, in_xe), (1, in_xe, in_xo)):
        count = prepare_received(
            four, right_of, d, x_even, first, second, look, d * (MAXT // 2), MAXT // 8, count
        )
    chosen[LAST] = count
    run_tiles(pairs, chosen, count, left, near, right, sums, 0, jnp.minimum(EARLY, count))


def contact_end(
    pairs, parts, in_xo, in_xe, in_ye, in_yo, drag, after, left, near, right, chosen, sums_in, force, sums
):
    count = chosen[LAST]
    run_tiles(pairs, chosen, count, left, near, right, sums, EARLY, count)

    def put(n, at, position):
        for c in range(3):
            x = position(c) - 1.5
            w = sums[8 * n : 8 * n + 8, 3, :]
            y = sums[8 * n : 8 * n + 8, c, :]
            force[c, at : at + 8, :] = drag[c, at : at + 8, :] + 0.5 * (x * w - y)

    for n in range(NB // 8):
        put(n, 8 * n, lambda c, n=n: parts[8 * n : 8 * n + 8, c, :])
    for d, (even, first, second) in enumerate(received(in_xe, in_xo, in_ye, in_yo)):
        for k in range(2):
            put(
                NB // 8 + 2 * d + k,
                NB + d * SLOTS + 8 * k,
                lambda c, k=k, even=even, first=first, second=second: jnp.where(
                    even, first[8 * k : 8 * k + 8, c, :], second[8 * k : 8 * k + 8, c, :]
                ),
            )
        for c in range(3):
            force[c, NB + d * SLOTS + MOVERS : NB + (d + 1) * SLOTS, :] = jnp.zeros((SLOTS - MOVERS, 128), F32)


def pairs_of(first, count, last):
    up = [(i, i + 1) for i in range(first, last, 2)]
    return up + [(b, a) for a, b in up]


def swap(array, axis, first):
    count = lax.axis_size(axis)
    return lax.ppermute(array, axis, pairs_of(first, count, count - 1))


def body(
    particles,
    send_list,
    move_count,
    tile_pairs,
    tile_count,
    drag_tiles,
    cell_slot,
    fluid_velocity,
    pressure_init,
    source,
    solid_old,
    screening,
):
    parts = particles[0, 0]
    sends = send_list[0, 0]
    moves = move_count[0, 0]
    tiles = drag_tiles[0, 0].T
    pairs = tile_pairs[0, 0].T
    slots = cell_slot[0, 0]
    cells = (8, 8, 128)
    ye, yo = call(pack_y, (shape(Y_TILES, 8, 128), shape(Y_TILES, 8, 128)), [VM, SM, VM])(parts, sends, fluid_velocity)
    got_ye = swap(ye, "gy", 0)
    got_yo = swap(yo, "gy", 1)
    xe, flow_x = call(pack_first, (shape(X_TILES, 8, 128), shape(3, 8, 16, 128)), [VM, SM, VM, VM, VM])(
        parts, sends, fluid_velocity, got_ye, got_yo
    )
    got_xe = swap(xe, "gx", 0)
    xo = call(pack_second, shape(X_TILES, 8, 128), [VM, SM, VM])(parts, sends, flow_x)
    got_xo = swap(xo, "gx", 1)
    operands = (
        jax.ShapeDtypeStruct((POOL // 4, 128, 128), BF16),
        jax.ShapeDtypeStruct((POOL, 16, 128), BF16),
        jax.ShapeDtypeStruct((OWNABLE, 32, 256), BF16),
        shape(OWNABLE, 8, 128),
    )
    prepared = call(
        contact_near, operands, [SM, SM] + [VM] * 4, [pltpu.SMEM((LIST,), jnp.int32)], flops=10**8
    )(pairs, tile_count, parts, got_ye, got_yo, xo)
    drag, dep, fe, gain, rest = call(
        couple,
        (shape(3, 384, 128), shape(4, 10, 16, 128), shape(D_TILES, 8, 128), shape(*cells), shape(*cells)),
        [VM, HB, HB, HB] + [VM] * 11,
        [
            pltpu.VMEM((OWNABLE, 8, 128), F32),
            pltpu.VMEM((100, 8, 128), F32),
            pltpu.VMEM((100, 8, 128), F32),
            pltpu.SMEM((OWNABLE,), F32),
            pltpu.SMEM((4, SLOTS), jnp.int32),
            pltpu.SMEM((2, 4), jnp.int32),
            pltpu.SMEM((4, 384), jnp.int32),
            pltpu.SemaphoreType.DMA((3,)),
        ],
    )(
        parts, sends, moves, tiles, slots, flow_x, got_xo, got_xe, got_ye, got_yo, prepared[3],
        pressure_init, screening, source, solid_old,
    )
    got_fe = swap(fe, "gx", 0)
    fo = call(pack_fo, shape(D_TILES, 8, 128), [VM] * 4)(dep, pressure_init, gain, rest)
    got_fo = swap(fo, "gx", 1)
    *more, chosen = call(
        contact_more,
        (*operands, jax.ShapeDtypeStruct((LIST,), jnp.int32)),
        [SM, SM] + [VM] * 7,
        flops=10**8,
        aliases={5: 0, 6: 1, 7: 2, 8: 3},
    )(pairs, tile_count, got_xo, got_xe, fo, *prepared)
    load, drag_x, pres_w, gain_w, rest_w, he, ho = call(
        fold_x,
        (
            shape(16, 16, 128), shape(3, 8, 16, 128), shape(16, 8, 128), shape(16, 8, 128), shape(16, 8, 128),
            shape(H_TILES, 8, 128), shape(H_TILES, 8, 128),
        ),
        [VM] * 7,
    )(dep, pressure_init, gain, rest, got_fo, got_fe, more[3])
    got_he = swap(he, "gy", 0)
    got_ho = swap(ho, "gy", 1)
    force, unused = call(
        contact_end,
        (shape(3, 384, 128), operands[3]),
        [SM] + [VM] * 10 + [SM, VM],
        flops=10**9,
        aliases={12: 1},
    )(pairs, parts, got_xo, got_xe, got_ye, got_yo, drag, ho, *more[:3], chosen, more[3])
    pressure, drag_sum = call(
        finish,
        (shape(*cells), shape(3, *cells)),
        [VM] * 7,
        [pltpu.VMEM((16, 16, 128), F32)] * 4,
    )(load, drag_x, pres_w, gain_w, rest_w, got_he, got_ho)
    return (pressure, drag_sum, force.transpose(1, 0, 2)[None, None])


def solution(mesh):
    in_specs = (
        P("gx", "gy", None, None, None),
        P("gx", "gy", None, None),
        P("gx", "gy", None, None),
        P("gx", "gy", None, None),
        P("gx", "gy"),
        P("gx", "gy", None, None),
        P("gx", "gy", None, None),
        P(None, "gx", "gy", None),
        P("gx", "gy", None),
        P("gx", "gy", None),
        P("gx", "gy", None),
        P("gx", "gy", None),
    )
    out_specs = (P("gx", "gy", None), P(None, "gx", "gy", None), P("gx", "gy", None, None, None))
    return jax.shard_map(body, mesh=mesh, in_specs=in_specs, out_specs=out_specs, check_vma=False)
```

```python
import functools

import jax
import jax.numpy as jnp
from jax import lax
from jax.experimental import pallas as pl
from jax.experimental.pallas import tpu as pltpu
from jax.sharding import PartitionSpec as P

F32 = jnp.float32
BF16 = jnp.bfloat16
NB = 128
SLOTS = 64
MOVERS = 16
PAIRS = (SLOTS - MOVERS) // 2
GROUP = MOVERS + PAIRS
OWNABLE = NB + 4 * MOVERS
POOL = 384
MAXT = 512
ITERS = 4
CONTACT_UNROLL = 32
EARLY = 96
LIST = 640
LAST = LIST - 1
PREPARE = 4
COUPLE_UNROLL = 32

VM = pl.BlockSpec(memory_space=pltpu.VMEM)
SM = pl.BlockSpec(memory_space=pltpu.SMEM)
HB = pl.BlockSpec(memory_space=pltpu.HBM)
PARAMS = pltpu.CompilerParams(vmem_limit_bytes=32 * 2**20)


def shape(*dims):
    return jax.ShapeDtypeStruct(dims, F32)


def call(kernel, outs, in_specs, scratch=(), flops=10**6, moved=10**6, aliases=None):
    return pl.pallas_call(
        kernel,
        out_shape=outs,
        in_specs=in_specs,
        out_specs=jax.tree.map(lambda o: SM if len(o.shape) == 1 else VM, outs),
        scratch_shapes=list(scratch),
        input_output_aliases=aliases or {},
        compiler_params=PARAMS,
        cost_estimate=pl.CostEstimate(flops=flops, bytes_accessed=moved, transcendentals=0),
    )


def put_blocks(parts, sends, direction, out):
    for s in range(MOVERS):
        out[s] = parts[sends[direction, s]]
    for k in range(PAIRS):
        out[MOVERS + k, 0:4, :] = parts[sends[direction, MOVERS + k], 0:4, :]
        out[MOVERS + k, 4:8, :] = parts[sends[direction, MOVERS + PAIRS + k], 0:4, :]


def fetch(sources, targets, sems):
    copies = [pltpu.make_async_copy(a, b, sems.at[n]) for n, (a, b) in enumerate(zip(sources, targets, strict=True))]
    for copy in copies:
        copy.start()
    return copies


Y_TILES = GROUP + 3
X_TILES = GROUP + 6


def pack_y(parts, sends, flow, out_e, out_o):
    parity = lax.axis_index("gy") % 2
    for out, up in ((out_e, parity == 0), (out_o, parity == 1)):
        put_blocks(parts, sends, jnp.where(up, 2, 3), out)
        for c in range(3):
            out[GROUP + c] = jnp.where(up, flow[c, :, 7, :], flow[c, :, 0, :])


def put_flow(flow_x, up, out):
    edge = jnp.where(up, 7, 0)
    for c in range(3):
        out[GROUP + 2 * c] = flow_x[c, edge, 0:8, :]
        out[GROUP + 2 * c + 1] = flow_x[c, edge, 8:16, :]


def pack_first(parts, sends, flow, in_e, in_o, out, flow_x):
    even = lax.axis_index("gy") % 2 == 0
    for c in range(3):
        flow_x[c, :, 4:12, :] = flow[c]
        a = in_e[GROUP + c]
        b = in_o[GROUP + c]
        flow_x[c, :, 12, :] = jnp.where(even, a, b)
        flow_x[c, :, 3, :] = jnp.where(even, b, a)
    up = lax.axis_index("gx") % 2 == 0
    put_blocks(parts, sends, jnp.where(up, 0, 1), out)
    put_flow(flow_x, up, out)


def pack_second(parts, sends, flow_x, out):
    up = lax.axis_index("gx") % 2 == 1
    put_blocks(parts, sends, jnp.where(up, 0, 1), out)
    put_flow(flow_x, up, out)


def couple(
    parts, sends_in, moves_in, tiles_in, slots, flow_x, in_xo, in_xe, in_ye, in_yo, after,
    pres, screen, source, solid,
    drag, dep, out_o, gain, rest,
    pool, table, sums, owned, sends, moves, tiles, sems,
):
    copies = fetch((sends_in, moves_in, tiles_in), (sends, moves, tiles), sems)
    for k in range(NB):
        owned[k] = 1.0
    x_even = lax.axis_index("gx") % 2 == 0
    y_even = lax.axis_index("gy") % 2 == 0
    pool[0:NB] = parts[...]
    for d, (up, even, a, b) in enumerate(
        ((0, x_even, in_xe, in_xo), (1, x_even, in_xe, in_xo), (0, y_even, in_ye, in_yo), (1, y_even, in_ye, in_yo))
    ):
        first, second = (b, a) if up == 0 else (a, b)
        pool[NB + d * MOVERS : NB + (d + 1) * MOVERS] = jnp.where(even, first[0:MOVERS], second[0:MOVERS])

    for c in range(3):
        high = jnp.where(x_even, in_xe[GROUP + 2 * c], in_xo[GROUP + 2 * c])
        high2 = jnp.where(x_even, in_xe[GROUP + 2 * c + 1], in_xo[GROUP + 2 * c + 1])
        low = jnp.where(x_even, in_xo[GROUP + 2 * c], in_xe[GROUP + 2 * c])
        low2 = jnp.where(x_even, in_xo[GROUP + 2 * c + 1], in_xe[GROUP + 2 * c + 1])
        for x in range(10):
            if x == 0:
                one, two = low, low2
            elif x == 9:
                one, two = high, high2
            else:
                one, two = flow_x[c, x - 1, 0:8, :], flow_x[c, x - 1, 8:16, :]
            table[x * 10 : x * 10 + 5, 4 + c, :] = one[3:8]
            table[x * 10 + 5 : x * 10 + 10, 4 + c, :] = two[0:5]
    sums[...] = jnp.zeros_like(sums)
    drag[...] = jnp.zeros_like(drag)
    for copy in copies:
        copy.wait()

    for d in range(4):

        def leave(s, carry, d=d):
            owned[sends[d, s]] = 0.0
            return carry

        lax.fori_loop(0, moves[0, d], leave, 0)
        for s in range(MOVERS):
            owned[NB + d * MOVERS + s] = jnp.where(s < moves[1, d], 1.0, 0.0)

    row = lax.broadcasted_iota(jnp.int32, (8, NB), 0)
    low_rows = row < 4
    last_row = row == 7
    half = jnp.where(low_rows, 0, 1)
    depth_rows = lax.broadcasted_iota(jnp.int32, (128, NB), 0)

    def one_block(m, at):
        own = owned[m]
        state = pool[m]
        code = jnp.broadcast_to(slots[pl.ds(at, 1), :], (8, NB))
        depth = code & 127
        slot = code >> 7
        columns = [tiles[k, at] for k in range(4)]
        seen = [jnp.take_along_axis(table[n], depth, axis=1, mode="promise_in_bounds") for n in columns]
        at_particle = jnp.where(
            slot < 2, jnp.where(slot == 0, seen[0], seen[1]), jnp.where(slot == 2, seen[2], seen[3])
        )
        coeff = jnp.broadcast_to(state[7:8], (8, NB))
        radius = jnp.broadcast_to(state[3:4], (8, NB))
        values = jnp.where(last_row, radius * radius * radius, coeff * (at_particle - state)) * own
        both = jnp.where(low_rows, pltpu.roll(values, 4, 0), values)
        for c in range(3):
            drag[c, pl.ds(at, 1), :] = both[c : c + 1]
        first = jnp.where(slot == half, both, 0.0)
        second = jnp.where(slot == half + 2, both, 0.0)
        sixteen = jnp.concatenate([first, second], axis=0)
        upper = sixteen.astype(BF16)
        lower = (sixteen - upper.astype(F32)).astype(BF16)
        pick = (depth_rows == jnp.broadcast_to(depth[0:1], (128, NB))).astype(BF16)
        spread = lax.dot_general(
            jnp.concatenate([upper, lower], axis=0), pick, (((1,), (1,)), ((), ())),
            preferred_element_type=F32,
        )
        spread = spread[0:16] + spread[16:32]
        parts_ = (
            jnp.where(low_rows, spread[0:8], 0.0), jnp.where(low_rows, 0.0, spread[0:8]),
            jnp.where(low_rows, spread[8:16], 0.0), jnp.where(low_rows, 0.0, spread[8:16]),
        )
        return columns, parts_

    def add(columns, pieces):
        olds = [sums[n] for n in columns]
        for n, old, piece in zip(columns, olds, pieces, strict=True):
            sums[n] = old + piece

    def blocks(g, carry):
        made = []
        for u in range(COUPLE_UNROLL):
            m = g * COUPLE_UNROLL + u
            at = jnp.where(m < NB, m, NB + ((m - NB) // MOVERS) * SLOTS + (m - NB) % MOVERS)
            made.append(one_block(m, at))
        for columns, pieces in made:
            add(columns, pieces)
        return carry

    lax.fori_loop(0, OWNABLE // COUPLE_UNROLL, blocks, 0)
    dep[...] = jnp.zeros_like(dep)
    for n in range(100):
        total = sums[n]
        total = total[0:4] + total[4:8]
        for f in range(4):
            dep[f, n // 10, n % 10 + 3, :] = total[f]
    gain[...] = 1.0 / (6.0 + screen[...])
    rest[...] = source[...] - 2.0 * solid[...]
    put_rims(dep, pres, gain, rest, jnp.logical_not(x_even), out_o)


P_AT = 14
G_AT = P_AT + 4
S_AT = G_AT + 3
D_TILES = S_AT + 3


def put_rims(dep, pres, gain, rest, up, out):
    first = jnp.where(up, 6, 0)
    rim = jnp.where(up, 9, 0)
    for r in range(4):
        out[2 * r] = dep[3, first + r, 0:8, :]
        out[2 * r + 1] = dep[3, first + r, 8:16, :]
    for c in range(3):
        out[8 + 2 * c] = dep[c, rim, 0:8, :]
        out[9 + 2 * c] = dep[c, rim, 8:16, :]
    for at, ref, count in ((P_AT, pres, 4), (G_AT, gain, 3), (S_AT, rest, 3)):
        start = jnp.where(up, 8 - count, 0)
        for r in range(count):
            out[at + r] = ref[start + r]


def pack_fe(dep, pres, gain, rest, out):
    put_rims(dep, pres, gain, rest, lax.axis_index("gx") % 2 == 0, out)


H_DRAG = 7
H_FIELDS = H_DRAG + 3
H_TILES = H_FIELDS + 24


def fold_x(dep, pres, gain, rest, in_o, in_e, after, load, drag, pres_w, gain_w, rest_w, out_e, out_o):
    even = lax.axis_index("gx") % 2 == 0

    def from_up(at):
        return jnp.where(even, in_e[at], in_o[at])

    def from_down(at):
        return jnp.where(even, in_o[at], in_e[at])

    def two(side, at):
        return jnp.concatenate([side(at), side(at + 1)], axis=0)

    for x in range(16):
        total = jnp.zeros((16, 128), F32)
        if 3 <= x <= 12:
            total = total + dep[3, x - 3]
        if 1 <= x <= 4:
            total = total + two(from_down, 2 * (x - 1))
        if 11 <= x <= 14:
            total = total + two(from_up, 2 * (x - 11))
        load[x] = total
    for c in range(3):
        drag[c] = dep[c, 1:9]
        drag[c, 0] += two(from_down, 8 + 2 * c)
        drag[c, 7] += two(from_up, 8 + 2 * c)
    for wide, ref, at, count in ((pres_w, pres, P_AT, 4), (gain_w, gain, G_AT, 3), (rest_w, rest, S_AT, 3)):
        wide[4:12] = ref[...]
        if count == 3:
            wide[0] = jnp.zeros((8, 128), F32)
            wide[15] = jnp.zeros((8, 128), F32)
        for r in range(count):
            wide[4 - count + r] = from_down(at + r)
            wide[12 + r] = from_up(at + r)
    parity = lax.axis_index("gy") % 2
    for out, up in ((out_e, parity == 0), (out_o, parity == 1)):
        for x in range(14):
            row = 4 * (x % 2)
            out[x // 2, row : row + 4, :] = jnp.where(up, load[x + 1, 9:13, :], load[x + 1, 3:7, :])
        for c in range(3):
            out[H_DRAG + c] = jnp.where(up, drag[c, :, 12, :], drag[c, :, 3, :])
        at = H_FIELDS
        for wide in (pres_w, gain_w, rest_w):
            for x in range(16):
                row = 4 * (x % 2)
                out[at + x // 2, row : row + 4, :] = jnp.where(up, wide[x, 4:8, :], wide[x, 0:4, :])
            at += 8


def finish(load, drag, pres_w, gain_w, rest_w, in_e, in_o, pressure, drag_sum, now, new, gain, off):
    even = lax.axis_index("gy") % 2 == 0

    def half(side_up, at, x):
        row = 4 * (x % 2)
        a = in_e[at + x // 2, row : row + 4, :]
        b = in_o[at + x // 2, row : row + 4, :]
        return jnp.where(even, a, b) if side_up else jnp.where(even, b, a)

    for c in range(3):
        drag_sum[c] = drag[c, :, 4:12, :]
        a = in_e[H_DRAG + c]
        b = in_o[H_DRAG + c]
        drag_sum[c, :, 0, :] += jnp.where(even, b, a)
        drag_sum[c, :, 7, :] += jnp.where(even, a, b)

    def rows(wide, n, x):
        at = H_FIELDS + 8 * n
        return jnp.concatenate([half(False, at, x), wide[x], half(True, at, x)], axis=0)

    for x in range(16):
        now[x] = rows(pres_w, 0, x)
    for x in range(1, 15):
        off[x] = load[x]
        off[x, 1:5, :] += half(False, 0, x - 1)
        off[x, 11:15, :] += half(True, 0, x - 1)
        g = rows(gain_w, 1, x)
        gain[x] = g
        off[x] = g * (rows(rest_w, 2, x) + 2.0 * off[x])
    lane = lax.broadcasted_iota(jnp.int32, (16, 128), 1)
    inner_low = lane > 0
    inner_high = lane < 127
    source, target = now, new
    for sweep in range(ITERS):
        for x in range(sweep + 1, 15 - sweep):
            p = source[x]
            near = source[x - 1] + source[x + 1]
            near = near + pltpu.roll(p, 1, 0) + pltpu.roll(p, 15, 0)
            near = near + jnp.where(inner_low, pltpu.roll(p, 1, 1), 0.0)
            near = near + jnp.where(inner_high, pltpu.roll(p, 127, 1), 0.0)
            target[x] = gain[x] * near + off[x]
        source, target = target, source
    pressure[...] = source[4:12, 4:12, :]


def head(v):
    return v.astype(BF16).astype(F32)

def preparers(left, near, right):
    row = lax.broadcasted_iota(jnp.int32, (8, 128), 0)
    first_four = row < 4
    space = row < 3
    bias = jnp.where(space, 1.5, 0.0)
    sign = jnp.where(row == 7, 1.0, jnp.where(first_four, 0.0, -1.0))
    turned_sign = jnp.where(space, -1.0, jnp.where(row == 3, 1.0, 0.0))
    last = jnp.where(row == 7, 1.0, 0.0)

    def left_of(tile, m):
        centred = tile - bias
        v = jnp.where(first_four, centred, pltpu.roll(centred * centred, 4, 0))
        h = head(v)
        rest = v - h
        mid = head(rest)
        low = rest - mid
        extra = jnp.where(space, 1.0, jnp.where(first_four, 0.0, low))
        shifted = jnp.where(first_four, 1.0, jnp.where(row == 7, 0.0, pltpu.roll(mid, 4, 0)))
        near[m] = jnp.concatenate([jnp.where(space, h, shifted), jnp.where(space, low, 0.0)], axis=0).astype(BF16)
        return [h, h, mid, extra]

    def right_of(tile, n):
        centred = tile - bias
        square = jnp.where(first_four, centred * centred, 0.0)
        t = jnp.broadcast_to(jnp.sum(square * turned_sign, axis=0, keepdims=True), (8, 128))
        r2 = jnp.broadcast_to(square[3:4], (8, 128))
        d = jnp.where(first_four, 2.0 * centred, sign)
        h = head(d)
        mid = head(d - h)

        def terms(v):
            a = head(v)
            b = head(v - a)
            return a, b, v - a - b

        ta, tb, tc = terms(t)
        ra, rb, rc = terms(r2)
        fourth = jnp.where(row == 0, ta, jnp.where(row == 1, tb, jnp.where(row == 2, tc, sign)))
        reach = jnp.where(row == 3, h, last)
        reach_mid = jnp.where(row == 3, mid, 0.0)
        fourth_reach = jnp.where(row == 0, ra, jnp.where(row == 1, rb, jnp.where(row == 2, rc, last)))
        right[n, :, 0:128] = jnp.concatenate([h, mid, h, fourth], axis=0).astype(BF16)
        right[n, :, 128:256] = jnp.concatenate([reach, reach_mid, reach, fourth_reach], axis=0).astype(BF16)

    def four(tiles, m):
        rows = []
        for b, tile in enumerate(tiles):
            rows += left_of(tile, m + b)
        left[m // 4] = jnp.concatenate(rows, axis=0).astype(BF16).T

    return four, right_of


def lister(pairs, total, chosen, from_x):
    def along_x(m):
        return (m >= NB) & (m < NB + 2 * SLOTS)

    def look(first, count, size):
        for v in range(size):
            t = first + v
            needs = along_x(pairs[0, t]) | along_x(pairs[1, t])
            wanted = needs if from_x else jnp.logical_not(needs)
            chosen[count] = t
            count = count + jnp.where(wanted & (t < total), 1, 0)
        return count

    return look


def run_tiles(pairs, chosen, count, left, near, right, sums, begin, end):
    def tile(n):
        t = chosen[jnp.minimum(n, count - 1)]
        i = pairs[0, t]
        j = pairs[1, t]
        q = i - NB
        i = jnp.where(i < NB, i, NB + (q // SLOTS) * MOVERS + q % SLOTS)
        mine = right[i]
        place = j % 4
        none = jnp.zeros_like(mine)
        weights = jnp.concatenate([jnp.where(place == k, mine, none) for k in range(4)], axis=0)
        both = jnp.dot(left[j // 4], weights, preferred_element_type=F32)
        overlap = jnp.maximum(both[:, :128], 0.0)
        reach = both[:, 128:]
        guess = pl.reciprocal(reach, approx=True)
        weight = overlap * (guess * (2.0 - reach * guess))
        upper = weight.astype(BF16)
        lower = (weight - upper.astype(F32)).astype(BF16)
        a = near[j]
        got = jnp.dot(a, upper, preferred_element_type=F32) + jnp.dot(a, lower, preferred_element_type=F32)
        got = got[0:8] + pltpu.roll(got[0:8], 4, 0) + got[8:16]
        return i, got * jnp.where(n < count, 1.0, 0.0)

    def step(g, carry):
        made = [tile(begin + g * CONTACT_UNROLL + u) for u in range(CONTACT_UNROLL)]
        for i, got in made:
            sums[i] += got
        return carry

    lax.fori_loop(0, jnp.maximum(end - begin + CONTACT_UNROLL - 1, 0) // CONTACT_UNROLL, step, 0)


def prepare_received(four, right_of, d, even, first, second, look, at, part, count):
    for u in range(MOVERS // 4):
        tiles = [jnp.where(even, first[4 * u + b], second[4 * u + b]) for b in range(4)]
        four(tiles, NB + d * SLOTS + 4 * u)
        for b in range(4):
            right_of(tiles[b], NB + d * MOVERS + 4 * u + b)
    count = look(at, count, part)

    def others(k, count):
        for u in range(2):
            s = MOVERS + 8 * k + 4 * u
            tiles = [jnp.where(even, first[s + b], second[s + b]) for b in range(4)]
            four(tiles, NB + d * SLOTS + s)
            four([pltpu.roll(tile, 4, 0) for tile in tiles], NB + d * SLOTS + s + PAIRS)
        return look(at + (1 + k) * part, count, part)

    return lax.fori_loop(0, PAIRS // 8, others, count)


def contact_near(pairs, total_ref, parts, in_ye, in_yo, after, left, near, right, sums, chosen):
    total = total_ref[0, 0]
    sums[...] = jnp.zeros_like(sums)
    four, right_of = preparers(left, near, right)
    look = lister(pairs, total, chosen, False)
    groups = NB // 4 // PREPARE
    part = MAXT // 2 // groups

    def own(k, count):
        for u in range(PREPARE):
            m = 4 * (k * PREPARE + u)
            tiles = [parts[m + b] for b in range(4)]
            four(tiles, m)
            for b in range(4):
                right_of(tiles[b], m + b)
        return look(k * part, count, part)

    count = lax.fori_loop(0, groups, own, jnp.int32(0))
    y_even = lax.axis_index("gy") % 2 == 0
    for d, first, second in ((2, in_yo, in_ye), (3, in_ye, in_yo)):
        at = MAXT // 2 + (d - 2) * (MAXT // 4)
        count = prepare_received(four, right_of, d, y_even, first, second, look, at, MAXT // 16, count)
    run_tiles(pairs, chosen, count, left, near, right, sums, 0, count)


def received(in_xe, in_xo, in_ye, in_yo):
    x_even = lax.axis_index("gx") % 2 == 0
    y_even = lax.axis_index("gy") % 2 == 0
    return ((x_even, in_xo, in_xe), (x_even, in_xe, in_xo), (y_even, in_yo, in_ye), (y_even, in_ye, in_yo))


def contact_more(
    pairs, total_ref, in_xo, in_xe, after, left_in, near_in, right_in, sums_in,
    left, near, right, sums, chosen,
):
    total = total_ref[0, 0]
    four, right_of = preparers(left, near, right)
    look = lister(pairs, total, chosen, True)
    x_even = lax.axis_index("gx") % 2 == 0
    count = jnp.int32(0)
    for d, first, second in ((0, in_xo, in_xe), (1, in_xe, in_xo)):
        count = prepare_received(
            four, right_of, d, x_even, first, second, look, d * (MAXT // 2), MAXT // 8, count
        )
    chosen[LAST] = count
    run_tiles(pairs, chosen, count, left, near, right, sums, 0, jnp.minimum(EARLY, count))


def contact_end(
    pairs, parts, in_xo, in_xe, in_ye, in_yo, drag, after, left, near, right, chosen, sums_in, force, sums
):
    count = chosen[LAST]
    run_tiles(pairs, chosen, count, left, near, right, sums, EARLY, count)

    def put(n, at, position):
        for c in range(3):
            x = position(c) - 1.5
            w = sums[8 * n : 8 * n + 8, 3, :]
            y = sums[8 * n : 8 * n + 8, c, :]
            force[c, at : at + 8, :] = drag[c, at : at + 8, :] + 0.5 * (x * w - y)

    for n in range(NB // 8):
        put(n, 8 * n, lambda c, n=n: parts[8 * n : 8 * n + 8, c, :])
    for d, (even, first, second) in enumerate(received(in_xe, in_xo, in_ye, in_yo)):
        for k in range(2):
            put(
                NB // 8 + 2 * d + k,
                NB + d * SLOTS + 8 * k,
                lambda c, k=k, even=even, first=first, second=second: jnp.where(
                    even, first[8 * k : 8 * k + 8, c, :], second[8 * k : 8 * k + 8, c, :]
                ),
            )
        for c in range(3):
            force[c, NB + d * SLOTS + MOVERS : NB + (d + 1) * SLOTS, :] = jnp.zeros((SLOTS - MOVERS, 128), F32)


def pairs_of(first, count, last):
    up = [(i, i + 1) for i in range(first, last, 2)]
    return up + [(b, a) for a, b in up]


def swap(array, axis, first):
    count = lax.axis_size(axis)
    return lax.ppermute(array, axis, pairs_of(first, count, count - 1))


def body(
    particles,
    send_list,
    move_count,
    tile_pairs,
    tile_count,
    drag_tiles,
    cell_slot,
    fluid_velocity,
    pressure_init,
    source,
    solid_old,
    screening,
):
    parts = particles[0, 0]
    sends = send_list[0, 0]
    moves = move_count[0, 0]
    tiles = drag_tiles[0, 0].T
    pairs = tile_pairs[0, 0].T
    slots = cell_slot[0, 0]
    cells = (8, 8, 128)
    ye, yo = call(pack_y, (shape(Y_TILES, 8, 128), shape(Y_TILES, 8, 128)), [VM, SM, VM])(parts, sends, fluid_velocity)
    got_ye = swap(ye, "gy", 0)
    got_yo = swap(yo, "gy", 1)
    xe, flow_x = call(pack_first, (shape(X_TILES, 8, 128), shape(3, 8, 16, 128)), [VM, SM, VM, VM, VM])(
        parts, sends, fluid_velocity, got_ye, got_yo
    )
    got_xe = swap(xe, "gx", 0)
    xo = call(pack_second, shape(X_TILES, 8, 128), [VM, SM, VM])(parts, sends, flow_x)
    got_xo = swap(xo, "gx", 1)
    operands = (
        jax.ShapeDtypeStruct((POOL // 4, 128, 128), BF16),
        jax.ShapeDtypeStruct((POOL, 16, 128), BF16),
        jax.ShapeDtypeStruct((OWNABLE, 32, 256), BF16),
        shape(OWNABLE, 8, 128),
    )
    prepared = call(
        contact_near, operands, [SM, SM] + [VM] * 4, [pltpu.SMEM((LIST,), jnp.int32)], flops=10**8
    )(pairs, tile_count, parts, got_ye, got_yo, xo)
    drag, dep, fo, gain, rest = call(
        couple,
        (shape(3, 384, 128), shape(4, 10, 16, 128), shape(D_TILES, 8, 128), shape(*cells), shape(*cells)),
        [VM, HB, HB, HB] + [VM] * 11,
        [
            pltpu.VMEM((OWNABLE, 8, 128), F32),
            pltpu.VMEM((100, 8, 128), F32),
            pltpu.VMEM((100, 8, 128), F32),
            pltpu.SMEM((OWNABLE,), F32),
            pltpu.SMEM((4, SLOTS), jnp.int32),
            pltpu.SMEM((2, 4), jnp.int32),
            pltpu.SMEM((4, 384), jnp.int32),
            pltpu.SemaphoreType.DMA((3,)),
        ],
    )(
        parts, sends, moves, tiles, slots, flow_x, got_xo, got_xe, got_ye, got_yo, prepared[3],
        pressure_init, screening, source, solid_old,
    )
    got_fo = swap(fo, "gx", 1)
    fe = call(pack_fe, shape(D_TILES, 8, 128), [VM] * 4)(dep, pressure_init, gain, rest)
    got_fe = swap(fe, "gx", 0)
    *more, chosen = call(
        contact_more,
        (*operands, jax.ShapeDtypeStruct((LIST,), jnp.int32)),
        [SM, SM] + [VM] * 7,
        flops=10**8,
        aliases={5: 0, 6: 1, 7: 2, 8: 3},
    )(pairs, tile_count, got_xo, got_xe, fe, *prepared)
    load, drag_x, pres_w, gain_w, rest_w, he, ho = call(
        fold_x,
        (
            shape(16, 16, 128), shape(3, 8, 16, 128), shape(16, 8, 128), shape(16, 8, 128), shape(16, 8, 128),
            shape(H_TILES, 8, 128), shape(H_TILES, 8, 128),
        ),
        [VM] * 7,
    )(dep, pressure_init, gain, rest, got_fo, got_fe, more[3])
    got_he = swap(he, "gy", 0)
    got_ho = swap(ho, "gy", 1)
    force, unused = call(
        contact_end,
        (shape(3, 384, 128), operands[3]),
        [SM] + [VM] * 10 + [SM, VM],
        flops=10**9,
        aliases={12: 1},
    )(pairs, parts, got_xo, got_xe, got_ye, got_yo, drag, ho, *more[:3], chosen, more[3])
    pressure, drag_sum = call(
        finish,
        (shape(*cells), shape(3, *cells)),
        [VM] * 7,
        [pltpu.VMEM((16, 16, 128), F32)] * 4,
    )(load, drag_x, pres_w, gain_w, rest_w, got_he, got_ho)
    return (pressure, drag_sum, force.transpose(1, 0, 2)[None, None])


def solution(mesh):
    in_specs = (
        P("gx", "gy", None, None, None),
        P("gx", "gy", None, None),
        P("gx", "gy", None, None),
        P("gx", "gy", None, None),
        P("gx", "gy"),
        P("gx", "gy", None, None),
        P("gx", "gy", None, None),
        P(None, "gx", "gy", None),
        P("gx", "gy", None),
        P("gx", "gy", None),
        P("gx", "gy", None),
        P("gx", "gy", None),
    )
    out_specs = (P("gx", "gy", None), P(None, "gx", "gy", None), P("gx", "gy", None, None, None))
    return jax.shard_map(body, mesh=mesh, in_specs=in_specs, out_specs=out_specs, check_vma=False)
```

```python
import functools

import jax
import jax.numpy as jnp
from jax import lax
from jax.experimental import pallas as pl
from jax.experimental.pallas import tpu as pltpu
from jax.sharding import PartitionSpec as P

F32 = jnp.float32
BF16 = jnp.bfloat16
NB = 128
SLOTS = 64
MOVERS = 16
PAIRS = (SLOTS - MOVERS) // 2
GROUP = MOVERS + PAIRS
OWNABLE = NB + 4 * MOVERS
POOL = 384
MAXT = 512
ITERS = 4
CONTACT_UNROLL = 32
EARLY = 96
LIST = 640
LAST = LIST - 1
PREPARE = 4
COUPLE_UNROLL = 32

VM = pl.BlockSpec(memory_space=pltpu.VMEM)
SM = pl.BlockSpec(memory_space=pltpu.SMEM)
HB = pl.BlockSpec(memory_space=pltpu.HBM)
PARAMS = pltpu.CompilerParams(vmem_limit_bytes=32 * 2**20)


def shape(*dims):
    return jax.ShapeDtypeStruct(dims, F32)


def call(kernel, outs, in_specs, scratch=(), flops=10**6, moved=10**6):
    return pl.pallas_call(
        kernel,
        out_shape=outs,
        in_specs=in_specs,
        out_specs=jax.tree.map(lambda o: SM if len(o.shape) == 1 else VM, outs),
        scratch_shapes=list(scratch),
        compiler_params=PARAMS,
        cost_estimate=pl.CostEstimate(flops=flops, bytes_accessed=moved, transcendentals=0),
    )


def put_blocks(parts, sends, direction, out):
    for s in range(MOVERS):
        out[s] = parts[sends[direction, s]]
    for k in range(PAIRS):
        out[MOVERS + k, 0:4, :] = parts[sends[direction, MOVERS + k], 0:4, :]
        out[MOVERS + k, 4:8, :] = parts[sends[direction, MOVERS + PAIRS + k], 0:4, :]


def fetch(sources, targets, sems):
    copies = [pltpu.make_async_copy(a, b, sems.at[n]) for n, (a, b) in enumerate(zip(sources, targets, strict=True))]
    for copy in copies:
        copy.start()
    return copies


Y_TILES = GROUP + 3
X_TILES = GROUP + 6


def pack_y(parts, sends, flow, out_e, out_o):
    parity = lax.axis_index("gy") % 2
    for out, up in ((out_e, parity == 0), (out_o, parity == 1)):
        put_blocks(parts, sends, jnp.where(up, 2, 3), out)
        for c in range(3):
            out[GROUP + c] = jnp.where(up, flow[c, :, 7, :], flow[c, :, 0, :])


def put_flow(flow_x, up, out):
    edge = jnp.where(up, 7, 0)
    for c in range(3):
        out[GROUP + 2 * c] = flow_x[c, edge, 0:8, :]
        out[GROUP + 2 * c + 1] = flow_x[c, edge, 8:16, :]


def pack_first(parts, sends, flow, in_e, in_o, out, flow_x):
    even = lax.axis_index("gy") % 2 == 0
    for c in range(3):
        flow_x[c, :, 4:12, :] = flow[c]
        a = in_e[GROUP + c]
        b = in_o[GROUP + c]
        flow_x[c, :, 12, :] = jnp.where(even, a, b)
        flow_x[c, :, 3, :] = jnp.where(even, b, a)
    up = lax.axis_index("gx") % 2 == 0
    put_blocks(parts, sends, jnp.where(up, 0, 1), out)
    put_flow(flow_x, up, out)


def pack_second(parts, sends, flow_x, out):
    up = lax.axis_index("gx") % 2 == 1
    put_blocks(parts, sends, jnp.where(up, 0, 1), out)
    put_flow(flow_x, up, out)


def couple(
    parts, sends_in, moves_in, tiles_in, slots, flow_x, in_xo, in_xe, in_ye, in_yo, after,
    pres, screen, source, solid,
    drag, dep, out_o, gain, rest,
    pool, table, sums, owned, blocks_held, sends, moves, tiles, sems,
):
    copies = fetch((sends_in, moves_in, tiles_in), (sends, moves, tiles), sems)
    for k in range(NB):
        owned[k] = 1.0
    x_even = lax.axis_index("gx") % 2 == 0
    y_even = lax.axis_index("gy") % 2 == 0
    pool[0:NB] = parts[...]
    for d, (up, even, a, b) in enumerate(
        ((0, x_even, in_xe, in_xo), (1, x_even, in_xe, in_xo), (0, y_even, in_ye, in_yo), (1, y_even, in_ye, in_yo))
    ):
        first, second = (b, a) if up == 0 else (a, b)
        pool[NB + d * MOVERS : NB + (d + 1) * MOVERS] = jnp.where(even, first[0:MOVERS], second[0:MOVERS])

    for c in range(3):
        high = jnp.where(x_even, in_xe[GROUP + 2 * c], in_xo[GROUP + 2 * c])
        high2 = jnp.where(x_even, in_xe[GROUP + 2 * c + 1], in_xo[GROUP + 2 * c + 1])
        low = jnp.where(x_even, in_xo[GROUP + 2 * c], in_xe[GROUP + 2 * c])
        low2 = jnp.where(x_even, in_xo[GROUP + 2 * c + 1], in_xe[GROUP + 2 * c + 1])
        for x in range(10):
            if x == 0:
                one, two = low, low2
            elif x == 9:
                one, two = high, high2
            else:
                one, two = flow_x[c, x - 1, 0:8, :], flow_x[c, x - 1, 8:16, :]
            table[x * 10 : x * 10 + 5, 4 + c, :] = one[3:8]
            table[x * 10 + 5 : x * 10 + 10, 4 + c, :] = two[0:5]
    sums[...] = jnp.zeros_like(sums)
    drag[...] = jnp.zeros_like(drag)
    for copy in copies:
        copy.wait()

    for d in range(4):

        def leave(s, carry, d=d):
            owned[sends[d, s]] = 0.0
            return carry

        lax.fori_loop(0, moves[0, d], leave, 0)
        for s in range(MOVERS):
            owned[NB + d * MOVERS + s] = jnp.where(s < moves[1, d], 1.0, 0.0)
    held = jnp.int32(0)
    for m in range(OWNABLE):
        blocks_held[held] = m
        held = held + jnp.where(owned[m] > 0.5, 1, 0)

    row = lax.broadcasted_iota(jnp.int32, (8, NB), 0)
    low_rows = row < 4
    last_row = row == 7
    half = jnp.where(low_rows, 0, 1)
    depth_rows = lax.broadcasted_iota(jnp.int32, (128, NB), 0)

    def one_block(m, at, counts):
        state = pool[m]
        code = jnp.broadcast_to(slots[pl.ds(at, 1), :], (8, NB))
        depth = code & 127
        slot = code >> 7
        columns = [tiles[k, at] for k in range(4)]
        seen = [jnp.take_along_axis(table[n], depth, axis=1, mode="promise_in_bounds") for n in columns]
        at_particle = jnp.where(
            slot < 2, jnp.where(slot == 0, seen[0], seen[1]), jnp.where(slot == 2, seen[2], seen[3])
        )
        coeff = jnp.broadcast_to(state[7:8], (8, NB))
        radius = jnp.broadcast_to(state[3:4], (8, NB))
        values = jnp.where(last_row, radius * radius * radius, coeff * (at_particle - state))
        both = jnp.where(low_rows, pltpu.roll(values, 4, 0), values)
        for c in range(3):
            drag[c, pl.ds(at, 1), :] = both[c : c + 1]
        first = jnp.where(slot == half, both, 0.0)
        second = jnp.where(slot == half + 2, both, 0.0)
        sixteen = jnp.concatenate([first, second], axis=0)
        upper = sixteen.astype(BF16)
        lower = (sixteen - upper.astype(F32)).astype(BF16)
        pick = (depth_rows == jnp.broadcast_to(depth[0:1], (128, NB))).astype(BF16)
        spread = lax.dot_general(
            jnp.concatenate([upper, lower], axis=0), pick, (((1,), (1,)), ((), ())),
            preferred_element_type=F32,
        )
        spread = (spread[0:16] + spread[16:32]) * counts
        parts_ = (
            jnp.where(low_rows, spread[0:8], 0.0), jnp.where(low_rows, 0.0, spread[0:8]),
            jnp.where(low_rows, spread[8:16], 0.0), jnp.where(low_rows, 0.0, spread[8:16]),
        )
        return columns, parts_

    def add(columns, pieces):
        olds = [sums[n] for n in columns]
        for n, old, piece in zip(columns, olds, pieces, strict=True):
            sums[n] = old + piece

    def blocks(g, carry):
        made = []
        for u in range(COUPLE_UNROLL):
            n = g * COUPLE_UNROLL + u
            m = blocks_held[jnp.minimum(n, held - 1)]
            at = jnp.where(m < NB, m, NB + ((m - NB) // MOVERS) * SLOTS + (m - NB) % MOVERS)
            made.append(one_block(m, at, jnp.where(n < held, 1.0, 0.0)))
        for columns, pieces in made:
            add(columns, pieces)
        return carry

    lax.fori_loop(0, (held + COUPLE_UNROLL - 1) // COUPLE_UNROLL, blocks, 0)
    dep[...] = jnp.zeros_like(dep)
    for n in range(100):
        total = sums[n]
        total = total[0:4] + total[4:8]
        for f in range(4):
            dep[f, n // 10, n % 10 + 3, :] = total[f]
    gain[...] = 1.0 / (6.0 + screen[...])
    rest[...] = source[...] - 2.0 * solid[...]
    put_rims(dep, pres, gain, rest, jnp.logical_not(x_even), out_o)


P_AT = 14
G_AT = P_AT + 4
S_AT = G_AT + 3
D_TILES = S_AT + 3


def put_rims(dep, pres, gain, rest, up, out):
    first = jnp.where(up, 6, 0)
    rim = jnp.where(up, 9, 0)
    for r in range(4):
        out[2 * r] = dep[3, first + r, 0:8, :]
        out[2 * r + 1] = dep[3, first + r, 8:16, :]
    for c in range(3):
        out[8 + 2 * c] = dep[c, rim, 0:8, :]
        out[9 + 2 * c] = dep[c, rim, 8:16, :]
    for at, ref, count in ((P_AT, pres, 4), (G_AT, gain, 3), (S_AT, rest, 3)):
        start = jnp.where(up, 8 - count, 0)
        for r in range(count):
            out[at + r] = ref[start + r]


def pack_fe(dep, pres, gain, rest, out):
    put_rims(dep, pres, gain, rest, lax.axis_index("gx") % 2 == 0, out)


H_DRAG = 7
H_FIELDS = H_DRAG + 3
H_TILES = H_FIELDS + 24


def fold_x(dep, pres, gain, rest, in_o, in_e, after, load, drag, pres_w, gain_w, rest_w, out_e, out_o):
    even = lax.axis_index("gx") % 2 == 0

    def from_up(at):
        return jnp.where(even, in_e[at], in_o[at])

    def from_down(at):
        return jnp.where(even, in_o[at], in_e[at])

    def two(side, at):
        return jnp.concatenate([side(at), side(at + 1)], axis=0)

    for x in range(16):
        total = jnp.zeros((16, 128), F32)
        if 3 <= x <= 12:
            total = total + dep[3, x - 3]
        if 1 <= x <= 4:
            total = total + two(from_down, 2 * (x - 1))
        if 11 <= x <= 14:
            total = total + two(from_up, 2 * (x - 11))
        load[x] = total
    for c in range(3):
        drag[c] = dep[c, 1:9]
        drag[c, 0] += two(from_down, 8 + 2 * c)
        drag[c, 7] += two(from_up, 8 + 2 * c)
    for wide, ref, at, count in ((pres_w, pres, P_AT, 4), (gain_w, gain, G_AT, 3), (rest_w, rest, S_AT, 3)):
        wide[4:12] = ref[...]
        if count == 3:
            wide[0] = jnp.zeros((8, 128), F32)
            wide[15] = jnp.zeros((8, 128), F32)
        for r in range(count):
            wide[4 - count + r] = from_down(at + r)
            wide[12 + r] = from_up(at + r)
    parity = lax.axis_index("gy") % 2
    for out, up in ((out_e, parity == 0), (out_o, parity == 1)):
        for x in range(14):
            row = 4 * (x % 2)
            out[x // 2, row : row + 4, :] = jnp.where(up, load[x + 1, 9:13, :], load[x + 1, 3:7, :])
        for c in range(3):
            out[H_DRAG + c] = jnp.where(up, drag[c, :, 12, :], drag[c, :, 3, :])
        at = H_FIELDS
        for wide in (pres_w, gain_w, rest_w):
            for x in range(16):
                row = 4 * (x % 2)
                out[at + x // 2, row : row + 4, :] = jnp.where(up, wide[x, 4:8, :], wide[x, 0:4, :])
            at += 8


def finish(load, drag, pres_w, gain_w, rest_w, in_e, in_o, pressure, drag_sum, now, new, gain, off):
    even = lax.axis_index("gy") % 2 == 0

    def half(side_up, at, x):
        row = 4 * (x % 2)
        a = in_e[at + x // 2, row : row + 4, :]
        b = in_o[at + x // 2, row : row + 4, :]
        return jnp.where(even, a, b) if side_up else jnp.where(even, b, a)

    for c in range(3):
        drag_sum[c] = drag[c, :, 4:12, :]
        a = in_e[H_DRAG + c]
        b = in_o[H_DRAG + c]
        drag_sum[c, :, 0, :] += jnp.where(even, b, a)
        drag_sum[c, :, 7, :] += jnp.where(even, a, b)

    def rows(wide, n, x):
        at = H_FIELDS + 8 * n
        return jnp.concatenate([half(False, at, x), wide[x], half(True, at, x)], axis=0)

    for x in range(16):
        now[x] = rows(pres_w, 0, x)
    for x in range(1, 15):
        off[x] = load[x]
        off[x, 1:5, :] += half(False, 0, x - 1)
        off[x, 11:15, :] += half(True, 0, x - 1)
        g = rows(gain_w, 1, x)
        gain[x] = g
        off[x] = g * (rows(rest_w, 2, x) + 2.0 * off[x])
    lane = lax.broadcasted_iota(jnp.int32, (16, 128), 1)
    inner_low = lane > 0
    inner_high = lane < 127
    source, target = now, new
    for sweep in range(ITERS):
        for x in range(sweep + 1, 15 - sweep):
            p = source[x]
            near = source[x - 1] + source[x + 1]
            near = near + pltpu.roll(p, 1, 0) + pltpu.roll(p, 15, 0)
            near = near + jnp.where(inner_low, pltpu.roll(p, 1, 1), 0.0)
            near = near + jnp.where(inner_high, pltpu.roll(p, 127, 1), 0.0)
            target[x] = gain[x] * near + off[x]
        source, target = target, source
    pressure[...] = source[4:12, 4:12, :]


def head(v):
    return v.astype(BF16).astype(F32)

def preparers(left, near, right):
    row = lax.broadcasted_iota(jnp.int32, (8, 128), 0)
    first_four = row < 4
    space = row < 3
    bias = jnp.where(space, 1.5, 0.0)
    sign = jnp.where(row == 7, 1.0, jnp.where(first_four, 0.0, -1.0))
    turned_sign = jnp.where(space, -1.0, jnp.where(row == 3, 1.0, 0.0))
    last = jnp.where(row == 7, 1.0, 0.0)

    def left_of(tile, m):
        centred = tile - bias
        v = jnp.where(first_four, centred, pltpu.roll(centred * centred, 4, 0))
        h = head(v)
        rest = v - h
        mid = head(rest)
        low = rest - mid
        extra = jnp.where(space, 1.0, jnp.where(first_four, 0.0, low))
        shifted = jnp.where(first_four, 1.0, jnp.where(row == 7, 0.0, pltpu.roll(mid, 4, 0)))
        near[m] = jnp.concatenate([jnp.where(space, h, shifted), jnp.where(space, low, 0.0)], axis=0).astype(BF16)
        return [h, h, mid, extra]

    def right_of(tile, n):
        centred = tile - bias
        square = jnp.where(first_four, centred * centred, 0.0)
        t = jnp.broadcast_to(jnp.sum(square * turned_sign, axis=0, keepdims=True), (8, 128))
        r2 = jnp.broadcast_to(square[3:4], (8, 128))
        d = jnp.where(first_four, 2.0 * centred, sign)
        h = head(d)
        mid = head(d - h)

        def terms(v):
            a = head(v)
            b = head(v - a)
            return a, b, v - a - b

        ta, tb, tc = terms(t)
        ra, rb, rc = terms(r2)
        fourth = jnp.where(row == 0, ta, jnp.where(row == 1, tb, jnp.where(row == 2, tc, sign)))
        reach = jnp.where(row == 3, h, last)
        reach_mid = jnp.where(row == 3, mid, 0.0)
        fourth_reach = jnp.where(row == 0, ra, jnp.where(row == 1, rb, jnp.where(row == 2, rc, last)))
        right[n, :, 0:128] = jnp.concatenate([h, mid, h, fourth], axis=0).astype(BF16)
        right[n, :, 128:256] = jnp.concatenate([reach, reach_mid, reach, fourth_reach], axis=0).astype(BF16)

    def four(tiles, m):
        rows = []
        for b, tile in enumerate(tiles):
            rows += left_of(tile, m + b)
        left[m // 4] = jnp.concatenate(rows, axis=0).astype(BF16).T

    return four, right_of


def lister(pairs, total, chosen, from_x):
    def along_x(m):
        return (m >= NB) & (m < NB + 2 * SLOTS)

    def look(first, count, size):
        for v in range(size):
            t = first + v
            needs = along_x(pairs[0, t]) | along_x(pairs[1, t])
            wanted = needs if from_x else jnp.logical_not(needs)
            chosen[count] = t
            count = count + jnp.where(wanted & (t < total), 1, 0)
        return count

    return look


def run_tiles(pairs, chosen, count, left, near, right, sums, begin, end):
    def tile(n):
        t = chosen[jnp.minimum(n, count - 1)]
        i = pairs[0, t]
        j = pairs[1, t]
        q = i - NB
        i = jnp.where(i < NB, i, NB + (q // SLOTS) * MOVERS + q % SLOTS)
        mine = right[i]
        place = j % 4
        none = jnp.zeros_like(mine)
        weights = jnp.concatenate([jnp.where(place == k, mine, none) for k in range(4)], axis=0)
        both = jnp.dot(left[j // 4], weights, preferred_element_type=F32)
        overlap = jnp.maximum(both[:, :128], 0.0)
        reach = both[:, 128:]
        guess = pl.reciprocal(reach, approx=True)
        weight = overlap * (guess * (2.0 - reach * guess))
        upper = weight.astype(BF16)
        lower = (weight - upper.astype(F32)).astype(BF16)
        a = near[j]
        got = jnp.dot(a, upper, preferred_element_type=F32) + jnp.dot(a, lower, preferred_element_type=F32)
        got = got[0:8] + pltpu.roll(got[0:8], 4, 0) + got[8:16]
        return i, got * jnp.where(n < count, 1.0, 0.0)

    def step(g, carry):
        made = [tile(begin + g * CONTACT_UNROLL + u) for u in range(CONTACT_UNROLL)]
        for i, got in made:
            sums[i] += got
        return carry

    lax.fori_loop(0, jnp.maximum(end - begin + CONTACT_UNROLL - 1, 0) // CONTACT_UNROLL, step, 0)


def prepare_received(four, right_of, d, even, first, second, look, at, part, count):
    for u in range(MOVERS // 4):
        tiles = [jnp.where(even, first[4 * u + b], second[4 * u + b]) for b in range(4)]
        four(tiles, NB + d * SLOTS + 4 * u)
        for b in range(4):
            right_of(tiles[b], NB + d * MOVERS + 4 * u + b)
    count = look(at, count, part)

    def others(k, count):
        for u in range(2):
            s = MOVERS + 8 * k + 4 * u
            tiles = [jnp.where(even, first[s + b], second[s + b]) for b in range(4)]
            four(tiles, NB + d * SLOTS + s)
            four([pltpu.roll(tile, 4, 0) for tile in tiles], NB + d * SLOTS + s + PAIRS)
        return look(at + (1 + k) * part, count, part)

    return lax.fori_loop(0, PAIRS // 8, others, count)


def contact_near(pairs, total_ref, parts, in_ye, in_yo, after, left, near, right, sums, chosen):
    total = total_ref[0, 0]
    sums[...] = jnp.zeros_like(sums)
    four, right_of = preparers(left, near, right)
    look = lister(pairs, total, chosen, False)
    groups = NB // 4 // PREPARE
    part = MAXT // 2 // groups

    def own(k, count):
        for u in range(PREPARE):
            m = 4 * (k * PREPARE + u)
            tiles = [parts[m + b] for b in range(4)]
            four(tiles, m)
            for b in range(4):
                right_of(tiles[b], m + b)
        return look(k * part, count, part)

    count = lax.fori_loop(0, groups, own, jnp.int32(0))
    y_even = lax.axis_index("gy") % 2 == 0
    for d, first, second in ((2, in_yo, in_ye), (3, in_ye, in_yo)):
        at = MAXT // 2 + (d - 2) * (MAXT // 4)
        count = prepare_received(four, right_of, d, y_even, first, second, look, at, MAXT // 16, count)
    run_tiles(pairs, chosen, count, left, near, right, sums, 0, count)


def received(in_xe, in_xo, in_ye, in_yo):
    x_even = lax.axis_index("gx") % 2 == 0
    y_even = lax.axis_index("gy") % 2 == 0
    return ((x_even, in_xo, in_xe), (x_even, in_xe, in_xo), (y_even, in_yo, in_ye), (y_even, in_ye, in_yo))


def contact_more(
    pairs, total_ref, in_xo, in_xe, after, left_in, near_in, right_in, sums_in,
    left, near, right, sums, chosen,
):
    total = total_ref[0, 0]
    for made, kept, size, skip in ((left, left_in, 4, 2 * SLOTS), (near, near_in, 1, 2 * SLOTS)):
        made[0 : NB // size] = kept[0 : NB // size]
        made[(NB + skip) // size :] = kept[(NB + skip) // size :]
    right[0:NB] = right_in[0:NB]
    right[NB + 2 * MOVERS :] = right_in[NB + 2 * MOVERS :]
    sums[...] = sums_in[...]
    four, right_of = preparers(left, near, right)
    look = lister(pairs, total, chosen, True)
    x_even = lax.axis_index("gx") % 2 == 0
    count = jnp.int32(0)
    for d, first, second in ((0, in_xo, in_xe), (1, in_xe, in_xo)):
        count = prepare_received(
            four, right_of, d, x_even, first, second, look, d * (MAXT // 2), MAXT // 8, count
        )
    chosen[LAST] = count
    run_tiles(pairs, chosen, count, left, near, right, sums, 0, jnp.minimum(EARLY, count))


def contact_end(
    pairs, parts, in_xo, in_xe, in_ye, in_yo, drag, after, left, near, right, chosen, sums_in, force, sums
):
    sums[...] = sums_in[...]
    count = chosen[LAST]
    run_tiles(pairs, chosen, count, left, near, right, sums, EARLY, count)

    def put(n, at, position):
        for c in range(3):
            x = position(c) - 1.5
            w = sums[8 * n : 8 * n + 8, 3, :]
            y = sums[8 * n : 8 * n + 8, c, :]
            force[c, at : at + 8, :] = drag[c, at : at + 8, :] + 0.5 * (x * w - y)

    for n in range(NB // 8):
        put(n, 8 * n, lambda c, n=n: parts[8 * n : 8 * n + 8, c, :])
    for d, (even, first, second) in enumerate(received(in_xe, in_xo, in_ye, in_yo)):
        for k in range(2):
            put(
                NB // 8 + 2 * d + k,
                NB + d * SLOTS + 8 * k,
                lambda c, k=k, even=even, first=first, second=second: jnp.where(
                    even, first[8 * k : 8 * k + 8, c, :], second[8 * k : 8 * k + 8, c, :]
                ),
            )
        for c in range(3):
            force[c, NB + d * SLOTS + MOVERS : NB + (d + 1) * SLOTS, :] = jnp.zeros((SLOTS - MOVERS, 128), F32)


def pairs_of(first, count, last):
    up = [(i, i + 1) for i in range(first, last, 2)]
    return up + [(b, a) for a, b in up]


def swap(array, axis, first):
    count = lax.axis_size(axis)
    return lax.ppermute(array, axis, pairs_of(first, count, count - 1))


def body(
    particles,
    send_list,
    move_count,
    tile_pairs,
    tile_count,
    drag_tiles,
    cell_slot,
    fluid_velocity,
    pressure_init,
    source,
    solid_old,
    screening,
):
    parts = particles[0, 0]
    sends = send_list[0, 0]
    moves = move_count[0, 0]
    tiles = drag_tiles[0, 0].T
    pairs = tile_pairs[0, 0].T
    slots = cell_slot[0, 0]
    cells = (8, 8, 128)
    ye, yo = call(pack_y, (shape(Y_TILES, 8, 128), shape(Y_TILES, 8, 128)), [VM, SM, VM])(parts, sends, fluid_velocity)
    got_ye = swap(ye, "gy", 0)
    got_yo = swap(yo, "gy", 1)
    xe, flow_x = call(pack_first, (shape(X_TILES, 8, 128), shape(3, 8, 16, 128)), [VM, SM, VM, VM, VM])(
        parts, sends, fluid_velocity, got_ye, got_yo
    )
    got_xe = swap(xe, "gx", 0)
    xo = call(pack_second, shape(X_TILES, 8, 128), [VM, SM, VM])(parts, sends, flow_x)
    got_xo = swap(xo, "gx", 1)
    operands = (
        jax.ShapeDtypeStruct((POOL // 4, 128, 128), BF16),
        jax.ShapeDtypeStruct((POOL, 16, 128), BF16),
        jax.ShapeDtypeStruct((OWNABLE, 32, 256), BF16),
        shape(OWNABLE, 8, 128),
    )
    prepared = call(
        contact_near, operands, [SM, SM] + [VM] * 4, [pltpu.SMEM((LIST,), jnp.int32)], flops=10**8
    )(pairs, tile_count, parts, got_ye, got_yo, xo)
    drag, dep, fo, gain, rest = call(
        couple,
        (shape(3, 384, 128), shape(4, 10, 16, 128), shape(D_TILES, 8, 128), shape(*cells), shape(*cells)),
        [VM, HB, HB, HB] + [VM] * 11,
        [
            pltpu.VMEM((OWNABLE, 8, 128), F32),
            pltpu.VMEM((100, 8, 128), F32),
            pltpu.VMEM((100, 8, 128), F32),
            pltpu.SMEM((OWNABLE,), F32),
            pltpu.SMEM((OWNABLE + 1,), jnp.int32),
            pltpu.SMEM((4, SLOTS), jnp.int32),
            pltpu.SMEM((2, 4), jnp.int32),
            pltpu.SMEM((4, 384), jnp.int32),
            pltpu.SemaphoreType.DMA((3,)),
        ],
    )(
        parts, sends, moves, tiles, slots, flow_x, got_xo, got_xe, got_ye, got_yo, prepared[3],
        pressure_init, screening, source, solid_old,
    )
    got_fo = swap(fo, "gx", 1)
    fe = call(pack_fe, shape(D_TILES, 8, 128), [VM] * 4)(dep, pressure_init, gain, rest)
    got_fe = swap(fe, "gx", 0)
    *more, chosen = call(
        contact_more,
        (*operands, jax.ShapeDtypeStruct((LIST,), jnp.int32)),
        [SM, SM] + [VM] * 7,
        flops=10**8,
    )(pairs, tile_count, got_xo, got_xe, fe, *prepared)
    load, drag_x, pres_w, gain_w, rest_w, he, ho = call(
        fold_x,
        (
            shape(16, 16, 128), shape(3, 8, 16, 128), shape(16, 8, 128), shape(16, 8, 128), shape(16, 8, 128),
            shape(H_TILES, 8, 128), shape(H_TILES, 8, 128),
        ),
        [VM] * 7,
    )(dep, pressure_init, gain, rest, got_fo, got_fe, more[3])
    got_he = swap(he, "gy", 0)
    got_ho = swap(ho, "gy", 1)
    force = call(
        contact_end,
        shape(3, 384, 128),
        [SM] + [VM] * 10 + [SM, VM],
        [pltpu.VMEM((OWNABLE, 8, 128), F32)],
        flops=10**9,
    )(pairs, parts, got_xo, got_xe, got_ye, got_yo, drag, ho, *more[:3], chosen, more[3])
    pressure, drag_sum = call(
        finish,
        (shape(*cells), shape(3, *cells)),
        [VM] * 7,
        [pltpu.VMEM((16, 16, 128), F32)] * 4,
    )(load, drag_x, pres_w, gain_w, rest_w, got_he, got_ho)
    return (pressure, drag_sum, force.transpose(1, 0, 2)[None, None])


def solution(mesh):
    in_specs = (
        P("gx", "gy", None, None, None),
        P("gx", "gy", None, None),
        P("gx", "gy", None, None),
        P("gx", "gy", None, None),
        P("gx", "gy"),
        P("gx", "gy", None, None),
        P("gx", "gy", None, None),
        P(None, "gx", "gy", None),
        P("gx", "gy", None),
        P("gx", "gy", None),
        P("gx", "gy", None),
        P("gx", "gy", None),
    )
    out_specs = (P("gx", "gy", None), P(None, "gx", "gy", None), P("gx", "gy", None, None, None))
    return jax.shard_map(body, mesh=mesh, in_specs=in_specs, out_specs=out_specs, check_vma=False)
```

```python
import functools

import jax
import jax.numpy as jnp
from jax import lax
from jax.experimental import pallas as pl
from jax.experimental.pallas import tpu as pltpu
from jax.sharding import PartitionSpec as P

F32 = jnp.float32
BF16 = jnp.bfloat16
NB = 128
SLOTS = 64
MOVERS = 16
PAIRS = (SLOTS - MOVERS) // 2
GROUP = MOVERS + PAIRS
OWNABLE = NB + 4 * MOVERS
POOL = 384
MAXT = 512
ITERS = 4
CONTACT_UNROLL = 32
EARLY = 128
LIST = 640
LAST = LIST - 1
PREPARE = 4
COUPLE_UNROLL = 32

VM = pl.BlockSpec(memory_space=pltpu.VMEM)
SM = pl.BlockSpec(memory_space=pltpu.SMEM)
HB = pl.BlockSpec(memory_space=pltpu.HBM)
PARAMS = pltpu.CompilerParams(vmem_limit_bytes=32 * 2**20)


def shape(*dims):
    return jax.ShapeDtypeStruct(dims, F32)


def call(kernel, outs, in_specs, scratch=(), flops=10**6, moved=10**6):
    return pl.pallas_call(
        kernel,
        out_shape=outs,
        in_specs=in_specs,
        out_specs=jax.tree.map(lambda o: SM if len(o.shape) == 1 else VM, outs),
        scratch_shapes=list(scratch),
        compiler_params=PARAMS,
        cost_estimate=pl.CostEstimate(flops=flops, bytes_accessed=moved, transcendentals=0),
    )


def put_blocks(parts, sends, direction, out):
    for s in range(MOVERS):
        out[s] = parts[sends[direction, s]]
    for k in range(PAIRS):
        out[MOVERS + k, 0:4, :] = parts[sends[direction, MOVERS + k], 0:4, :]
        out[MOVERS + k, 4:8, :] = parts[sends[direction, MOVERS + PAIRS + k], 0:4, :]


def fetch(sources, targets, sems):
    copies = [pltpu.make_async_copy(a, b, sems.at[n]) for n, (a, b) in enumerate(zip(sources, targets, strict=True))]
    for copy in copies:
        copy.start()
    return copies


Y_TILES = GROUP + 3
X_TILES = GROUP + 6


def pack_y(parts, sends, flow, out_e, out_o):
    parity = lax.axis_index("gy") % 2
    for out, up in ((out_e, parity == 0), (out_o, parity == 1)):
        put_blocks(parts, sends, jnp.where(up, 2, 3), out)
        for c in range(3):
            out[GROUP + c] = jnp.where(up, flow[c, :, 7, :], flow[c, :, 0, :])


def put_flow(flow_x, up, out):
    edge = jnp.where(up, 7, 0)
    for c in range(3):
        out[GROUP + 2 * c] = flow_x[c, edge, 0:8, :]
        out[GROUP + 2 * c + 1] = flow_x[c, edge, 8:16, :]


def pack_first(parts, sends, flow, in_e, in_o, out, flow_x):
    even = lax.axis_index("gy") % 2 == 0
    for c in range(3):
        flow_x[c, :, 4:12, :] = flow[c]
        a = in_e[GROUP + c]
        b = in_o[GROUP + c]
        flow_x[c, :, 12, :] = jnp.where(even, a, b)
        flow_x[c, :, 3, :] = jnp.where(even, b, a)
    up = lax.axis_index("gx") % 2 == 0
    put_blocks(parts, sends, jnp.where(up, 0, 1), out)
    put_flow(flow_x, up, out)


def pack_second(parts, sends, flow_x, out):
    up = lax.axis_index("gx") % 2 == 1
    put_blocks(parts, sends, jnp.where(up, 0, 1), out)
    put_flow(flow_x, up, out)


def couple(
    parts, sends_in, moves_in, tiles_in, slots, flow_x, in_xo, in_xe, in_ye, in_yo, after,
    pres, screen, source, solid,
    drag, dep, out_o, gain, rest,
    pool, table, sums, owned, blocks_held, sends, moves, tiles, sems,
):
    copies = fetch((sends_in, moves_in, tiles_in), (sends, moves, tiles), sems)
    for k in range(NB):
        owned[k] = 1.0
    x_even = lax.axis_index("gx") % 2 == 0
    y_even = lax.axis_index("gy") % 2 == 0
    pool[0:NB] = parts[...]
    for d, (up, even, a, b) in enumerate(
        ((0, x_even, in_xe, in_xo), (1, x_even, in_xe, in_xo), (0, y_even, in_ye, in_yo), (1, y_even, in_ye, in_yo))
    ):
        first, second = (b, a) if up == 0 else (a, b)
        pool[NB + d * MOVERS : NB + (d + 1) * MOVERS] = jnp.where(even, first[0:MOVERS], second[0:MOVERS])

    for c in range(3):
        high = jnp.where(x_even, in_xe[GROUP + 2 * c], in_xo[GROUP + 2 * c])
        high2 = jnp.where(x_even, in_xe[GROUP + 2 * c + 1], in_xo[GROUP + 2 * c + 1])
        low = jnp.where(x_even, in_xo[GROUP + 2 * c], in_xe[GROUP + 2 * c])
        low2 = jnp.where(x_even, in_xo[GROUP + 2 * c + 1], in_xe[GROUP + 2 * c + 1])
        for x in range(10):
            if x == 0:
                one, two = low, low2
            elif x == 9:
                one, two = high, high2
            else:
                one, two = flow_x[c, x - 1, 0:8, :], flow_x[c, x - 1, 8:16, :]
            table[x * 10 : x * 10 + 5, 4 + c, :] = one[3:8]
            table[x * 10 + 5 : x * 10 + 10, 4 + c, :] = two[0:5]
    sums[...] = jnp.zeros_like(sums)
    drag[...] = jnp.zeros_like(drag)
    for copy in copies:
        copy.wait()

    for d in range(4):

        def leave(s, carry, d=d):
            owned[sends[d, s]] = 0.0
            return carry

        lax.fori_loop(0, moves[0, d], leave, 0)
        for s in range(MOVERS):
            owned[NB + d * MOVERS + s] = jnp.where(s < moves[1, d], 1.0, 0.0)
    held = jnp.int32(0)
    for m in range(OWNABLE):
        blocks_held[held] = m
        held = held + jnp.where(owned[m] > 0.5, 1, 0)

    row = lax.broadcasted_iota(jnp.int32, (8, NB), 0)
    low_rows = row < 4
    last_row = row == 7
    half = jnp.where(low_rows, 0, 1)
    depth_rows = lax.broadcasted_iota(jnp.int32, (128, NB), 0)

    def one_block(m, at, counts):
        state = pool[m]
        code = jnp.broadcast_to(slots[pl.ds(at, 1), :], (8, NB))
        depth = code & 127
        slot = code >> 7
        columns = [tiles[k, at] for k in range(4)]
        seen = [jnp.take_along_axis(table[n], depth, axis=1, mode="promise_in_bounds") for n in columns]
        at_particle = jnp.where(
            slot < 2, jnp.where(slot == 0, seen[0], seen[1]), jnp.where(slot == 2, seen[2], seen[3])
        )
        coeff = jnp.broadcast_to(state[7:8], (8, NB))
        radius = jnp.broadcast_to(state[3:4], (8, NB))
        values = jnp.where(last_row, radius * radius * radius, coeff * (at_particle - state))
        both = jnp.where(low_rows, pltpu.roll(values, 4, 0), values)
        for c in range(3):
            drag[c, pl.ds(at, 1), :] = both[c : c + 1]
        first = jnp.where(slot == half, both, 0.0)
        second = jnp.where(slot == half + 2, both, 0.0)
        sixteen = jnp.concatenate([first, second], axis=0)
        upper = sixteen.astype(BF16)
        lower = (sixteen - upper.astype(F32)).astype(BF16)
        pick = (depth_rows == jnp.broadcast_to(depth[0:1], (128, NB))).astype(BF16)
        spread = lax.dot_general(
            jnp.concatenate([upper, lower], axis=0), pick, (((1,), (1,)), ((), ())),
            preferred_element_type=F32,
        )
        spread = (spread[0:16] + spread[16:32]) * counts
        parts_ = (
            jnp.where(low_rows, spread[0:8], 0.0), jnp.where(low_rows, 0.0, spread[0:8]),
            jnp.where(low_rows, spread[8:16], 0.0), jnp.where(low_rows, 0.0, spread[8:16]),
        )
        return columns, parts_

    def add(columns, pieces):
        olds = [sums[n] for n in columns]
        for n, old, piece in zip(columns, olds, pieces, strict=True):
            sums[n] = old + piece

    def blocks(g, carry):
        made = []
        for u in range(COUPLE_UNROLL):
            n = g * COUPLE_UNROLL + u
            m = blocks_held[jnp.minimum(n, held - 1)]
            at = jnp.where(m < NB, m, NB + ((m - NB) // MOVERS) * SLOTS + (m - NB) % MOVERS)
            made.append(one_block(m, at, jnp.where(n < held, 1.0, 0.0)))
        for columns, pieces in made:
            add(columns, pieces)
        return carry

    lax.fori_loop(0, (held + COUPLE_UNROLL - 1) // COUPLE_UNROLL, blocks, 0)
    dep[...] = jnp.zeros_like(dep)
    for n in range(100):
        total = sums[n]
        total = total[0:4] + total[4:8]
        for f in range(4):
            dep[f, n // 10, n % 10 + 3, :] = total[f]
    gain[...] = 1.0 / (6.0 + screen[...])
    rest[...] = source[...] - 2.0 * solid[...]
    put_rims(dep, pres, gain, rest, jnp.logical_not(x_even), out_o)


P_AT = 14
G_AT = P_AT + 4
S_AT = G_AT + 3
D_TILES = S_AT + 3


def put_rims(dep, pres, gain, rest, up, out):
    first = jnp.where(up, 6, 0)
    rim = jnp.where(up, 9, 0)
    for r in range(4):
        out[2 * r] = dep[3, first + r, 0:8, :]
        out[2 * r + 1] = dep[3, first + r, 8:16, :]
    for c in range(3):
        out[8 + 2 * c] = dep[c, rim, 0:8, :]
        out[9 + 2 * c] = dep[c, rim, 8:16, :]
    for at, ref, count in ((P_AT, pres, 4), (G_AT, gain, 3), (S_AT, rest, 3)):
        start = jnp.where(up, 8 - count, 0)
        for r in range(count):
            out[at + r] = ref[start + r]


def pack_fe(dep, pres, gain, rest, out):
    put_rims(dep, pres, gain, rest, lax.axis_index("gx") % 2 == 0, out)


H_DRAG = 7
H_FIELDS = H_DRAG + 3
H_TILES = H_FIELDS + 24


def fold_x(dep, pres, gain, rest, in_o, in_e, after, load, drag, pres_w, gain_w, rest_w, out_e, out_o):
    even = lax.axis_index("gx") % 2 == 0

    def from_up(at):
        return jnp.where(even, in_e[at], in_o[at])

    def from_down(at):
        return jnp.where(even, in_o[at], in_e[at])

    def two(side, at):
        return jnp.concatenate([side(at), side(at + 1)], axis=0)

    for x in range(16):
        total = jnp.zeros((16, 128), F32)
        if 3 <= x <= 12:
            total = total + dep[3, x - 3]
        if 1 <= x <= 4:
            total = total + two(from_down, 2 * (x - 1))
        if 11 <= x <= 14:
            total = total + two(from_up, 2 * (x - 11))
        load[x] = total
    for c in range(3):
        drag[c] = dep[c, 1:9]
        drag[c, 0] += two(from_down, 8 + 2 * c)
        drag[c, 7] += two(from_up, 8 + 2 * c)
    for wide, ref, at, count in ((pres_w, pres, P_AT, 4), (gain_w, gain, G_AT, 3), (rest_w, rest, S_AT, 3)):
        wide[4:12] = ref[...]
        if count == 3:
            wide[0] = jnp.zeros((8, 128), F32)
            wide[15] = jnp.zeros((8, 128), F32)
        for r in range(count):
            wide[4 - count + r] = from_down(at + r)
            wide[12 + r] = from_up(at + r)
    parity = lax.axis_index("gy") % 2
    for out, up in ((out_e, parity == 0), (out_o, parity == 1)):
        for x in range(14):
            row = 4 * (x % 2)
            out[x // 2, row : row + 4, :] = jnp.where(up, load[x + 1, 9:13, :], load[x + 1, 3:7, :])
        for c in range(3):
            out[H_DRAG + c] = jnp.where(up, drag[c, :, 12, :], drag[c, :, 3, :])
        at = H_FIELDS
        for wide in (pres_w, gain_w, rest_w):
            for x in range(16):
                row = 4 * (x % 2)
                out[at + x // 2, row : row + 4, :] = jnp.where(up, wide[x, 4:8, :], wide[x, 0:4, :])
            at += 8


def finish(load, drag, pres_w, gain_w, rest_w, in_e, in_o, pressure, drag_sum, now, new, gain, off):
    even = lax.axis_index("gy") % 2 == 0

    def half(side_up, at, x):
        row = 4 * (x % 2)
        a = in_e[at + x // 2, row : row + 4, :]
        b = in_o[at + x // 2, row : row + 4, :]
        return jnp.where(even, a, b) if side_up else jnp.where(even, b, a)

    for c in range(3):
        drag_sum[c] = drag[c, :, 4:12, :]
        a = in_e[H_DRAG + c]
        b = in_o[H_DRAG + c]
        drag_sum[c, :, 0, :] += jnp.where(even, b, a)
        drag_sum[c, :, 7, :] += jnp.where(even, a, b)

    def rows(wide, n, x):
        at = H_FIELDS + 8 * n
        return jnp.concatenate([half(False, at, x), wide[x], half(True, at, x)], axis=0)

    for x in range(16):
        now[x] = rows(pres_w, 0, x)
    for x in range(1, 15):
        off[x] = load[x]
        off[x, 1:5, :] += half(False, 0, x - 1)
        off[x, 11:15, :] += half(True, 0, x - 1)
        g = rows(gain_w, 1, x)
        gain[x] = g
        off[x] = g * (rows(rest_w, 2, x) + 2.0 * off[x])
    lane = lax.broadcasted_iota(jnp.int32, (16, 128), 1)
    inner_low = lane > 0
    inner_high = lane < 127
    source, target = now, new
    for sweep in range(ITERS):
        for x in range(sweep + 1, 15 - sweep):
            p = source[x]
            near = source[x - 1] + source[x + 1]
            near = near + pltpu.roll(p, 1, 0) + pltpu.roll(p, 15, 0)
            near = near + jnp.where(inner_low, pltpu.roll(p, 1, 1), 0.0)
            near = near + jnp.where(inner_high, pltpu.roll(p, 127, 1), 0.0)
            target[x] = gain[x] * near + off[x]
        source, target = target, source
    pressure[...] = source[4:12, 4:12, :]


def head(v):
    return v.astype(BF16).astype(F32)

def preparers(left, near, right):
    row = lax.broadcasted_iota(jnp.int32, (8, 128), 0)
    first_four = row < 4
    space = row < 3
    bias = jnp.where(space, 1.5, 0.0)
    sign = jnp.where(row == 7, 1.0, jnp.where(first_four, 0.0, -1.0))
    turned_sign = jnp.where(space, -1.0, jnp.where(row == 3, 1.0, 0.0))
    last = jnp.where(row == 7, 1.0, 0.0)

    def left_of(tile, m):
        centred = tile - bias
        v = jnp.where(first_four, centred, pltpu.roll(centred * centred, 4, 0))
        h = head(v)
        rest = v - h
        mid = head(rest)
        low = rest - mid
        extra = jnp.where(space, 1.0, jnp.where(first_four, 0.0, low))
        shifted = jnp.where(first_four, 1.0, jnp.where(row == 7, 0.0, pltpu.roll(mid, 4, 0)))
        near[m] = jnp.concatenate([jnp.where(space, h, shifted), jnp.where(space, low, 0.0)], axis=0).astype(BF16)
        return [h, h, mid, extra]

    def right_of(tile, n):
        centred = tile - bias
        square = jnp.where(first_four, centred * centred, 0.0)
        t = jnp.broadcast_to(jnp.sum(square * turned_sign, axis=0, keepdims=True), (8, 128))
        r2 = jnp.broadcast_to(square[3:4], (8, 128))
        d = jnp.where(first_four, 2.0 * centred, sign)
        h = head(d)
        mid = head(d - h)

        def terms(v):
            a = head(v)
            b = head(v - a)
            return a, b, v - a - b

        ta, tb, tc = terms(t)
        ra, rb, rc = terms(r2)
        fourth = jnp.where(row == 0, ta, jnp.where(row == 1, tb, jnp.where(row == 2, tc, sign)))
        reach = jnp.where(row == 3, h, last)
        reach_mid = jnp.where(row == 3, mid, 0.0)
        fourth_reach = jnp.where(row == 0, ra, jnp.where(row == 1, rb, jnp.where(row == 2, rc, last)))
        right[n, :, 0:128] = jnp.concatenate([h, mid, h, fourth], axis=0).astype(BF16)
        right[n, :, 128:256] = jnp.concatenate([reach, reach_mid, reach, fourth_reach], axis=0).astype(BF16)

    def four(tiles, m):
        rows = []
        for b, tile in enumerate(tiles):
            rows += left_of(tile, m + b)
        left[m // 4] = jnp.concatenate(rows, axis=0).astype(BF16).T

    return four, right_of


def lister(pairs, total, chosen, from_x):
    def along_x(m):
        return (m >= NB) & (m < NB + 2 * SLOTS)

    def look(first, count, size):
        for v in range(size):
            t = first + v
            needs = along_x(pairs[0, t]) | along_x(pairs[1, t])
            wanted = needs if from_x else jnp.logical_not(needs)
            chosen[count] = t
            count = count + jnp.where(wanted & (t < total), 1, 0)
        return count

    return look


def run_tiles(pairs, chosen, count, left, near, right, sums, begin, end):
    def tile(n):
        t = chosen[jnp.minimum(n, count - 1)]
        i = pairs[0, t]
        j = pairs[1, t]
        q = i - NB
        i = jnp.where(i < NB, i, NB + (q // SLOTS) * MOVERS + q % SLOTS)
        mine = right[i]
        place = j % 4
        none = jnp.zeros_like(mine)
        weights = jnp.concatenate([jnp.where(place == k, mine, none) for k in range(4)], axis=0)
        both = jnp.dot(left[j // 4], weights, preferred_element_type=F32)
        overlap = jnp.maximum(both[:, :128], 0.0)
        reach = both[:, 128:]
        guess = pl.reciprocal(reach, approx=True)
        weight = overlap * (guess * (2.0 - reach * guess))
        upper = weight.astype(BF16)
        lower = (weight - upper.astype(F32)).astype(BF16)
        a = near[j]
        got = jnp.dot(a, upper, preferred_element_type=F32) + jnp.dot(a, lower, preferred_element_type=F32)
        got = got[0:8] + pltpu.roll(got[0:8], 4, 0) + got[8:16]
        return i, got * jnp.where(n < count, 1.0, 0.0)

    def step(g, carry):
        made = [tile(begin + g * CONTACT_UNROLL + u) for u in range(CONTACT_UNROLL)]
        for i, got in made:
            sums[i] += got
        return carry

    lax.fori_loop(0, jnp.maximum(end - begin + CONTACT_UNROLL - 1, 0) // CONTACT_UNROLL, step, 0)


def prepare_received(four, right_of, d, even, first, second, look, at, part, count):
    for u in range(MOVERS // 4):
        tiles = [jnp.where(even, first[4 * u + b], second[4 * u + b]) for b in range(4)]
        four(tiles, NB + d * SLOTS + 4 * u)
        for b in range(4):
            right_of(tiles[b], NB + d * MOVERS + 4 * u + b)
    count = look(at, count, part)

    def others(k, count):
        for u in range(2):
            s = MOVERS + 8 * k + 4 * u
            tiles = [jnp.where(even, first[s + b], second[s + b]) for b in range(4)]
            four(tiles, NB + d * SLOTS + s)
            four([pltpu.roll(tile, 4, 0) for tile in tiles], NB + d * SLOTS + s + PAIRS)
        return look(at + (1 + k) * part, count, part)

    return lax.fori_loop(0, PAIRS // 8, others, count)


def contact_near(pairs, total_ref, parts, in_ye, in_yo, after, left, near, right, sums, chosen):
    total = total_ref[0, 0]
    sums[...] = jnp.zeros_like(sums)
    four, right_of = preparers(left, near, right)
    look = lister(pairs, total, chosen, False)
    groups = NB // 4 // PREPARE
    part = MAXT // 2 // groups

    def own(k, count):
        for u in range(PREPARE):
            m = 4 * (k * PREPARE + u)
            tiles = [parts[m + b] for b in range(4)]
            four(tiles, m)
            for b in range(4):
                right_of(tiles[b], m + b)
        return look(k * part, count, part)

    count = lax.fori_loop(0, groups, own, jnp.int32(0))
    y_even = lax.axis_index("gy") % 2 == 0
    for d, first, second in ((2, in_yo, in_ye), (3, in_ye, in_yo)):
        at = MAXT // 2 + (d - 2) * (MAXT // 4)
        count = prepare_received(four, right_of, d, y_even, first, second, look, at, MAXT // 16, count)
    run_tiles(pairs, chosen, count, left, near, right, sums, 0, count)


def received(in_xe, in_xo, in_ye, in_yo):
    x_even = lax.axis_index("gx") % 2 == 0
    y_even = lax.axis_index("gy") % 2 == 0
    return ((x_even, in_xo, in_xe), (x_even, in_xe, in_xo), (y_even, in_yo, in_ye), (y_even, in_ye, in_yo))


def contact_more(
    pairs, total_ref, in_xo, in_xe, after, left_in, near_in, right_in, sums_in,
    left, near, right, sums, chosen,
):
    total = total_ref[0, 0]
    for made, kept, size, skip in ((left, left_in, 4, 2 * SLOTS), (near, near_in, 1, 2 * SLOTS)):
        made[0 : NB // size] = kept[0 : NB // size]
        made[(NB + skip) // size :] = kept[(NB + skip) // size :]
    right[0:NB] = right_in[0:NB]
    right[NB + 2 * MOVERS :] = right_in[NB + 2 * MOVERS :]
    sums[...] = sums_in[...]
    four, right_of = preparers(left, near, right)
    look = lister(pairs, total, chosen, True)
    x_even = lax.axis_index("gx") % 2 == 0
    count = jnp.int32(0)
    for d, first, second in ((0, in_xo, in_xe), (1, in_xe, in_xo)):
        count = prepare_received(
            four, right_of, d, x_even, first, second, look, d * (MAXT // 2), MAXT // 8, count
        )
    chosen[LAST] = count
    run_tiles(pairs, chosen, count, left, near, right, sums, 0, jnp.minimum(EARLY, count))


def contact_end(
    pairs, parts, in_xo, in_xe, in_ye, in_yo, drag, after, left, near, right, chosen, sums_in, force, sums
):
    sums[...] = sums_in[...]
    count = chosen[LAST]
    run_tiles(pairs, chosen, count, left, near, right, sums, EARLY, count)

    def put(n, at, position):
        for c in range(3):
            x = position(c) - 1.5
            w = sums[8 * n : 8 * n + 8, 3, :]
            y = sums[8 * n : 8 * n + 8, c, :]
            force[c, at : at + 8, :] = drag[c, at : at + 8, :] + 0.5 * (x * w - y)

    for n in range(NB // 8):
        put(n, 8 * n, lambda c, n=n: parts[8 * n : 8 * n + 8, c, :])
    for d, (even, first, second) in enumerate(received(in_xe, in_xo, in_ye, in_yo)):
        for k in range(2):
            put(
                NB // 8 + 2 * d + k,
                NB + d * SLOTS + 8 * k,
                lambda c, k=k, even=even, first=first, second=second: jnp.where(
                    even, first[8 * k : 8 * k + 8, c, :], second[8 * k : 8 * k + 8, c, :]
                ),
            )
        for c in range(3):
            force[c, NB + d * SLOTS + MOVERS : NB + (d + 1) * SLOTS, :] = jnp.zeros((SLOTS - MOVERS, 128), F32)


def pairs_of(first, count, last):
    up = [(i, i + 1) for i in range(first, last, 2)]
    return up + [(b, a) for a, b in up]


def swap(array, axis, first):
    count = lax.axis_size(axis)
    return lax.ppermute(array, axis, pairs_of(first, count, count - 1))


def body(
    particles,
    send_list,
    move_count,
    tile_pairs,
    tile_count,
    drag_tiles,
    cell_slot,
    fluid_velocity,
    pressure_init,
    source,
    solid_old,
    screening,
):
    parts = particles[0, 0]
    sends = send_list[0, 0]
    moves = move_count[0, 0]
    tiles = drag_tiles[0, 0].T
    pairs = tile_pairs[0, 0].T
    slots = cell_slot[0, 0]
    cells = (8, 8, 128)
    ye, yo = call(pack_y, (shape(Y_TILES, 8, 128), shape(Y_TILES, 8, 128)), [VM, SM, VM])(parts, sends, fluid_velocity)
    got_ye = swap(ye, "gy", 0)
    got_yo = swap(yo, "gy", 1)
    xe, flow_x = call(pack_first, (shape(X_TILES, 8, 128), shape(3, 8, 16, 128)), [VM, SM, VM, VM, VM])(
        parts, sends, fluid_velocity, got_ye, got_yo
    )
    got_xe = swap(xe, "gx", 0)
    xo = call(pack_second, shape(X_TILES, 8, 128), [VM, SM, VM])(parts, sends, flow_x)
    got_xo = swap(xo, "gx", 1)
    operands = (
        jax.ShapeDtypeStruct((POOL // 4, 128, 128), BF16),
        jax.ShapeDtypeStruct((POOL, 16, 128), BF16),
        jax.ShapeDtypeStruct((OWNABLE, 32, 256), BF16),
        shape(OWNABLE, 8, 128),
    )
    prepared = call(
        contact_near, operands, [SM, SM] + [VM] * 4, [pltpu.SMEM((LIST,), jnp.int32)], flops=10**8
    )(pairs, tile_count, parts, got_ye, got_yo, xo)
    drag, dep, fo, gain, rest = call(
        couple,
        (shape(3, 384, 128), shape(4, 10, 16, 128), shape(D_TILES, 8, 128), shape(*cells), shape(*cells)),
        [VM, HB, HB, HB] + [VM] * 11,
        [
            pltpu.VMEM((OWNABLE, 8, 128), F32),
            pltpu.VMEM((100, 8, 128), F32),
            pltpu.VMEM((100, 8, 128), F32),
            pltpu.SMEM((OWNABLE,), F32),
            pltpu.SMEM((OWNABLE + 1,), jnp.int32),
            pltpu.SMEM((4, SLOTS), jnp.int32),
            pltpu.SMEM((2, 4), jnp.int32),
            pltpu.SMEM((4, 384), jnp.int32),
            pltpu.SemaphoreType.DMA((3,)),
        ],
    )(
        parts, sends, moves, tiles, slots, flow_x, got_xo, got_xe, got_ye, got_yo, prepared[3],
        pressure_init, screening, source, solid_old,
    )
    got_fo = swap(fo, "gx", 1)
    fe = call(pack_fe, shape(D_TILES, 8, 128), [VM] * 4)(dep, pressure_init, gain, rest)
    got_fe = swap(fe, "gx", 0)
    *more, chosen = call(
        contact_more,
        (*operands, jax.ShapeDtypeStruct((LIST,), jnp.int32)),
        [SM, SM] + [VM] * 7,
        flops=10**8,
    )(pairs, tile_count, got_xo, got_xe, fe, *prepared)
    load, drag_x, pres_w, gain_w, rest_w, he, ho = call(
        fold_x,
        (
            shape(16, 16, 128), shape(3, 8, 16, 128), shape(16, 8, 128), shape(16, 8, 128), shape(16, 8, 128),
            shape(H_TILES, 8, 128), shape(H_TILES, 8, 128),
        ),
        [VM] * 7,
    )(dep, pressure_init, gain, rest, got_fo, got_fe, more[3])
    got_he = swap(he, "gy", 0)
    got_ho = swap(ho, "gy", 1)
    force = call(
        contact_end,
        shape(3, 384, 128),
        [SM] + [VM] * 10 + [SM, VM],
        [pltpu.VMEM((OWNABLE, 8, 128), F32)],
        flops=10**9,
    )(pairs, parts, got_xo, got_xe, got_ye, got_yo, drag, ho, *more[:3], chosen, more[3])
    pressure, drag_sum = call(
        finish,
        (shape(*cells), shape(3, *cells)),
        [VM] * 7,
        [pltpu.VMEM((16, 16, 128), F32)] * 4,
    )(load, drag_x, pres_w, gain_w, rest_w, got_he, got_ho)
    return (pressure, drag_sum, force.transpose(1, 0, 2)[None, None])


def solution(mesh):
    in_specs = (
        P("gx", "gy", None, None, None),
        P("gx", "gy", None, None),
        P("gx", "gy", None, None),
        P("gx", "gy", None, None),
        P("gx", "gy"),
        P("gx", "gy", None, None),
        P("gx", "gy", None, None),
        P(None, "gx", "gy", None),
        P("gx", "gy", None),
        P("gx", "gy", None),
        P("gx", "gy", None),
        P("gx", "gy", None),
    )
    out_specs = (P("gx", "gy", None), P(None, "gx", "gy", None), P("gx", "gy", None, None, None))
    return jax.shard_map(body, mesh=mesh, in_specs=in_specs, out_specs=out_specs, check_vma=False)
```
